128 devices in a mesh: dom: 32 (over z, y_hi, x), rep: 4 (over y_lo, core).
Axes of the slice: x: 4, y: 4 (y_hi: 2, y_lo: 2; y = y_hi * 2 + y_lo), z: 4, core: 2. Of those that a mesh axis runs over, the one named last changes fastest.
Arguments:
- embeddings: float32 [1048576, 256], P(('dom', 'rep')), may hold values from -1.5 to 1.5
- row_state: float32 [1048576], P(('dom', 'rep')), may hold values from 0.01 to 0.1
- relations: float32 [64, 256], replicated, may hold values from 0.1 to 1.9
- rel_state: float32 [64, 256], replicated, may hold values from 2 to 40
- edge_src: int32 [32, 4, 2, 4, 1000], P('dom', 'rep'), may hold values from 0 to 8191
- edge_dst: int32 [32, 4, 2, 4, 1000], P('dom', 'rep'), may hold values from 0 to 8191
- edge_rel: int32 [32, 4, 2, 4, 1000], P('dom', 'rep'), may hold values from 0 to 63
- batch_count: int32 [32, 4, 2], P('dom', 'rep'), may hold values from 1 to 4, as said below
Outputs:
- new_embeddings: float32 [1048576, 256], P(('dom', 'rep'))
- new_row_state: float32 [1048576], P(('dom', 'rep'))
- new_relations: float32 [64, 256], replicated
- new_rel_state: float32 [64, 256], replicated
The draws below stay inside these ranges and needn't reach their ends.
Inputs may be any that keep to these rules, and one draw needn't show every extreme that they name: `batch_count`: batches at or past the count are ignored; some bucket of each round set reaches 4.
All inputs are finite; a program needn't handle non-finite values.
Results may differ from the reference program's by a relative error of at most 0.0031.
Values may be sent and summed in bfloat16 or wider, within the bound.
A program may use at most 128 MiB of HBM per device.

```python
import math
import jax
import jax.numpy as jnp
import numpy as np
from jax import lax

D = 256
REL = 64
ROWS_DEV = 8192
BATCH = 1000
NB_CAP = 4
ROUNDS = 2
NODES = 1048576
N_DOM = 32
N_REP = 4


def draw_batch_count(key, part):
    key_extra = jax.random.fold_in(key, 11)
    key_keep = jax.random.fold_in(key, 12)
    key_place = jax.random.fold_in(key, 13)
    extra = jax.random.randint(key_extra, (N_DOM, N_REP, ROUNDS), 0, NB_CAP)
    keep_flag = jax.random.randint(key_keep, (N_DOM, N_REP, ROUNDS), 0, 2)
    counted = 1 + extra * keep_flag
    places = jax.random.randint(key_place, (ROUNDS,), 0, N_DOM * N_REP)
    flat_index = jnp.arange(N_DOM * N_REP, dtype=jnp.int32).reshape(N_DOM, N_REP, 1)
    counted = jnp.where(flat_index == places[None, None, :], NB_CAP, counted)
    return counted.astype(jnp.int32)


def touch_ends(values, own_key, least, largest):
    index_at = [jax.random.randint(jax.random.fold_in(own_key, axis), (), 0, length) for axis, length in enumerate(values.shape)]
    main_axis = values.shape.index(max(values.shape))
    next_to = index_at[:main_axis] + [(index_at[main_axis] + 1) % values.shape[main_axis]] + index_at[main_axis + 1:]
    return values.at[tuple(index_at)].set(least).at[tuple(next_to)].set(largest)


def steps_of(own_key, dims, pieces, least, top_value):
    def one(dim, parts):
        heights = jax.random.uniform(jax.random.fold_in(jax.random.fold_in(own_key, 6), dim), (parts,), jnp.float32, least / len(pieces), top_value / len(pieces))
        return jnp.repeat(jnp.exp(heights), dims[dim] // parts).reshape((-1,) + (1,) * (len(dims) - dim - 1))

    level = one(*pieces[0])
    for cut in pieces[1:]:
        level = level * one(*cut)
    return level


def rank_bounds(count, skew):
    portions = [(1 << 20) // math.isqrt(rank ** skew) + 1 for rank in range(1, count + 1)]
    deviation = 1 + sum(portions) // (1 << 30)
    return np.cumsum(np.array([max(1, weight // deviation) for weight in portions]))


def skewed_ids(key, shape, count, lean):
    table = rank_bounds(count, lean)
    pick = jax.random.randint(jax.random.fold_in(key, 1), shape, 0, int(table[count - 1]))
    grade = jnp.searchsorted(jnp.asarray(table, jnp.int32), pick, side="right")
    return jax.random.permutation(jax.random.fold_in(key, 2), count)[grade].astype(jnp.int32)


def centred(key, extent, deviation, most, pieces=(), kind=jnp.bfloat16):
    values = deviation * jax.random.normal(key, extent, jnp.float32)
    if pieces:
        values = values * steps_of(key, extent, pieces, -0.22, 0.18)
    return jnp.clip(values, -most, most).astype(kind)


def setup_inputs(seed: int = 0) -> dict:
    keys = jax.random.split(jax.random.key(seed), 9)
    embeddings = centred(keys[0], (NODES, D), 0.25, 1.5, ((0, 128),), jnp.float32)
    row_state = jnp.clip(jnp.exp(math.log(0.1) - 2.3025851 * jax.random.uniform(keys[1], (NODES,), jnp.float32) ** steps_of(keys[1], (NODES,), ((0, 128),), -0.2, 0.2)), 0.01, 0.1)
    relations = jnp.clip(1.0 + 0.18 * jax.random.normal(keys[2], (REL, D), jnp.float32), 0.1, 1.9)
    rel_state = jnp.clip(jnp.exp(jax.random.uniform(keys[3], (REL, D), jnp.float32, math.log(2.0), math.log(40.0))), 2.0, 40.0)
    edge_src = touch_ends(jax.random.randint(keys[4], (N_DOM, N_REP, ROUNDS, NB_CAP, BATCH), 0, ROWS_DEV), jax.random.fold_in(keys[4], 1), 0, ROWS_DEV - 1).astype(jnp.int32)
    edge_dst = touch_ends(jax.random.randint(keys[5], (N_DOM, N_REP, ROUNDS, NB_CAP, BATCH), 0, ROWS_DEV), jax.random.fold_in(keys[5], 1), 0, ROWS_DEV - 1).astype(jnp.int32)
    edge_rel = touch_ends(skewed_ids(keys[6], (N_DOM, N_REP, ROUNDS, NB_CAP, BATCH), REL, 2), jax.random.fold_in(keys[6], 3), 0, REL - 1).astype(jnp.int32)
    batch_count = draw_batch_count(jax.random.fold_in(keys[8], 71), 0)
    return dict(embeddings=embeddings, row_state=row_state, relations=relations, rel_state=rel_state, edge_src=edge_src, edge_dst=edge_dst, edge_rel=edge_rel, batch_count=batch_count)


learn_rate = 0.1
rel_rate = 0.1

def batch_terms(source_rows, target_rows, kind_index, relations):
    rel_count = relations.shape[0]
    onehot = (kind_index[:, None] == jnp.arange(rel_count, dtype=jnp.int32)[None, :]).astype(relations.dtype)
    diagonal = jnp.dot(onehot, relations, precision=lax.Precision.HIGHEST)
    source_full = source_rows.astype(relations.dtype)
    queries = (source_full * diagonal).astype(jnp.bfloat16)
    scores = lax.dot_general(queries, target_rows, (((1,), (1,)), ((), ())), preferred_element_type=jnp.float32)
    size_rows = scores.shape[0]
    on_diag = jnp.arange(size_rows)[:, None] == jnp.arange(size_rows)[None, :]
    probs = jax.nn.sigmoid(scores)
    weights_bf = jnp.where(on_diag, probs - 1.0, probs / (size_rows - 1)).astype(jnp.bfloat16)
    grad_query = jnp.dot(weights_bf, target_rows, preferred_element_type=jnp.float32)
    grad_target = lax.dot_general(weights_bf, queries, (((0,), (0,)), ((), ())), preferred_element_type=jnp.float32)
    grad_source = grad_query * diagonal
    grad_rel = lax.dot_general(onehot, grad_query * source_full, (((0,), (0,)), ((), ())), precision=lax.Precision.HIGHEST)
    return (grad_source, grad_target, grad_rel)

def reference(embeddings, row_state, relations, rel_state, edge_src, edge_dst, edge_rel, batch_count):
    groups = N_DOM * N_REP
    bit_count = N_DOM.bit_length() - 1
    embed_table = embeddings.reshape(groups, ROWS_DEV, D)
    states = row_state.reshape(groups, ROWS_DEV)
    for number in range(ROUNDS):
        mask_value = 1 << bit_count - 1 - number
        rows_bf = embed_table.astype(jnp.bfloat16)

        def device_step(device, carried):
            row_grads, rel_grad = carried
            dom_index = device // N_REP
            rep_index = device % N_REP
            partner = (dom_index ^ mask_value) * N_REP + rep_index
            own_rows = rows_bf[device]
            other_rows = rows_bf[partner]
            live_batches = batch_count[dom_index, rep_index, number]

            def batch_step(batch_number, inner_carry):
                own_grad, other_grad, rel_inner = inner_carry
                sources = edge_src[dom_index, rep_index, number, batch_number]
                targets = edge_dst[dom_index, rep_index, number, batch_number]
                kind_index = edge_rel[dom_index, rep_index, number, batch_number]
                source_grad, target_grad, kind_grad = batch_terms(jnp.take(own_rows, sources, axis=0), jnp.take(other_rows, targets, axis=0), kind_index, relations)
                return (own_grad.at[sources].add(source_grad), other_grad.at[targets].add(target_grad), rel_inner + kind_grad)
            empty_grad = jnp.zeros((ROWS_DEV, D), embed_table.dtype)
            own_grad, other_grad, rel_grad = lax.fori_loop(0, live_batches, batch_step, (empty_grad, empty_grad, rel_grad))
            row_grads = row_grads.at[device].add(own_grad).at[partner].add(other_grad)
            return (row_grads, rel_grad)
        row_grads, rel_grad = lax.fori_loop(0, groups, device_step, (jnp.zeros_like(embed_table), jnp.zeros_like(relations)))
        states = states + lax.optimization_barrier(jnp.mean(row_grads * row_grads, axis=-1))
        embed_table = embed_table - learn_rate * row_grads / jnp.sqrt(states)[:, :, None]
        rel_state = rel_state + rel_grad * rel_grad
        relations = relations - rel_rate * rel_grad / jnp.sqrt(rel_state)
    return (embed_table.reshape(NODES, D), states.reshape(NODES), relations, rel_state)
```

```python
import functools

import jax
import jax.numpy as jnp
from jax import lax
from jax.experimental import pallas as pl
from jax.experimental.pallas import tpu as pltpu
from jax.sharding import PartitionSpec as P

ROUNDS = 2

learn_rate = 0.1
rel_rate = 0.1


SMEM = pl.BlockSpec(memory_space=pltpu.SMEM)
VMEM = pl.BlockSpec(memory_space=pltpu.VMEM)
ANY = pl.BlockSpec(memory_space=pl.ANY)
UNROLL = 8
BLOCK = 256
LANES = 128


def params(**kw):
    return pltpu.CompilerParams(vmem_limit_bytes=60 * 1024 * 1024, **kw)


def cost(flops, nbytes):
    return pl.CostEstimate(flops=flops, bytes_accessed=nbytes, transcendentals=0)


def round_up(n, m):
    return (n + m - 1) // m * m


def gather_rows(index_ref, batch, count, table, rows):
    @pl.loop(0, count // UNROLL)
    def _(step):
        base = pl.multiple_of(step * UNROLL, UNROLL)
        for j in range(UNROLL):
            rows[pl.ds(base + j, 1), :] = table[pl.ds(index_ref[batch, base + j], 1), :]

    if rows.shape[0] > count:
        rows[count:, :] = jnp.zeros((rows.shape[0] - count, rows.shape[1]), rows.dtype)


def scatter_rows(index_ref, batch, count, rows, total):
    @pl.loop(0, count // UNROLL)
    def _(step):
        base = pl.multiple_of(step * UNROLL, UNROLL)
        for j in range(UNROLL):
            row = index_ref[batch, base + j]
            total[pl.ds(row, 1), :] += rows[pl.ds(base + j, 1), :]


def pack(index, table, batches, count, name):
    height = round_up(count, 16)
    width = table.shape[1]

    def body(index_ref, table_ref, *refs):
        outs, rows = refs[:-1], refs[-1]
        for out, batch in zip(outs, batches):
            gather_rows(index_ref, batch, count, table_ref, rows)
            out[...] = rows[...].astype(out.dtype)

    return pl.pallas_call(
        body,
        out_shape=[jax.ShapeDtypeStruct((height, width), jnp.bfloat16)] * len(batches),
        in_specs=[SMEM, VMEM],
        out_specs=[VMEM] * len(batches),
        scratch_shapes=[pltpu.VMEM((height, width), jnp.float32)],
        compiler_params=params(),
        cost_estimate=cost(0, table.size * 4 + 6_000_000 * len(batches)),
        name=name,
    )(index, table)


def batch_kernel(batch, count, live_ref, kind_ref, source_ref, target_ref, rel_ref, rel_in,
                 grad_source, grad_target, rel_out, query_t, total_t, product):
    height, width = source_ref.shape
    full = round_up(height, BLOCK)
    kinds = rel_ref.shape[0]
    neg_share = 0.5 / (count - 1)

    @pl.when(batch >= live_ref[0])
    def _():
        rel_out[...] = rel_in[...]

    @pl.when(batch < live_ref[0])
    def _():
        rel = rel_ref[...]
        high = rel.astype(jnp.bfloat16)
        rest = rel - high.astype(jnp.float32)
        mid = rest.astype(jnp.bfloat16)
        low = (rest - mid.astype(jnp.float32)).astype(jnp.bfloat16)
        parts = jnp.concatenate([high, mid, low], axis=0)
        kind = jnp.broadcast_to(kind_ref[...], (3 * kinds, full))
        row = lax.broadcasted_iota(jnp.int32, (3 * kinds, full), 0)
        hot = jnp.where((row % kinds) == kind, 1.0, 0.0).astype(jnp.bfloat16)
        diagonal = lax.dot_general(
            hot, parts, (((0,), (0,)), ((), ())), preferred_element_type=jnp.float32
        )
        source = source_ref[...].astype(jnp.float32)
        target = target_ref[...]
        if full > height:
            gap = jnp.zeros((full - height, width), jnp.float32)
            source = jnp.concatenate([source, gap], axis=0)
            target = jnp.concatenate([target, gap.astype(target.dtype)], axis=0)
        query_full = (source * diagonal).astype(jnp.bfloat16).astype(jnp.float32)
        query_t[...] = query_full.T.astype(jnp.bfloat16)
        half_query = (query_full * 0.5).astype(jnp.bfloat16)
        eye = lax.broadcasted_iota(jnp.int32, (BLOCK, BLOCK), 0) == lax.broadcasted_iota(
            jnp.int32, (BLOCK, BLOCK), 1
        )
        for block in range(full // BLOCK):
            here = slice(block * BLOCK, (block + 1) * BLOCK)
            pieces = []
            for col in range(full // BLOCK):
                there = slice(col * BLOCK, (col + 1) * BLOCK)
                half = jnp.tanh(
                    lax.dot_general(
                        half_query[here],
                        target[there],
                        (((1,), (1,)), ((), ())),
                        preferred_element_type=jnp.float32,
                    )
                )
                weight = half * neg_share + neg_share
                if col == block:
                    weight = jnp.where(eye, half * 0.5 - 0.5, weight)
                pieces.append(weight.astype(jnp.bfloat16))
            weights = jnp.concatenate(pieces, axis=1)
            grad_query = jnp.dot(weights, target, preferred_element_type=jnp.float32)
            tall = min(height - block * BLOCK, BLOCK)
            grad_source[block * BLOCK : block * BLOCK + tall, :] = (
                grad_query * diagonal[here]
            )[:tall]
            product[here, :] = grad_query * source[here]
            part = jnp.dot(query_t[:, here], weights, preferred_element_type=jnp.float32)
            if block == 0:
                total_t[...] = part
            else:
                total_t[...] += part
        grad_target[...] = total_t[...].T[:height].astype(grad_target.dtype)
        value = product[...]
        upper = value.astype(jnp.bfloat16)
        lower = (value - upper.astype(jnp.float32)).astype(jnp.bfloat16)
        one = hot[:kinds]
        rel_out[...] = (
            rel_in[...]
            + jnp.dot(one, upper, preferred_element_type=jnp.float32)
            + jnp.dot(one, lower, preferred_element_type=jnp.float32)
        )


def run_batch(batch, count, live, kind, source, target, relations, rel_grad):
    height, width = source.shape
    full = round_up(height, BLOCK)
    return pl.pallas_call(
        functools.partial(batch_kernel, batch, count),
        out_shape=[
            jax.ShapeDtypeStruct((height, width), jnp.float32),
            jax.ShapeDtypeStruct((height, width), jnp.bfloat16),
            jax.ShapeDtypeStruct(rel_grad.shape, jnp.float32),
        ],
        in_specs=[SMEM] + [VMEM] * 5,
        out_specs=[VMEM] * 3,
        scratch_shapes=[
            pltpu.VMEM((width, full), jnp.bfloat16),
            pltpu.VMEM((width, full), jnp.float32),
            pltpu.VMEM((full, width), jnp.float32),
        ],
        compiler_params=params(),
        cost_estimate=cost(0, 20_000_000),
        name="batch_terms",
    )(live, kind, source, target, relations, rel_grad)


def first_total(count, row_count, live, other_live, source_index, other_index, own, returned):
    height, width = own[0].shape
    total_own = len(own)

    def body(live_ref, other_ref, source_ref, index_ref, *refs):
        own_refs = refs[:total_own]
        back_refs = refs[total_own:-2]
        total, rows = refs[-2:]
        total[...] = jnp.zeros_like(total)
        for batch, ref in enumerate(own_refs):

            @pl.when(batch < live_ref[0])
            def _():
                scatter_rows(source_ref, batch, count, ref, total)

        for batch, ref in enumerate(back_refs):

            @pl.when(batch < other_ref[0])
            def _():
                rows[...] = ref[...].astype(jnp.float32)
                scatter_rows(index_ref, batch, count, rows, total)

    return pl.pallas_call(
        body,
        out_shape=jax.ShapeDtypeStruct((row_count, width), jnp.float32),
        in_specs=[SMEM] * 4 + [VMEM] * (len(own) + len(returned)),
        out_specs=VMEM,
        scratch_shapes=[pltpu.VMEM((height, width), jnp.float32)],
        compiler_params=params(),
        cost_estimate=cost(0, 60_000_000),
        name="first_total",
    )(live, other_live, source_index, other_index, *own, *returned)


def finish(count, other_live, other_index, total, returned, first, table, state):
    row_count, width = table.shape
    height = returned[0].shape[0]
    groups = row_count // LANES
    step_rows = 1024
    steps = row_count // step_rows

    def body(live_ref, index_ref, total_hbm, *refs):
        back_refs = refs[: len(returned)]
        table_hbm, state_ref, out_hbm, state_out, total_v, table_v, rows, state_t, mean_t, sems = refs[
            len(returned) :
        ]
        load_total = pltpu.make_async_copy(total_hbm, total_v, sems.at[0])
        load_table = pltpu.make_async_copy(table_hbm, table_v, sems.at[1])
        load_total.start()
        load_table.start()
        spare = jnp.zeros((LANES - groups, LANES), jnp.float32)
        state_t[...] = jnp.concatenate([state_ref[...], spare], axis=0).T
        mean_t[...] = jnp.zeros_like(mean_t)
        load_total.wait()
        for place, ref in enumerate(back_refs):

            @pl.when(first + place < live_ref[0])
            def _():
                rows[...] = ref[...].astype(jnp.float32)
                scatter_rows(index_ref, first + place, count, rows, total_v)

        load_table.wait()
        lane = lax.broadcasted_iota(jnp.int32, (LANES, LANES), 1)
        saves = []
        for step in range(steps):

            @pl.loop(step * step_rows // LANES, (step + 1) * step_rows // LANES)
            def _(group):
                here = pl.ds(pl.multiple_of(group * LANES, LANES), LANES)
                grad = total_v[here, :]
                mean = jnp.sum(grad * grad, axis=1, keepdims=True) * (1.0 / width)
                mine = lane == group
                old = jnp.sum(jnp.where(mine, state_t[...], 0.0), axis=1, keepdims=True)
                mean_t[...] = jnp.where(mine, mean, mean_t[...])
                scale = learn_rate / jnp.sqrt(old + mean)
                table_v[here, :] = table_v[here, :] - grad * scale

            part = pl.ds(step * step_rows, step_rows)
            save = pltpu.make_async_copy(table_v.at[part], out_hbm.at[part], sems.at[2 + step])
            save.start()
            saves.append(save)
        state_out[...] = (state_t[...] + mean_t[...]).T[:groups]
        for save in saves:
            save.wait()

    return pl.pallas_call(
        body,
        out_shape=[
            jax.ShapeDtypeStruct((row_count, width), jnp.float32),
            jax.ShapeDtypeStruct((groups, LANES), jnp.float32),
        ],
        in_specs=[SMEM, SMEM, ANY] + [VMEM] * len(returned) + [ANY, VMEM],
        out_specs=[ANY, VMEM],
        scratch_shapes=[
            pltpu.VMEM((row_count, width), jnp.float32),
            pltpu.VMEM((row_count, width), jnp.float32),
            pltpu.VMEM((height, width), jnp.float32),
            pltpu.VMEM((LANES, LANES), jnp.float32),
            pltpu.VMEM((LANES, LANES), jnp.float32),
            pltpu.SemaphoreType.DMA((2 + steps,)),
        ],
        compiler_params=params(),
        cost_estimate=cost(0, 50_000_000),
        name="finish",
    )(other_live, other_index, total, *returned, table, state)


def from_partner(shard, axis, distance):
    return lax.ppermute(shard, axis, [(i, i ^ 1 << distance) for i in range(lax.axis_size(axis))])


def on_device(
    embeddings, row_state, relations, rel_state, edge_src, edge_dst, edge_rel, batch_count
):
    bit_count = lax.axis_size("dom").bit_length() - 1
    row_count, _ = embeddings.shape
    batches, count = edge_src.shape[-2:]
    padded = round_up(count, BLOCK)
    state = row_state.reshape(row_count // LANES, LANES)
    spots = [bit_count - 1 - number for number in range(ROUNDS)]
    told = []
    for number in range(ROUNDS):
        note = jnp.concatenate([edge_dst[0, 0, number].reshape(-1), batch_count[0, 0, number].reshape(1)])
        told.append(from_partner(note, "dom", spots[number]))
    for number in range(ROUNDS):
        swap_bit = spots[number]
        source_index = edge_src[0, 0, number]
        other_index = told[number][: batches * count].reshape(batches, count)
        other_live = told[number][batches * count :]
        live = batch_count[0, 0, number].reshape(1)
        kinds = jnp.pad(edge_rel[0, 0, number], ((0, 0), (0, padded - count)), constant_values=-1)
        sent = pack(other_index, embeddings, (0,), count, "pack_first")
        arrived = [from_partner(sent[0], "dom", swap_bit)]
        more = pack(other_index, embeddings, tuple(range(1, batches)), count, "pack_rest")
        arrived += [from_partner(rows, "dom", swap_bit) for rows in more]
        sources = pack(source_index, embeddings, tuple(range(batches)), count, "pack_own")
        rel_grad = jnp.zeros(relations.shape, jnp.float32)
        own, returned = [], []
        for batch in range(batches):
            grad_source, grad_target, rel_grad = run_batch(
                batch, count, live, kinds[batch][None], sources[batch], arrived[batch], relations, rel_grad
            )
            own.append(grad_source)
            returned.append(from_partner(grad_target, "dom", swap_bit))
        rel_total = lax.psum(rel_grad, ("dom", "rep"))
        early = batches - 2
        total = first_total(
            count, row_count, live, other_live, source_index, other_index, own, returned[:early]
        )
        embeddings, state = finish(
            count, other_live, other_index, total, returned[early:], early, embeddings, state
        )
        rel_state = rel_state + rel_total * rel_total
        relations = relations - rel_rate * rel_total / jnp.sqrt(rel_state)
    return (embeddings, state.reshape(row_count), relations, rel_state)


def solution(mesh):
    return jax.shard_map(
        on_device,
        mesh=mesh,
        in_specs=(
            P(("dom", "rep"), None),
            P(("dom", "rep")),
            P(),
            P(),
            P("dom", "rep", None, None, None),
            P("dom", "rep", None, None, None),
            P("dom", "rep", None, None, None),
            P("dom", "rep", None),
        ),
        out_specs=(P(("dom", "rep"), None), P(("dom", "rep")), P(), P()),
        check_vma=False,
    )
```

```python
import functools

import jax
import jax.numpy as jnp
from jax import lax
from jax.experimental import pallas as pl
from jax.experimental.pallas import tpu as pltpu
from jax.sharding import PartitionSpec as P

ROUNDS = 2

learn_rate = 0.1
rel_rate = 0.1


SMEM = pl.BlockSpec(memory_space=pltpu.SMEM)
VMEM = pl.BlockSpec(memory_space=pltpu.VMEM)
ANY = pl.BlockSpec(memory_space=pl.ANY)
UNROLL = 8
BLOCK = 256
LANES = 128


def params(**kw):
    return pltpu.CompilerParams(vmem_limit_bytes=60 * 1024 * 1024, **kw)


def cost(flops, nbytes):
    return pl.CostEstimate(flops=flops, bytes_accessed=nbytes, transcendentals=0)


def round_up(n, m):
    return (n + m - 1) // m * m


def gather_rows(index_ref, batch, count, table, rows):
    @pl.loop(0, count // UNROLL)
    def _(step):
        base = pl.multiple_of(step * UNROLL, UNROLL)
        for j in range(UNROLL):
            rows[pl.ds(base + j, 1), :] = table[pl.ds(index_ref[batch, base + j], 1), :]

    if rows.shape[0] > count:
        rows[count:, :] = jnp.zeros((rows.shape[0] - count, rows.shape[1]), rows.dtype)


def scatter_rows(index_ref, batch, count, rows, total):
    @pl.loop(0, count // UNROLL)
    def _(step):
        base = pl.multiple_of(step * UNROLL, UNROLL)
        for j in range(UNROLL):
            row = index_ref[batch, base + j]
            total[pl.ds(row, 1), :] += rows[pl.ds(base + j, 1), :]


def pack(index, table, batches, count, name):
    height = round_up(count, 16)
    width = table.shape[1]

    def body(index_ref, table_ref, *refs):
        outs, rows = refs[:-1], refs[-1]
        for out, batch in zip(outs, batches):
            gather_rows(index_ref, batch, count, table_ref, rows)
            out[...] = rows[...].astype(out.dtype)

    return pl.pallas_call(
        body,
        out_shape=[jax.ShapeDtypeStruct((height, width), jnp.bfloat16)] * len(batches),
        in_specs=[SMEM, VMEM],
        out_specs=[VMEM] * len(batches),
        scratch_shapes=[pltpu.VMEM((height, width), jnp.float32)],
        compiler_params=params(),
        cost_estimate=cost(0, table.size * 4 + 6_000_000 * len(batches)),
        name=name,
    )(index, table)


def batch_kernel(batch, count, live_ref, kind_ref, source_ref, target_ref, rel_ref, rel_in,
                 grad_source, grad_target, rel_out, query_t, total_t, product):
    height, width = source_ref.shape
    full = round_up(height, BLOCK)
    kinds = rel_ref.shape[0]
    neg_share = 0.5 / (count - 1)

    @pl.when(batch >= live_ref[0])
    def _():
        rel_out[...] = rel_in[...]

    @pl.when(batch < live_ref[0])
    def _():
        rel = rel_ref[...]
        high = rel.astype(jnp.bfloat16)
        rest = rel - high.astype(jnp.float32)
        mid = rest.astype(jnp.bfloat16)
        low = (rest - mid.astype(jnp.float32)).astype(jnp.bfloat16)
        parts = jnp.concatenate([high, mid, low], axis=0)
        kind = jnp.broadcast_to(kind_ref[...], (3 * kinds, full))
        row = lax.broadcasted_iota(jnp.int32, (3 * kinds, full), 0)
        hot = jnp.where((row % kinds) == kind, 1.0, 0.0).astype(jnp.bfloat16)
        diagonal = lax.dot_general(
            hot, parts, (((0,), (0,)), ((), ())), preferred_element_type=jnp.float32
        )
        source = source_ref[...].astype(jnp.float32)
        target = target_ref[...]
        if full > height:
            gap = jnp.zeros((full - height, width), jnp.float32)
            source = jnp.concatenate([source, gap], axis=0)
            target = jnp.concatenate([target, gap.astype(target.dtype)], axis=0)
        query_full = (source * diagonal).astype(jnp.bfloat16).astype(jnp.float32)
        query_t[...] = query_full.T.astype(jnp.bfloat16)
        half_query = (query_full * 0.5).astype(jnp.bfloat16)
        eye = lax.broadcasted_iota(jnp.int32, (BLOCK, BLOCK), 0) == lax.broadcasted_iota(
            jnp.int32, (BLOCK, BLOCK), 1
        )
        for block in range(full // BLOCK):
            here = slice(block * BLOCK, (block + 1) * BLOCK)
            pieces = []
            for col in range(full // BLOCK):
                there = slice(col * BLOCK, (col + 1) * BLOCK)
                half = jnp.tanh(
                    lax.dot_general(
                        half_query[here],
                        target[there],
                        (((1,), (1,)), ((), ())),
                        preferred_element_type=jnp.float32,
                    )
                )
                weight = half * neg_share + neg_share
                if col == block:
                    weight = jnp.where(eye, half * 0.5 - 0.5, weight)
                pieces.append(weight.astype(jnp.bfloat16))
            weights = jnp.concatenate(pieces, axis=1)
            grad_query = jnp.dot(weights, target, preferred_element_type=jnp.float32)
            tall = min(height - block * BLOCK, BLOCK)
            grad_source[block * BLOCK : block * BLOCK + tall, :] = (
                grad_query * diagonal[here]
            )[:tall]
            product[here, :] = grad_query * source[here]
            part = jnp.dot(query_t[:, here], weights, preferred_element_type=jnp.float32)
            if block == 0:
                total_t[...] = part
            else:
                total_t[...] += part
        grad_target[...] = total_t[...].T[:height].astype(grad_target.dtype)
        value = product[...]
        upper = value.astype(jnp.bfloat16)
        lower = (value - upper.astype(jnp.float32)).astype(jnp.bfloat16)
        one = hot[:kinds]
        rel_out[...] = (
            rel_in[...]
            + jnp.dot(one, upper, preferred_element_type=jnp.float32)
            + jnp.dot(one, lower, preferred_element_type=jnp.float32)
        )


def run_batch(batch, count, live, kind, source, target, relations, rel_grad):
    height, width = source.shape
    full = round_up(height, BLOCK)
    return pl.pallas_call(
        functools.partial(batch_kernel, batch, count),
        out_shape=[
            jax.ShapeDtypeStruct((height, width), jnp.float32),
            jax.ShapeDtypeStruct((height, width), jnp.bfloat16),
            jax.ShapeDtypeStruct(rel_grad.shape, jnp.float32),
        ],
        in_specs=[SMEM] + [VMEM] * 5,
        out_specs=[VMEM] * 3,
        scratch_shapes=[
            pltpu.VMEM((width, full), jnp.bfloat16),
            pltpu.VMEM((width, full), jnp.float32),
            pltpu.VMEM((full, width), jnp.float32),
        ],
        compiler_params=params(),
        cost_estimate=cost(0, 20_000_000),
        name="batch_terms",
    )(live, kind, source, target, relations, rel_grad)


def first_total(count, row_count, live, other_live, source_index, other_index, own, returned):
    height, width = own[0].shape
    total_own = len(own)

    def body(live_ref, other_ref, source_ref, index_ref, *refs):
        own_refs = refs[:total_own]
        back_refs = refs[total_own:-2]
        total, rows = refs[-2:]
        total[...] = jnp.zeros_like(total)
        for batch, ref in enumerate(own_refs):

            @pl.when(batch < live_ref[0])
            def _():
                scatter_rows(source_ref, batch, count, ref, total)

        for batch, ref in enumerate(back_refs):

            @pl.when(batch < other_ref[0])
            def _():
                rows[...] = ref[...].astype(jnp.float32)
                scatter_rows(index_ref, batch, count, rows, total)

    return pl.pallas_call(
        body,
        out_shape=jax.ShapeDtypeStruct((row_count, width), jnp.float32),
        in_specs=[SMEM] * 4 + [VMEM] * (len(own) + len(returned)),
        out_specs=VMEM,
        scratch_shapes=[pltpu.VMEM((height, width), jnp.float32)],
        compiler_params=params(),
        cost_estimate=cost(0, 60_000_000),
        name="first_total",
    )(live, other_live, source_index, other_index, *own, *returned)


def finish(count, other_live, other_index, total, returned, first, table, state):
    row_count, width = table.shape
    height = returned[0].shape[0]
    groups = row_count // LANES
    step_rows = 1024
    steps = row_count // step_rows

    def body(live_ref, index_ref, total_hbm, *refs):
        back_refs = refs[: len(returned)]
        table_hbm, state_ref, out_hbm, state_out, total_v, table_v, rows, state_t, mean_t, sems = refs[
            len(returned) :
        ]
        load_total = pltpu.make_async_copy(total_hbm, total_v, sems.at[0])
        load_table = pltpu.make_async_copy(table_hbm, table_v, sems.at[1])
        load_total.start()
        load_table.start()
        spare = jnp.zeros((LANES - groups, LANES), jnp.float32)
        state_t[...] = jnp.concatenate([state_ref[...], spare], axis=0).T
        mean_t[...] = jnp.zeros_like(mean_t)
        load_total.wait()
        for place, ref in enumerate(back_refs):

            @pl.when(first + place < live_ref[0])
            def _():
                rows[...] = ref[...].astype(jnp.float32)
                scatter_rows(index_ref, first + place, count, rows, total_v)

        load_table.wait()
        lane = lax.broadcasted_iota(jnp.int32, (LANES, LANES), 1)
        saves = []
        for step in range(steps):

            @pl.loop(step * step_rows // LANES, (step + 1) * step_rows // LANES)
            def _(group):
                here = pl.ds(pl.multiple_of(group * LANES, LANES), LANES)
                grad = total_v[here, :]
                mean = jnp.sum(grad * grad, axis=1, keepdims=True) * (1.0 / width)
                mine = lane == group
                old = jnp.sum(jnp.where(mine, state_t[...], 0.0), axis=1, keepdims=True)
                mean_t[...] = jnp.where(mine, mean, mean_t[...])
                scale = learn_rate / jnp.sqrt(old + mean)
                table_v[here, :] = table_v[here, :] - grad * scale

            part = pl.ds(step * step_rows, step_rows)
            save = pltpu.make_async_copy(table_v.at[part], out_hbm.at[part], sems.at[2 + step])
            save.start()
            saves.append(save)
        state_out[...] = (state_t[...] + mean_t[...]).T[:groups]
        for save in saves:
            save.wait()

    return pl.pallas_call(
        body,
        out_shape=[
            jax.ShapeDtypeStruct((row_count, width), jnp.float32),
            jax.ShapeDtypeStruct((groups, LANES), jnp.float32),
        ],
        in_specs=[SMEM, SMEM, ANY] + [VMEM] * len(returned) + [ANY, VMEM],
        out_specs=[ANY, VMEM],
        scratch_shapes=[
            pltpu.VMEM((row_count, width), jnp.float32),
            pltpu.VMEM((row_count, width), jnp.float32),
            pltpu.VMEM((height, width), jnp.float32),
            pltpu.VMEM((LANES, LANES), jnp.float32),
            pltpu.VMEM((LANES, LANES), jnp.float32),
            pltpu.SemaphoreType.DMA((2 + steps,)),
        ],
        compiler_params=params(),
        cost_estimate=cost(0, 50_000_000),
        name="finish",
    )(other_live, other_index, total, *returned, table, state)


def flip(index, bits):
    for place in range(8):
        step = 1 << place
        if bits & step:
            index = index + step * (1 - 2 * ((index // step) % 2))
    return index


def relation_kernel(stages, near, relations, rel_state, new_relations, new_state, *scratch):
    parts, received = scratch[:-3], scratch[-3]
    send_sems, recv_sems = scratch[-2:]
    dom, rep = lax.axis_index("dom"), lax.axis_index("rep")

    def device(peer):
        return (flip(dom, peer[0]), flip(rep, peer[1]))

    barrier = pltpu.get_barrier_semaphore()
    peers = [peer for stage in stages for peer in stage]
    for peer in peers:
        pl.semaphore_signal(
            barrier, inc=1, device_id=device(peer), device_id_type=pl.DeviceIdType.MESH
        )
    pl.semaphore_wait(barrier, len(peers))
    parts[0][...] = pair_sum([ref[...] for ref in near])
    slot = 0
    for number, stage in enumerate(stages):
        copies = []
        for peer in stage:
            copy = pltpu.make_async_remote_copy(
                src_ref=parts[number],
                dst_ref=received.at[slot],
                send_sem=send_sems.at[slot],
                recv_sem=recv_sems.at[slot],
                device_id=device(peer),
                device_id_type=pl.DeviceIdType.MESH,
            )
            copy.start()
            copies.append(copy)
            slot += 1
        for copy in copies:
            copy.wait()
        first = slot - len(stage)
        total = pair_sum([parts[number][...]] + [received[first + i] for i in range(len(stage))])
        if number + 1 < len(stages):
            parts[number + 1][...] = total
    state = rel_state[...] + total * total
    new_state[...] = state
    new_relations[...] = relations[...] - rel_rate * total / jnp.sqrt(state)


def pair_sum(values):
    while len(values) > 1:
        values = [values[i] + values[i + 1] for i in range(0, len(values), 2)]
    return values[0]


def relation_step(near, relations, rel_state):
    stages = [
        [(0, 1), (0, 2), (0, 3)],
        [(1, 0), (2, 0), (3, 0)],
        [(4, 0)],
    ]
    slots = sum(len(stage) for stage in stages)
    shape = relations.shape
    count = len(near)

    def body(*refs):
        relation_kernel(stages, refs[:count], *refs[count:])

    return pl.pallas_call(
        body,
        out_shape=[jax.ShapeDtypeStruct(shape, jnp.float32)] * 2,
        in_specs=[VMEM] * (count + 2),
        out_specs=[VMEM] * 2,
        scratch_shapes=[pltpu.VMEM(shape, jnp.float32)] * len(stages)
        + [
            pltpu.VMEM((slots,) + shape, jnp.float32),
            pltpu.SemaphoreType.DMA((slots,)),
            pltpu.SemaphoreType.DMA((slots,)),
        ],
        compiler_params=pltpu.CompilerParams(
            collective_id=0, has_side_effects=True, vmem_limit_bytes=8 * 1024 * 1024
        ),
        cost_estimate=cost(0, 30_000_000),
        name="relation_step",
    )(*near, relations, rel_state)


def from_partner(shard, axis, distance):
    return from_peer(shard, axis, 1 << distance)


def from_peer(shard, axis, bits):
    return lax.ppermute(shard, axis, [(i, i ^ bits) for i in range(lax.axis_size(axis))])


def on_device(
    embeddings, row_state, relations, rel_state, edge_src, edge_dst, edge_rel, batch_count
):
    bit_count = lax.axis_size("dom").bit_length() - 1
    row_count, _ = embeddings.shape
    batches, count = edge_src.shape[-2:]
    padded = round_up(count, BLOCK)
    state = row_state.reshape(row_count // LANES, LANES)
    spots = [bit_count - 1 - number for number in range(ROUNDS)]
    told = []
    for number in range(ROUNDS):
        note = jnp.concatenate([edge_dst[0, 0, number].reshape(-1), batch_count[0, 0, number].reshape(1)])
        told.append(from_partner(note, "dom", spots[number]))
    told = lax.optimization_barrier(told)
    for number in range(ROUNDS):
        swap_bit = spots[number]
        source_index = edge_src[0, 0, number]
        other_index = told[number][: batches * count].reshape(batches, count)
        other_live = told[number][batches * count :]
        live = batch_count[0, 0, number].reshape(1)
        kinds = jnp.pad(edge_rel[0, 0, number], ((0, 0), (0, padded - count)), constant_values=-1)
        sent = pack(other_index, embeddings, (0,), count, "pack_first")
        arrived = [from_partner(sent[0], "dom", swap_bit)]
        more = pack(other_index, embeddings, tuple(range(1, batches)), count, "pack_rest")
        arrived += [from_partner(rows, "dom", swap_bit) for rows in more]
        sources = pack(source_index, embeddings, tuple(range(batches)), count, "pack_own")
        rel_grad = jnp.zeros(relations.shape, jnp.float32)
        own, returned = [], []
        for batch in range(batches):
            grad_source, grad_target, rel_grad = run_batch(
                batch, count, live, kinds[batch][None], sources[batch], arrived[batch], relations, rel_grad
            )
            own.append(grad_source)
            if batch == batches - 1:
                near = [rel_grad] + [from_peer(rel_grad, "dom", bits) for bits in (8, 16, 24)]
            returned.append(from_partner(grad_target, "dom", swap_bit))
        early = batches - 2
        total = first_total(
            count, row_count, live, other_live, source_index, other_index, own, returned[:early]
        )
        near, total = lax.optimization_barrier((near, total))
        relations, rel_state = relation_step(near, relations, rel_state)
        relations, total = lax.optimization_barrier((relations, total))
        embeddings, state = finish(
            count, other_live, other_index, total, returned[early:], early, embeddings, state
        )
    return (embeddings, state.reshape(row_count), relations, rel_state)


def solution(mesh):
    return jax.shard_map(
        on_device,
        mesh=mesh,
        in_specs=(
            P(("dom", "rep"), None),
            P(("dom", "rep")),
            P(),
            P(),
            P("dom", "rep", None, None, None),
            P("dom", "rep", None, None, None),
            P("dom", "rep", None, None, None),
            P("dom", "rep", None),
        ),
        out_specs=(P(("dom", "rep"), None), P(("dom", "rep")), P(), P()),
        check_vma=False,
    )
```

```python
import functools

import jax
import jax.numpy as jnp
from jax import lax
from jax.experimental import pallas as pl
from jax.experimental.pallas import tpu as pltpu
from jax.sharding import PartitionSpec as P

ROUNDS = 2

learn_rate = 0.1
rel_rate = 0.1


SMEM = pl.BlockSpec(memory_space=pltpu.SMEM)
VMEM = pl.BlockSpec(memory_space=pltpu.VMEM)
ANY = pl.BlockSpec(memory_space=pl.ANY)
UNROLL = 8
GATHER_UNROLL = 8
BLOCK = 256
LANES = 128
MIB = 1024 * 1024


def params(mib, **kw):
    return pltpu.CompilerParams(vmem_limit_bytes=mib * MIB, **kw)


def cost(nbytes):
    return pl.CostEstimate(flops=0, bytes_accessed=nbytes, transcendentals=0)


def round_up(n, m):
    return (n + m - 1) // m * m


def piece(row):
    return pl.ds(pl.multiple_of(row * 2, 2), 2)


def half(start, count, side):
    return pl.ds(start * 2 + side, count, stride=2)


def gather_rows(index_ref, batch, count, table, rows, out):
    @pl.loop(0, count // GATHER_UNROLL)
    def _(step):
        base = step * GATHER_UNROLL
        for j in range(GATHER_UNROLL):
            rows[piece(base + j), :] = table[piece(index_ref[batch, base + j]), :]

    height = out.shape[0]
    if height > count:
        rows[2 * count : 2 * height, :] = jnp.zeros((2 * (height - count), LANES), rows.dtype)
    for side in range(2):
        out[:, side * LANES : (side + 1) * LANES] = rows[half(0, height, side), :].astype(out.dtype)


def scatter_rows(index_ref, batch, count, rows, total):
    @pl.loop(0, count // UNROLL)
    def _(step):
        base = step * UNROLL
        for j in range(UNROLL):
            row = piece(index_ref[batch, base + j])
            total[row, :] += rows[piece(base + j), :]


def spread(ref, rows):
    for side in range(2):
        rows[half(0, ref.shape[0], side), :] = ref[:, side * LANES : (side + 1) * LANES].astype(
            jnp.float32
        )


def pack_first(index, table, batches, count):
    height = round_up(count, 16)
    row_count, width = table.shape

    def body(index_ref, table_ref, long_hbm, *refs):
        outs, (long_v, rows, sem) = refs[:-3], refs[-3:]

        @pl.loop(0, row_count // LANES)
        def _(step):
            here = pl.multiple_of(step * LANES, LANES)
            for side in range(2):
                long_v[half(here, LANES, side), :] = table_ref[
                    pl.ds(here, LANES), side * LANES : (side + 1) * LANES
                ]

        save = pltpu.make_async_copy(long_v, long_hbm, sem)
        save.start()
        for out, batch in zip(outs, batches):
            gather_rows(index_ref, batch, count, long_v, rows, out)
        save.wait()

    return pl.pallas_call(
        body,
        out_shape=[jax.ShapeDtypeStruct((2 * row_count, LANES), jnp.float32)]
        + [jax.ShapeDtypeStruct((height, width), jnp.bfloat16)] * len(batches),
        in_specs=[SMEM, VMEM],
        out_specs=[ANY] + [VMEM] * len(batches),
        scratch_shapes=[
            pltpu.VMEM((2 * row_count, LANES), jnp.float32),
            pltpu.VMEM((2 * height, LANES), jnp.float32),
            pltpu.SemaphoreType.DMA,
        ],
        compiler_params=params(24),
        cost_estimate=cost(25_000_000),
        name="pack_first",
    )(index, table)


def pack(index, own_index, table, batches, own_batches, count, width):
    height = round_up(count, 16)
    outs_count = len(batches) + len(own_batches)

    def body(index_ref, own_ref, table_ref, *refs):
        outs, rows = refs[:-1], refs[-1]
        for out, batch in zip(outs, batches):
            gather_rows(index_ref, batch, count, table_ref, rows, out)
        for out, batch in zip(outs[len(batches) :], own_batches):
            gather_rows(own_ref, batch, count, table_ref, rows, out)

    return pl.pallas_call(
        body,
        out_shape=[jax.ShapeDtypeStruct((height, width), jnp.bfloat16)] * outs_count,
        in_specs=[SMEM, SMEM, VMEM],
        out_specs=[VMEM] * outs_count,
        scratch_shapes=[pltpu.VMEM((2 * height, LANES), jnp.float32)],
        compiler_params=params(16),
        cost_estimate=cost(30_000_000),
        name="pack_rest",
    )(index, own_index, table)


def batch_kernel(batch, count, live_ref, kind_ref, source_ref, target_ref, rel_ref, rel_in,
                 grad_source, grad_target, rel_out, query_t, total_t, product):
    height, width = source_ref.shape
    full = round_up(height, BLOCK)
    kinds = rel_ref.shape[0]
    neg_share = 0.5 / (count - 1)

    @pl.when(batch >= live_ref[0])
    def _():
        rel_out[...] = rel_in[...]

    @pl.when(batch < live_ref[0])
    def _():
        rel = rel_ref[...]
        high = rel.astype(jnp.bfloat16)
        rest = rel - high.astype(jnp.float32)
        mid = rest.astype(jnp.bfloat16)
        low = (rest - mid.astype(jnp.float32)).astype(jnp.bfloat16)
        parts = jnp.concatenate([high, mid, low], axis=0)
        kind = jnp.broadcast_to(kind_ref[...], (3 * kinds, full))
        row = lax.broadcasted_iota(jnp.int32, (3 * kinds, full), 0)
        hot = jnp.where((row % kinds) == kind, 1.0, 0.0).astype(jnp.bfloat16)
        diagonal = lax.dot_general(
            hot, parts, (((0,), (0,)), ((), ())), preferred_element_type=jnp.float32
        )
        source = source_ref[...].astype(jnp.float32)
        target = target_ref[...]
        if full > height:
            gap = jnp.zeros((full - height, width), jnp.float32)
            source = jnp.concatenate([source, gap], axis=0)
            target = jnp.concatenate([target, gap.astype(target.dtype)], axis=0)
        query_full = (source * diagonal).astype(jnp.bfloat16).astype(jnp.float32)
        query_t[...] = query_full.T.astype(jnp.bfloat16)
        half_query = (query_full * 0.5).astype(jnp.bfloat16)
        eye = lax.broadcasted_iota(jnp.int32, (BLOCK, BLOCK), 0) == lax.broadcasted_iota(
            jnp.int32, (BLOCK, BLOCK), 1
        )
        for block in range(full // BLOCK):
            here = slice(block * BLOCK, (block + 1) * BLOCK)
            pieces = []
            for col in range(full // BLOCK):
                there = slice(col * BLOCK, (col + 1) * BLOCK)
                slope = jnp.tanh(
                    lax.dot_general(
                        half_query[here],
                        target[there],
                        (((1,), (1,)), ((), ())),
                        preferred_element_type=jnp.float32,
                    )
                )
                weight = slope * neg_share + neg_share
                if col == block:
                    weight = jnp.where(eye, slope * 0.5 - 0.5, weight)
                pieces.append(weight.astype(jnp.bfloat16))
            weights = jnp.concatenate(pieces, axis=1)
            grad_query = jnp.dot(weights, target, preferred_element_type=jnp.float32)
            tall = min(height - block * BLOCK, BLOCK)
            grad_rows = (grad_query * diagonal[here])[:tall]
            for side in range(2):
                grad_source[half(block * BLOCK, tall, side), :] = grad_rows[
                    :, side * LANES : (side + 1) * LANES
                ]
            product[here, :] = grad_query * source[here]
            part = jnp.dot(query_t[:, here], weights, preferred_element_type=jnp.float32)
            if block == 0:
                total_t[...] = part
            else:
                total_t[...] += part
        grad_target[...] = total_t[...].T[:height].astype(grad_target.dtype)
        value = product[...]
        upper = value.astype(jnp.bfloat16)
        lower = (value - upper.astype(jnp.float32)).astype(jnp.bfloat16)
        one = hot[:kinds]
        rel_out[...] = (
            rel_in[...]
            + jnp.dot(one, upper, preferred_element_type=jnp.float32)
            + jnp.dot(one, lower, preferred_element_type=jnp.float32)
        )


def run_batch(batch, count, live, kind, source, target, relations, rel_grad):
    height, width = source.shape
    full = round_up(height, BLOCK)
    return pl.pallas_call(
        functools.partial(batch_kernel, batch, count),
        out_shape=[
            jax.ShapeDtypeStruct((2 * height, LANES), jnp.float32),
            jax.ShapeDtypeStruct((height, width), jnp.bfloat16),
            jax.ShapeDtypeStruct(rel_grad.shape, jnp.float32),
        ],
        in_specs=[SMEM] + [VMEM] * 5,
        out_specs=[VMEM] * 3,
        scratch_shapes=[
            pltpu.VMEM((width, full), jnp.bfloat16),
            pltpu.VMEM((width, full), jnp.float32),
            pltpu.VMEM((full, width), jnp.float32),
        ],
        compiler_params=params(16),
        cost_estimate=cost(15_000_000),
        name="batch_terms",
    )(live, kind, source, target, relations, rel_grad)


def first_total(count, row_count, live, other_live, source_index, other_index, own, returned):
    def body(live_ref, other_ref, source_ref, index_ref, *refs):
        own_refs = refs[: len(own)]
        back_refs = refs[len(own) : -2]
        total, rows = refs[-2:]
        total[...] = jnp.zeros_like(total)
        for batch, ref in enumerate(own_refs):

            @pl.when(batch < live_ref[0])
            def _():
                scatter_rows(source_ref, batch, count, ref, total)

        for batch, ref in enumerate(back_refs):

            @pl.when(batch < other_ref[0])
            def _():
                spread(ref, rows)
                scatter_rows(index_ref, batch, count, rows, total)

    return pl.pallas_call(
        body,
        out_shape=jax.ShapeDtypeStruct((2 * row_count, LANES), jnp.float32),
        in_specs=[SMEM] * 4 + [VMEM] * (len(own) + len(returned)),
        out_specs=VMEM,
        scratch_shapes=[pltpu.VMEM(own[0].shape, jnp.float32)],
        compiler_params=params(20),
        cost_estimate=cost(60_000_000),
        name="first_total",
    )(live, other_live, source_index, other_index, *own, *returned)


def finish(count, other_live, other_index, total, returned, first, table, state, width, next_index, next_batches):
    row_count = table.shape[0] // 2
    height = returned[0].shape[0]
    groups = row_count // LANES
    step_rows = 1024
    steps = row_count // step_rows
    last = next_index is None
    indices = [other_live, other_index] + ([] if last else [next_index])

    def body(*refs):
        live_ref, index_ref = refs[:2]
        next_ref = refs[len(indices) - 1]
        refs = list(refs[len(indices) :])
        total_hbm = refs.pop(0)
        back_refs = [refs.pop(0) for _ in returned]
        table_hbm, state_ref, out_hbm, state_out = [refs.pop(0) for _ in range(4)]
        next_outs = [refs.pop(0) for _ in next_batches]
        total_v, table_v, rows, state_t, mean_t, sems = refs[:6]
        out_v = refs[6] if last else table_v
        load_total = pltpu.make_async_copy(total_hbm, total_v, sems.at[0])
        load_table = pltpu.make_async_copy(table_hbm, table_v, sems.at[1])
        load_total.start()
        load_table.start()
        spare = jnp.zeros((LANES - groups, LANES), jnp.float32)
        state_t[...] = jnp.concatenate([state_ref[...], spare], axis=0).T
        mean_t[...] = jnp.zeros_like(mean_t)
        load_total.wait()
        for place, ref in enumerate(back_refs):

            @pl.when(first + place < live_ref[0])
            def _():
                spread(ref, rows)
                scatter_rows(index_ref, first + place, count, rows, total_v)

        load_table.wait()
        lane = lax.broadcasted_iota(jnp.int32, (LANES, LANES), 1)
        saves = []
        for step in range(steps):

            @pl.loop(step * step_rows // LANES, (step + 1) * step_rows // LANES)
            def _(group):
                base = pl.multiple_of(group * LANES, LANES)
                sides = [half(base, LANES, side) for side in range(2)]
                grads = [total_v[side, :] for side in sides]
                square = grads[0] * grads[0] + grads[1] * grads[1]
                mean = jnp.sum(square, axis=1, keepdims=True) * (1.0 / width)
                mine = lane == group
                old = jnp.sum(jnp.where(mine, state_t[...], 0.0), axis=1, keepdims=True)
                mean_t[...] = jnp.where(mine, mean, mean_t[...])
                scale = learn_rate / jnp.sqrt(old + mean)
                for number, side in enumerate(sides):
                    value = table_v[side, :] - grads[number] * scale
                    if last:
                        out_v[pl.ds(base, LANES), number * LANES : (number + 1) * LANES] = value
                    else:
                        out_v[side, :] = value

            tall = step_rows if last else 2 * step_rows
            part = pl.ds(step * tall, tall)
            save = pltpu.make_async_copy(out_v.at[part], out_hbm.at[part], sems.at[2 + step])
            save.start()
            saves.append(save)
        state_out[...] = (state_t[...] + mean_t[...]).T[:groups]
        for out, batch in zip(next_outs, next_batches):
            gather_rows(next_ref, batch, count, table_v, rows, out)
        for save in saves:
            save.wait()

    out_shape = (row_count, width) if last else table.shape
    return pl.pallas_call(
        body,
        out_shape=[
            jax.ShapeDtypeStruct(out_shape, jnp.float32),
            jax.ShapeDtypeStruct((groups, LANES), jnp.float32),
        ]
        + [jax.ShapeDtypeStruct((height, width), jnp.bfloat16)] * len(next_batches),
        in_specs=[SMEM] * len(indices) + [ANY] + [VMEM] * len(returned) + [ANY, VMEM],
        out_specs=[ANY, VMEM] + [VMEM] * len(next_batches),
        scratch_shapes=[
            pltpu.VMEM(table.shape, jnp.float32),
            pltpu.VMEM(table.shape, jnp.float32),
            pltpu.VMEM((2 * height, LANES), jnp.float32),
            pltpu.VMEM((LANES, LANES), jnp.float32),
            pltpu.VMEM((LANES, LANES), jnp.float32),
            pltpu.SemaphoreType.DMA((2 + steps,)),
        ]
        + ([pltpu.VMEM((row_count, width), jnp.float32)] if last else []),
        compiler_params=params(36 if last else 28),
        cost_estimate=cost(50_000_000),
        name="finish_last" if last else "finish_next",
    )(*indices, total, *returned, table, state)


def flip(index, bits):
    for place in range(8):
        step = 1 << place
        if bits & step:
            index = index + step * (1 - 2 * ((index // step) % 2))
    return index


def relation_kernel(stages, near, relations, rel_state, new_relations, new_state, *scratch):
    parts, received = scratch[:-3], scratch[-3]
    send_sems, recv_sems = scratch[-2:]
    dom, rep = lax.axis_index("dom"), lax.axis_index("rep")

    def device(peer):
        return (flip(dom, peer[0]), flip(rep, peer[1]))

    barrier = pltpu.get_barrier_semaphore()
    peers = [peer for stage in stages for peer in stage]
    for peer in peers:
        pl.semaphore_signal(
            barrier, inc=1, device_id=device(peer), device_id_type=pl.DeviceIdType.MESH
        )
    pl.semaphore_wait(barrier, len(peers))
    parts[0][...] = pair_sum([ref[...] for ref in near])
    slot = 0
    for number, stage in enumerate(stages):
        copies = []
        for peer in stage:
            copy = pltpu.make_async_remote_copy(
                src_ref=parts[number],
                dst_ref=received.at[slot],
                send_sem=send_sems.at[slot],
                recv_sem=recv_sems.at[slot],
                device_id=device(peer),
                device_id_type=pl.DeviceIdType.MESH,
            )
            copy.start()
            copies.append(copy)
            slot += 1
        for copy in copies:
            copy.wait()
        first = slot - len(stage)
        total = pair_sum([parts[number][...]] + [received[first + i] for i in range(len(stage))])
        if number + 1 < len(stages):
            parts[number + 1][...] = total
    state = rel_state[...] + total * total
    new_state[...] = state
    new_relations[...] = relations[...] - rel_rate * total / jnp.sqrt(state)


def pair_sum(values):
    while len(values) > 1:
        values = [values[i] + values[i + 1] for i in range(0, len(values), 2)]
    return values[0]


def relation_step(near, relations, rel_state):
    stages = [
        [(0, 1), (0, 2), (0, 3)],
        [(1, 0), (2, 0), (3, 0)],
        [(4, 0)],
    ]
    slots = sum(len(stage) for stage in stages)
    shape = relations.shape
    count = len(near)

    def body(*refs):
        relation_kernel(stages, refs[:count], *refs[count:])

    return pl.pallas_call(
        body,
        out_shape=[jax.ShapeDtypeStruct(shape, jnp.float32)] * 2,
        in_specs=[VMEM] * (count + 2),
        out_specs=[VMEM] * 2,
        scratch_shapes=[pltpu.VMEM(shape, jnp.float32)] * len(stages)
        + [
            pltpu.VMEM((slots,) + shape, jnp.float32),
            pltpu.SemaphoreType.DMA((slots,)),
            pltpu.SemaphoreType.DMA((slots,)),
        ],
        compiler_params=pltpu.CompilerParams(
            collective_id=0, has_side_effects=True, vmem_limit_bytes=8 * 1024 * 1024
        ),
        cost_estimate=cost(30_000_000),
        name="relation_step",
    )(*near, relations, rel_state)


def from_partner(shard, axis, distance):
    return from_peer(shard, axis, 1 << distance)


def from_peer(shard, axis, bits):
    return lax.ppermute(shard, axis, [(i, i ^ bits) for i in range(lax.axis_size(axis))])


def on_device(
    embeddings, row_state, relations, rel_state, edge_src, edge_dst, edge_rel, batch_count
):
    bit_count = lax.axis_size("dom").bit_length() - 1
    row_count, width = embeddings.shape
    batches, count = edge_src.shape[-2:]
    padded = round_up(count, BLOCK)
    state = row_state.reshape(row_count // LANES, LANES)
    spots = [bit_count - 1 - number for number in range(ROUNDS)]
    told = []
    for number in range(ROUNDS):
        note = jnp.concatenate([edge_dst[0, 0, number].reshape(-1), batch_count[0, 0, number].reshape(1)])
        told.append(from_partner(note, "dom", spots[number]))
    told = lax.optimization_barrier(told)
    other = [note[: batches * count].reshape(batches, count) for note in told]
    firsts = (0, 1)
    others = tuple(range(len(firsts), batches))
    table, *sent = pack_first(other[0], embeddings, firsts, count)
    for number in range(ROUNDS):
        last = number + 1 == ROUNDS
        swap_bit = spots[number]
        source_index = edge_src[0, 0, number]
        other_index = other[number]
        other_live = told[number][batches * count :]
        live = batch_count[0, 0, number].reshape(1)
        kinds = jnp.pad(edge_rel[0, 0, number], ((0, 0), (0, padded - count)), constant_values=-1)
        arrived = [from_partner(rows, "dom", swap_bit) for rows in sent]
        more = pack(other_index, source_index, table, others, tuple(range(batches)), count, width)
        sources = more[len(others) :]
        arrived += [from_partner(rows, "dom", swap_bit) for rows in more[: len(others)]]
        rel_grad = jnp.zeros(relations.shape, jnp.float32)
        own, returned = [], []
        for batch in range(batches):
            grad_source, grad_target, rel_grad = run_batch(
                batch, count, live, kinds[batch][None], sources[batch], arrived[batch], relations, rel_grad
            )
            own.append(grad_source)
            if batch == batches - 1:
                near = [rel_grad] + [from_peer(rel_grad, "dom", bits) for bits in (8, 16, 24)]
            returned.append(from_partner(grad_target, "dom", swap_bit))
        early = batches - 2
        total = first_total(
            count, row_count, live, other_live, source_index, other_index, own, returned[:early]
        )
        near, total = lax.optimization_barrier((near, total))
        relations, rel_state = relation_step(near, relations, rel_state)
        relations, total = lax.optimization_barrier((relations, total))
        table, state, *sent = finish(
            count,
            other_live,
            other_index,
            total,
            returned[early:],
            early,
            table,
            state,
            width,
            None if last else other[number + 1],
            () if last else firsts,
        )
    return (table, state.reshape(row_count), relations, rel_state)


def solution(mesh):
    return jax.shard_map(
        on_device,
        mesh=mesh,
        in_specs=(
            P(("dom", "rep"), None),
            P(("dom", "rep")),
            P(),
            P(),
            P("dom", "rep", None, None, None),
            P("dom", "rep", None, None, None),
            P("dom", "rep", None, None, None),
            P("dom", "rep", None),
        ),
        out_specs=(P(("dom", "rep"), None), P(("dom", "rep")), P(), P()),
        check_vma=False,
    )
```

```python
import functools

import jax
import jax.numpy as jnp
from jax import lax
from jax.experimental import pallas as pl
from jax.experimental.pallas import tpu as pltpu
from jax.sharding import PartitionSpec as P


ROUNDS = 2

learn_rate = 0.1
rel_rate = 0.1


SMEM = pl.BlockSpec(memory_space=pltpu.SMEM)
VMEM = pl.BlockSpec(memory_space=pltpu.VMEM)
ANY = pl.BlockSpec(memory_space=pl.ANY)
HBM = pl.BlockSpec(memory_space=pltpu.HBM)
UNROLL = 40
BLOCK = 256
LANES = 128
MIB = 1024 * 1024


def params(mib, **kw):
    return pltpu.CompilerParams(vmem_limit_bytes=mib * MIB, **kw)


def cost(nbytes):
    return pl.CostEstimate(flops=0, bytes_accessed=nbytes, transcendentals=0)


def round_up(n, m):
    return (n + m - 1) // m * m


def piece(row):
    return pl.ds(pl.multiple_of(row * 2, 2), 2)


def half(start, count, side):
    return pl.ds(start * 2 + side, count, stride=2)


def gather_rows(index_ref, batch, count, table, rows, out):
    @pl.loop(0, count // UNROLL)
    def _(step):
        base = step * UNROLL
        for j in range(UNROLL):
            rows[piece(base + j), :] = table[piece(index_ref[batch, base + j]), :]

    height = out.shape[0]
    if height > count:
        rows[2 * count : 2 * height, :] = jnp.zeros((2 * (height - count), LANES), rows.dtype)
    for side in range(2):
        out[:, side * LANES : (side + 1) * LANES] = rows[half(0, height, side), :].astype(out.dtype)


def scatter_rows(index_ref, batch, count, rows, total):
    @pl.loop(0, count // UNROLL)
    def _(step):
        base = step * UNROLL
        for j in range(UNROLL):
            row = piece(index_ref[batch, base + j])
            total[row, :] += rows[piece(base + j), :]


def spread(ref, rows):
    for side in range(2):
        rows[half(0, ref.shape[0], side), :] = ref[:, side * LANES : (side + 1) * LANES].astype(
            jnp.float32
        )


def pack_first(index, table, edge_dst, edge_rel, batch_count, batches):
    rounds, slots, count = edge_dst.shape
    height = round_up(count, 16)
    row_count, width = table.shape
    parts = 8
    part_rows = row_count // parts

    def body(index_ref, count_ref, table_hbm, dst_ref, rel_ref, long_hbm, *refs):
        notes, refs = refs[:rounds], refs[rounds:]
        outs, (table_v, long_v, rows, sems) = refs[:-4], refs[-4:]
        loads = []
        for part in range(parts):
            here = pl.ds(part * part_rows, part_rows)
            load = pltpu.make_async_copy(table_hbm.at[here], table_v.at[here], sems.at[part])
            load.start()
            loads.append(load)
        for number, note in enumerate(notes):
            note[:slots] = dst_ref[number]
            note[slots : 2 * slots] = rel_ref[number]
            note[2 * slots :] = jnp.full((1, count), count_ref[number], jnp.int32)
        for part in range(parts):
            loads[part].wait()

            @pl.loop(part * part_rows // LANES, (part + 1) * part_rows // LANES)
            def _(step):
                here = pl.multiple_of(step * LANES, LANES)
                for side in range(2):
                    long_v[half(here, LANES, side), :] = table_v[
                        pl.ds(here, LANES), side * LANES : (side + 1) * LANES
                    ]

        save = pltpu.make_async_copy(long_v, long_hbm, sems.at[parts])
        save.start()
        for out, batch in zip(outs, batches):
            gather_rows(index_ref, batch, count, long_v, rows, out)
        save.wait()

    return pl.pallas_call(
        body,
        out_shape=[jax.ShapeDtypeStruct((2 * row_count, LANES), jnp.float32)]
        + [jax.ShapeDtypeStruct((2 * slots + 1, count), jnp.int32)] * rounds
        + [jax.ShapeDtypeStruct((height, width), jnp.bfloat16)] * len(batches),
        in_specs=[SMEM, SMEM, HBM, VMEM, VMEM],
        out_specs=[HBM] + [VMEM] * (rounds + len(batches)),
        scratch_shapes=[
            pltpu.VMEM((row_count, width), jnp.float32),
            pltpu.VMEM((2 * row_count, LANES), jnp.float32),
            pltpu.VMEM((2 * height, LANES), jnp.float32),
            pltpu.SemaphoreType.DMA((parts + 1,)),
        ],
        compiler_params=params(56),
        cost_estimate=cost(25_000_000),
        name="pack_first",
    )(index, batch_count, table, edge_dst, edge_rel)


def pack(index, table, batches, count, width):
    height = round_up(count, 16)

    def body(index_ref, table_hbm, *refs):
        outs, (table_v, rows, sem) = refs[:-3], refs[-3:]
        pltpu.make_async_copy(table_hbm, table_v, sem).start()
        pltpu.make_async_copy(table_hbm, table_v, sem).wait()
        for out, batch in zip(outs, batches):
            gather_rows(index_ref, batch, count, table_v, rows, out)

    return pl.pallas_call(
        body,
        out_shape=[jax.ShapeDtypeStruct((height, width), jnp.bfloat16)] * len(batches),
        in_specs=[SMEM, HBM],
        out_specs=[VMEM] * len(batches),
        scratch_shapes=[
            pltpu.VMEM(table.shape, jnp.float32),
            pltpu.VMEM((2 * height, LANES), jnp.float32),
            pltpu.SemaphoreType.DMA,
        ],
        compiler_params=params(54),
        cost_estimate=cost(30_000_000),
    )(index, table)


def batch_kernel(batch, count, live_ref, kind_ref, source_ref, target_ref, rel_ref, rel_in,
                 grad_source, grad_target, rel_out, query_t, total_t, product):
    height, width = source_ref.shape
    full = round_up(height, BLOCK)
    kinds = rel_ref.shape[0]
    neg_share = 0.5 / (count - 1)

    @pl.when(batch >= live_ref[0])
    def _():
        rel_out[...] = rel_in[...]

    @pl.when(batch < live_ref[0])
    def _():
        rel = rel_ref[...]
        high = rel.astype(jnp.bfloat16)
        rest = rel - high.astype(jnp.float32)
        mid = rest.astype(jnp.bfloat16)
        low = (rest - mid.astype(jnp.float32)).astype(jnp.bfloat16)
        parts = jnp.concatenate([high, mid, low], axis=0)
        kind = jnp.broadcast_to(kind_ref[...], (3 * kinds, full))
        row = lax.broadcasted_iota(jnp.int32, (3 * kinds, full), 0)
        hot = jnp.where((row % kinds) == kind, 1.0, 0.0).astype(jnp.bfloat16)
        diagonal = lax.dot_general(
            hot, parts, (((0,), (0,)), ((), ())), preferred_element_type=jnp.float32
        )
        source = source_ref[...].astype(jnp.float32)
        target = target_ref[...]
        if full > height:
            gap = jnp.zeros((full - height, width), jnp.float32)
            source = jnp.concatenate([source, gap], axis=0)
            target = jnp.concatenate([target, gap.astype(target.dtype)], axis=0)
        query_full = (source * diagonal).astype(jnp.bfloat16).astype(jnp.float32)
        query_t[...] = query_full.T.astype(jnp.bfloat16)
        half_query = (query_full * 0.5).astype(jnp.bfloat16)
        eye = lax.broadcasted_iota(jnp.int32, (BLOCK, BLOCK), 0) == lax.broadcasted_iota(
            jnp.int32, (BLOCK, BLOCK), 1
        )
        for block in range(full // BLOCK):
            here = slice(block * BLOCK, (block + 1) * BLOCK)
            pieces = []
            for col in range(full // BLOCK):
                there = slice(col * BLOCK, (col + 1) * BLOCK)
                slope = jnp.tanh(
                    lax.dot_general(
                        half_query[here],
                        target[there],
                        (((1,), (1,)), ((), ())),
                        preferred_element_type=jnp.float32,
                    )
                )
                weight = slope * neg_share + neg_share
                if col == block:
                    weight = jnp.where(eye, slope * 0.5 - 0.5, weight)
                pieces.append(weight.astype(jnp.bfloat16))
            weights = jnp.concatenate(pieces, axis=1)
            grad_query = jnp.dot(weights, target, preferred_element_type=jnp.float32)
            tall = min(height - block * BLOCK, BLOCK)
            grad_rows = (grad_query * diagonal[here])[:tall]
            grad_source[block * BLOCK : block * BLOCK + tall, :] = grad_rows.astype(
                grad_source.dtype
            )
            product[here, :] = grad_query * source[here]
            part = jnp.dot(query_t[:, here], weights, preferred_element_type=jnp.float32)
            if block == 0:
                total_t[...] = part
            else:
                total_t[...] += part
        grad_rows = total_t[...].T[:height]
        for side in range(2):
            grad_target[half(0, height, side), :] = grad_rows[:, side * LANES : (side + 1) * LANES]
        value = product[...]
        upper = value.astype(jnp.bfloat16)
        lower = (value - upper.astype(jnp.float32)).astype(jnp.bfloat16)
        one = hot[:kinds]
        rel_out[...] = (
            rel_in[...]
            + jnp.dot(one, upper, preferred_element_type=jnp.float32)
            + jnp.dot(one, lower, preferred_element_type=jnp.float32)
        )


def run_batch(batch, count, live, kind, source, target, relations, rel_grad):
    height, width = source.shape
    full = round_up(height, BLOCK)
    return pl.pallas_call(
        functools.partial(batch_kernel, batch, count),
        out_shape=[
            jax.ShapeDtypeStruct((height, width), jnp.bfloat16),
            jax.ShapeDtypeStruct((2 * height, LANES), jnp.float32),
            jax.ShapeDtypeStruct(rel_grad.shape, jnp.float32),
        ],
        in_specs=[SMEM] + [VMEM] * 5,
        out_specs=[VMEM] * 3,
        scratch_shapes=[
            pltpu.VMEM((width, full), jnp.bfloat16),
            pltpu.VMEM((width, full), jnp.float32),
            pltpu.VMEM((full, width), jnp.float32),
        ],
        compiler_params=params(16),
        cost_estimate=cost(15_000_000),
        name="batch_terms",
    )(live, kind, source, target, relations, rel_grad)


def first_total(count, row_count, live, other_live, source_index, other_index, own, returned):
    def body(live_ref, other_ref, source_ref, index_ref, *refs):
        own_refs = refs[: len(own)]
        back_refs = refs[len(own) : -2]
        total, rows = refs[-2:]
        total[...] = jnp.zeros_like(total)
        for batch, ref in enumerate(own_refs):

            @pl.when(batch < live_ref[0])
            def _():
                scatter_rows(source_ref, batch, count, ref, total)

        for batch, ref in enumerate(back_refs):

            @pl.when(batch < other_ref[0])
            def _():
                spread(ref, rows)
                scatter_rows(index_ref, batch, count, rows, total)

    return pl.pallas_call(
        body,
        out_shape=jax.ShapeDtypeStruct((2 * row_count, LANES), jnp.float32),
        in_specs=[SMEM] * 4 + [VMEM] * (len(own) + len(returned)),
        out_specs=VMEM,
        scratch_shapes=[pltpu.VMEM(own[0].shape, jnp.float32)],
        compiler_params=params(20),
        cost_estimate=cost(60_000_000),
        name="first_total",
    )(live, other_live, source_index, other_index, *own, *returned)


def finish(count, other_live, other_index, total, returned, first, table, state, width, next_index, next_batches):
    row_count = table.shape[0] // 2
    height = returned[0].shape[0]
    groups = row_count // LANES
    step_rows = 1024
    steps = row_count // step_rows
    last = next_index is None
    indices = [other_live, other_index] + ([] if last else [next_index])

    def body(*refs):
        live_ref, index_ref = refs[:2]
        next_ref = refs[len(indices) - 1]
        refs = list(refs[len(indices) :])
        total_hbm = refs.pop(0)
        back_refs = [refs.pop(0) for _ in returned]
        table_hbm, state_ref, out_hbm, state_out = [refs.pop(0) for _ in range(4)]
        next_outs = [refs.pop(0) for _ in next_batches]
        total_v, table_v, rows, state_t, mean_t, sems = refs[:6]
        out_v = refs[6] if last else table_v
        load_total = pltpu.make_async_copy(total_hbm, total_v, sems.at[0])
        load_table = pltpu.make_async_copy(table_hbm, table_v, sems.at[1])
        load_total.start()
        load_table.start()
        spare = jnp.zeros((LANES - groups, LANES), jnp.float32)
        state_t[...] = jnp.concatenate([state_ref[...], spare], axis=0).T
        mean_t[...] = jnp.zeros_like(mean_t)
        load_total.wait()
        for place, ref in enumerate(back_refs):

            @pl.when(first + place < live_ref[0])
            def _():
                spread(ref, rows)
                scatter_rows(index_ref, first + place, count, rows, total_v)

        load_table.wait()
        lane = lax.broadcasted_iota(jnp.int32, (LANES, LANES), 1)
        saves = []
        for step in range(steps):

            @pl.loop(step * step_rows // LANES, (step + 1) * step_rows // LANES)
            def _(group):
                base = pl.multiple_of(group * LANES, LANES)
                sides = [half(base, LANES, side) for side in range(2)]
                grads = [total_v[side, :] for side in sides]
                square = grads[0] * grads[0] + grads[1] * grads[1]
                mean = jnp.sum(square, axis=1, keepdims=True) * (1.0 / width)
                mine = lane == group
                old = jnp.sum(jnp.where(mine, state_t[...], 0.0), axis=1, keepdims=True)
                mean_t[...] = jnp.where(mine, mean, mean_t[...])
                scale = learn_rate / jnp.sqrt(old + mean)
                values = [table_v[side, :] - grad * scale for side, grad in zip(sides, grads)]
                for number, value in enumerate(values):
                    if last:
                        out_v[pl.ds(base, LANES), number * LANES : (number + 1) * LANES] = value
                    else:
                        out_v[sides[number], :] = value

            tall = step_rows if last else 2 * step_rows
            part = pl.ds(step * tall, tall)
            save = pltpu.make_async_copy(out_v.at[part], out_hbm.at[part], sems.at[2 + step])
            save.start()
            saves.append(save)
        state_out[...] = (state_t[...] + mean_t[...]).T[:groups]
        for out, batch in zip(next_outs, next_batches):
            gather_rows(next_ref, batch, count, table_v, rows, out)
        for save in saves:
            save.wait()

    out_shape = (row_count, width) if last else table.shape
    return pl.pallas_call(
        body,
        out_shape=[
            jax.ShapeDtypeStruct(out_shape, jnp.float32),
            jax.ShapeDtypeStruct((groups, LANES), jnp.float32),
        ]
        + [jax.ShapeDtypeStruct((height, width), jnp.bfloat16)] * len(next_batches),
        in_specs=[SMEM] * len(indices) + [ANY] + [VMEM] * len(returned) + [HBM, VMEM],
        out_specs=[HBM, VMEM] + [VMEM] * len(next_batches),
        scratch_shapes=[
            pltpu.VMEM(table.shape, jnp.float32),
            pltpu.VMEM(table.shape, jnp.float32),
            pltpu.VMEM((2 * height, LANES), jnp.float32),
            pltpu.VMEM((LANES, LANES), jnp.float32),
            pltpu.VMEM((LANES, LANES), jnp.float32),
            pltpu.SemaphoreType.DMA((2 + steps,)),
        ]
        + ([pltpu.VMEM((row_count, width), jnp.float32)] if last else []),
        compiler_params=params(28 if last else 22),
        cost_estimate=cost(50_000_000),
        name="finish_last" if last else "finish_next",
    )(*indices, total, *returned, table, state)


def flip(index, bits):
    for place in range(8):
        step = 1 << place
        if bits & step:
            index = index + step * (1 - 2 * ((index // step) % 2))
    return index


def relation_kernel(stages, near, relations, rel_state, new_relations, new_state, *scratch):
    parts, received = scratch[:-3], scratch[-3]
    send_sems, recv_sems = scratch[-2:]
    dom, rep = lax.axis_index("dom"), lax.axis_index("rep")

    def device(peer):
        return (flip(dom, peer[0]), flip(rep, peer[1]))

    barrier = pltpu.get_barrier_semaphore()
    peers = [peer for stage in stages for peer in stage]
    for peer in peers:
        pl.semaphore_signal(
            barrier, inc=1, device_id=device(peer), device_id_type=pl.DeviceIdType.MESH
        )
    pl.semaphore_wait(barrier, len(peers))
    parts[0][...] = pair_sum([ref[...] for ref in near])
    slot = 0
    for number, stage in enumerate(stages):
        copies = []
        for peer in stage:
            copy = pltpu.make_async_remote_copy(
                src_ref=parts[number],
                dst_ref=received.at[slot],
                send_sem=send_sems.at[slot],
                recv_sem=recv_sems.at[slot],
                device_id=device(peer),
                device_id_type=pl.DeviceIdType.MESH,
            )
            copy.start()
            copies.append(copy)
            slot += 1
        for copy in copies:
            copy.wait()
        first = slot - len(stage)
        total = pair_sum([parts[number][...]] + [received[first + i] for i in range(len(stage))])
        if number + 1 < len(stages):
            parts[number + 1][...] = total
    state = rel_state[...] + total * total
    new_state[...] = state
    new_relations[...] = relations[...] - rel_rate * total / jnp.sqrt(state)


def pair_sum(values):
    while len(values) > 1:
        values = [values[i] + values[i + 1] for i in range(0, len(values), 2)]
    return values[0]


def relation_step(near, relations, rel_state):
    stages = [
        [(0, 1), (0, 2), (0, 3)],
        [(1, 0), (2, 0), (3, 0)],
        [(4, 0)],
    ]
    slots = sum(len(stage) for stage in stages)
    shape = relations.shape
    count = len(near)

    def body(*refs):
        relation_kernel(stages, refs[:count], *refs[count:])

    return pl.pallas_call(
        body,
        out_shape=[jax.ShapeDtypeStruct(shape, jnp.float32)] * 2,
        in_specs=[VMEM] * (count + 2),
        out_specs=[VMEM] * 2,
        scratch_shapes=[pltpu.VMEM(shape, jnp.float32)] * len(stages)
        + [
            pltpu.VMEM((slots,) + shape, jnp.float32),
            pltpu.SemaphoreType.DMA((slots,)),
            pltpu.SemaphoreType.DMA((slots,)),
        ],
        compiler_params=pltpu.CompilerParams(
            collective_id=0, has_side_effects=True, vmem_limit_bytes=8 * 1024 * 1024
        ),
        cost_estimate=cost(30_000_000),
        name="relation_step",
    )(*near, relations, rel_state)


def from_partner(shard, axis, distance):
    return from_peer(shard, axis, 1 << distance)


def from_peer(shard, axis, bits):
    return lax.ppermute(shard, axis, [(i, i ^ bits) for i in range(lax.axis_size(axis))])


def on_device(
    embeddings, row_state, relations, rel_state, edge_src, edge_dst, edge_rel, batch_count
):
    bit_count = lax.axis_size("dom").bit_length() - 1
    row_count, width = embeddings.shape
    batches, count = edge_src.shape[-2:]
    padded = round_up(count, BLOCK)
    state = row_state.reshape(row_count // LANES, LANES)
    spots = [bit_count - 1 - number for number in range(ROUNDS)]
    firsts = (0,)
    others = tuple(range(len(firsts), batches))
    table, *told = pack_first(
        edge_src[0, 0, 0], embeddings, edge_dst[0, 0], edge_rel[0, 0], batch_count[0, 0], firsts
    )
    told, sent = told[:ROUNDS], told[ROUNDS:]
    for number in range(ROUNDS):
        last = number + 1 == ROUNDS
        swap_bit = spots[number]
        source_index = edge_src[0, 0, number]
        live = batch_count[0, 0, number].reshape(1)
        note = from_partner(told[number], "dom", swap_bit)
        arrived = []
        for rows in sent:
            arrived.append(from_partner(rows, "dom", swap_bit))
        more = pack(source_index, table, others, count, width)
        for batch, rows in zip(others, more):
            arrived.append(from_partner(rows, "dom", swap_bit))
        other_index = note[:batches]
        other_live = note[2 * batches, :1]
        kinds = jnp.pad(
            note[batches : 2 * batches], ((0, 0), (0, padded - count)), constant_values=-1
        )
        targets = pack(other_index, table, tuple(range(batches)), count, width)
        rel_grad = jnp.zeros(relations.shape, jnp.float32)
        own, returned = [], []
        for batch in range(batches):
            grad_source, grad_target, rel_grad = run_batch(
                batch,
                count,
                other_live,
                kinds[batch][None],
                arrived[batch],
                targets[batch],
                relations,
                rel_grad,
            )
            own.append(grad_target)
            if batch == batches - 1:
                near = [rel_grad]
                for bits in (8, 16, 24):
                    near.append(from_peer(rel_grad, "dom", bits))
            returned.append(from_partner(grad_source, "dom", swap_bit))
        early = batches - 2
        total = first_total(
            count, row_count, other_live, live, other_index, source_index, own, returned[:early]
        )
        near, total = lax.optimization_barrier((near, total))
        relations, rel_state = relation_step(near, relations, rel_state)
        relations, total = lax.optimization_barrier((relations, total))
        table, state, *sent = finish(
            count,
            live,
            source_index,
            total,
            returned[early:],
            early,
            table,
            state,
            width,
            None if last else edge_src[0, 0, number + 1],
            () if last else firsts,
        )
    return (table, state.reshape(row_count), relations, rel_state)


def solution(mesh):
    return sharded(mesh)


def sharded(mesh):
    return jax.shard_map(
        on_device,
        mesh=mesh,
        in_specs=(
            P(("dom", "rep"), None),
            P(("dom", "rep")),
            P(),
            P(),
            P("dom", "rep", None, None, None),
            P("dom", "rep", None, None, None),
            P("dom", "rep", None, None, None),
            P("dom", "rep", None),
        ),
        out_specs=(P(("dom", "rep"), None), P(("dom", "rep")), P(), P()),
        check_vma=False,
    )
```

```python
import functools

import jax
import jax.numpy as jnp
from jax import lax
from jax.experimental import pallas as pl
from jax.experimental.pallas import tpu as pltpu
from jax.sharding import PartitionSpec as P


ROUNDS = 2

learn_rate = 0.1
rel_rate = 0.1


SMEM = pl.BlockSpec(memory_space=pltpu.SMEM)
VMEM = pl.BlockSpec(memory_space=pltpu.VMEM)
ANY = pl.BlockSpec(memory_space=pl.ANY)
HBM = pl.BlockSpec(memory_space=pltpu.HBM)
GATHER_UNROLL = 20
SCATTER_UNROLL = 8
BLOCK = 256
LANES = 128
MIB = 1024 * 1024


def params(mib, **kw):
    return pltpu.CompilerParams(vmem_limit_bytes=mib * MIB, **kw)


def cost(nbytes):
    return pl.CostEstimate(flops=0, bytes_accessed=nbytes, transcendentals=0)


def round_up(n, m):
    return (n + m - 1) // m * m


def piece(row):
    return pl.ds(pl.multiple_of(row * 2, 2), 2)


def half(start, count, side):
    return pl.ds(start * 2 + side, count, stride=2)


def gather_rows(index_ref, batch, count, table, rows, out):
    @pl.loop(0, count // GATHER_UNROLL)
    def _(step):
        base = step * GATHER_UNROLL
        for j in range(GATHER_UNROLL):
            rows[piece(base + j), :] = table[piece(index_ref[batch, base + j]), :]

    height = out.shape[0]
    if height > count:
        rows[2 * count : 2 * height, :] = jnp.zeros((2 * (height - count), LANES), rows.dtype)
    for side in range(2):
        out[:, side * LANES : (side + 1) * LANES] = rows[half(0, height, side), :].astype(out.dtype)


def scatter_rows(jobs, count):
    @pl.loop(0, count // SCATTER_UNROLL)
    def _(step):
        base = step * SCATTER_UNROLL
        for j in range(SCATTER_UNROLL):
            spots = [piece(index[batch, base + j]) for index, batch, _, _ in jobs]
            olds = [total[spot, :] for spot, (_, _, _, total) in zip(spots, jobs)]
            for spot, old, (_, _, rows, total) in zip(spots, olds, jobs):
                total[spot, :] = old + rows[piece(base + j), :]


def scatter_live(live_ref, jobs, count):
    for first in range(0, len(jobs), 2):
        pair = jobs[first : first + 2]
        if len(pair) == 2:

            @pl.when(pair[1][1] < live_ref[0])
            def _():
                scatter_rows(pair, count)

        @pl.when((pair[0][1] < live_ref[0]) & (pair[-1][1] >= live_ref[0]))
        def _():
            scatter_rows(pair[:1], count)


def spread(ref, rows):
    for side in range(2):
        rows[half(0, ref.shape[0], side), :] = ref[:, side * LANES : (side + 1) * LANES].astype(
            jnp.float32
        )


def pack_first(index, table, edge_dst, edge_rel, batch_count, batches):
    rounds, slots, count = edge_dst.shape
    height = round_up(count, 16)
    row_count, width = table.shape
    parts = 8
    part_rows = row_count // parts

    def body(index_ref, count_ref, table_hbm, dst_ref, rel_ref, long_hbm, *refs):
        notes, refs = refs[:rounds], refs[rounds:]
        outs, (table_v, long_v, rows, sems) = refs[:-4], refs[-4:]
        loads = []
        for part in range(parts):
            here = pl.ds(part * part_rows, part_rows)
            load = pltpu.make_async_copy(table_hbm.at[here], table_v.at[here], sems.at[part])
            load.start()
            loads.append(load)
        for number, note in enumerate(notes):
            note[:slots] = dst_ref[number]
            note[slots : 2 * slots] = rel_ref[number]
            note[2 * slots :] = jnp.full((1, count), count_ref[number], jnp.int32)
        for part in range(parts):
            loads[part].wait()

            @pl.loop(part * part_rows // LANES, (part + 1) * part_rows // LANES)
            def _(step):
                here = pl.multiple_of(step * LANES, LANES)
                for side in range(2):
                    long_v[half(here, LANES, side), :] = table_v[
                        pl.ds(here, LANES), side * LANES : (side + 1) * LANES
                    ]

        save = pltpu.make_async_copy(long_v, long_hbm, sems.at[parts])
        save.start()
        for out, batch in zip(outs, batches):
            gather_rows(index_ref, batch, count, long_v, rows, out)
        save.wait()

    return pl.pallas_call(
        body,
        out_shape=[jax.ShapeDtypeStruct((2 * row_count, LANES), jnp.float32)]
        + [jax.ShapeDtypeStruct((2 * slots + 1, count), jnp.int32)] * rounds
        + [jax.ShapeDtypeStruct((height, width), jnp.bfloat16)] * len(batches),
        in_specs=[SMEM, SMEM, HBM, VMEM, VMEM],
        out_specs=[HBM] + [VMEM] * (rounds + len(batches)),
        scratch_shapes=[
            pltpu.VMEM((row_count, width), jnp.float32),
            pltpu.VMEM((2 * row_count, LANES), jnp.float32),
            pltpu.VMEM((2 * height, LANES), jnp.float32),
            pltpu.SemaphoreType.DMA((parts + 1,)),
        ],
        compiler_params=params(56),
        cost_estimate=cost(25_000_000),
        name="pack_first",
    )(index, batch_count, table, edge_dst, edge_rel)


def pack(index, table, batches, count, width):
    height = round_up(count, 16)

    def body(index_ref, table_hbm, *refs):
        outs, (table_v, rows, sem) = refs[:-3], refs[-3:]
        pltpu.make_async_copy(table_hbm, table_v, sem).start()
        pltpu.make_async_copy(table_hbm, table_v, sem).wait()
        for out, batch in zip(outs, batches):
            gather_rows(index_ref, batch, count, table_v, rows, out)

    return pl.pallas_call(
        body,
        out_shape=[jax.ShapeDtypeStruct((height, width), jnp.bfloat16)] * len(batches),
        in_specs=[SMEM, HBM],
        out_specs=[VMEM] * len(batches),
        scratch_shapes=[
            pltpu.VMEM(table.shape, jnp.float32),
            pltpu.VMEM((2 * height, LANES), jnp.float32),
            pltpu.SemaphoreType.DMA,
        ],
        compiler_params=params(54),
        cost_estimate=cost(30_000_000),
    )(index, table)


def batch_kernel(batch, count, live_ref, kind_ref, source_ref, target_ref, rel_ref, rel_in,
                 grad_source, grad_target, rel_out, query_t, total_t, product):
    height, width = source_ref.shape
    full = round_up(height, BLOCK)
    kinds = rel_ref.shape[0]
    neg_share = 0.5 / (count - 1)

    @pl.when(batch >= live_ref[0])
    def _():
        rel_out[...] = rel_in[...]

    @pl.when(batch < live_ref[0])
    def _():
        rel = rel_ref[...]
        high = rel.astype(jnp.bfloat16)
        rest = rel - high.astype(jnp.float32)
        mid = rest.astype(jnp.bfloat16)
        low = (rest - mid.astype(jnp.float32)).astype(jnp.bfloat16)
        parts = jnp.concatenate([high, mid, low], axis=0)
        kind = jnp.broadcast_to(kind_ref[...], (3 * kinds, full))
        row = lax.broadcasted_iota(jnp.int32, (3 * kinds, full), 0)
        hot = jnp.where((row % kinds) == kind, 1.0, 0.0).astype(jnp.bfloat16)
        diagonal = lax.dot_general(
            hot, parts, (((0,), (0,)), ((), ())), preferred_element_type=jnp.float32
        )
        source = source_ref[...].astype(jnp.float32)
        target = target_ref[...]
        if full > height:
            gap = jnp.zeros((full - height, width), jnp.float32)
            source = jnp.concatenate([source, gap], axis=0)
            target = jnp.concatenate([target, gap.astype(target.dtype)], axis=0)
        query_full = (source * diagonal).astype(jnp.bfloat16).astype(jnp.float32)
        query_t[...] = query_full.T.astype(jnp.bfloat16)
        half_query = (query_full * 0.5).astype(jnp.bfloat16)
        eye = lax.broadcasted_iota(jnp.int32, (BLOCK, BLOCK), 0) == lax.broadcasted_iota(
            jnp.int32, (BLOCK, BLOCK), 1
        )
        for block in range(full // BLOCK):
            here = slice(block * BLOCK, (block + 1) * BLOCK)
            pieces = []
            for col in range(full // BLOCK):
                there = slice(col * BLOCK, (col + 1) * BLOCK)
                slope = jnp.tanh(
                    lax.dot_general(
                        half_query[here],
                        target[there],
                        (((1,), (1,)), ((), ())),
                        preferred_element_type=jnp.float32,
                    )
                )
                weight = slope * neg_share + neg_share
                if col == block:
                    weight = jnp.where(eye, slope * 0.5 - 0.5, weight)
                pieces.append(weight.astype(jnp.bfloat16))
            weights = jnp.concatenate(pieces, axis=1)
            grad_query = jnp.dot(weights, target, preferred_element_type=jnp.float32)
            tall = min(height - block * BLOCK, BLOCK)
            grad_rows = (grad_query * diagonal[here])[:tall]
            grad_source[block * BLOCK : block * BLOCK + tall, :] = grad_rows.astype(
                grad_source.dtype
            )
            product[here, :] = grad_query * source[here]
            part = jnp.dot(query_t[:, here], weights, preferred_element_type=jnp.float32)
            if block == 0:
                total_t[...] = part
            else:
                total_t[...] += part
        grad_rows = total_t[...].T[:height]
        for side in range(2):
            grad_target[half(0, height, side), :] = grad_rows[:, side * LANES : (side + 1) * LANES]
        value = product[...]
        upper = value.astype(jnp.bfloat16)
        lower = (value - upper.astype(jnp.float32)).astype(jnp.bfloat16)
        one = hot[:kinds]
        rel_out[...] = (
            rel_in[...]
            + jnp.dot(one, upper, preferred_element_type=jnp.float32)
            + jnp.dot(one, lower, preferred_element_type=jnp.float32)
        )


def run_batch(batch, count, live, kind, source, target, relations, rel_grad):
    height, width = source.shape
    full = round_up(height, BLOCK)
    return pl.pallas_call(
        functools.partial(batch_kernel, batch, count),
        out_shape=[
            jax.ShapeDtypeStruct((height, width), jnp.bfloat16),
            jax.ShapeDtypeStruct((2 * height, LANES), jnp.float32),
            jax.ShapeDtypeStruct(rel_grad.shape, jnp.float32),
        ],
        in_specs=[SMEM] + [VMEM] * 5,
        out_specs=[VMEM] * 3,
        scratch_shapes=[
            pltpu.VMEM((width, full), jnp.bfloat16),
            pltpu.VMEM((width, full), jnp.float32),
            pltpu.VMEM((full, width), jnp.float32),
        ],
        compiler_params=params(16),
        cost_estimate=cost(15_000_000),
        name="batch_terms",
    )(live, kind, source, target, relations, rel_grad)


def first_total(count, row_count, live, other_live, source_index, other_index, own, returned):
    def body(live_ref, other_ref, source_ref, index_ref, *refs):
        own_refs = refs[: len(own)]
        back_refs = refs[len(own) : len(own) + len(returned)]
        total, other = refs[len(own) + len(returned) :][:2]
        rows = refs[len(own) + len(returned) + 2 :]
        totals = (total, other)
        total[...] = jnp.zeros_like(total)
        other[...] = jnp.zeros_like(other)
        for ref, long in zip(back_refs, rows):
            spread(ref, long)
        scatter_live(
            live_ref,
            [(source_ref, batch, ref, totals[batch % 2]) for batch, ref in enumerate(own_refs)],
            count,
        )
        scatter_live(
            other_ref,
            [(index_ref, batch, ref, totals[batch % 2]) for batch, ref in enumerate(rows)],
            count,
        )
        total[...] += other[...]

    return pl.pallas_call(
        body,
        out_shape=jax.ShapeDtypeStruct((2 * row_count, LANES), jnp.float32),
        in_specs=[SMEM] * 4 + [VMEM] * (len(own) + len(returned)),
        out_specs=VMEM,
        scratch_shapes=[pltpu.VMEM((2 * row_count, LANES), jnp.float32)]
        + [pltpu.VMEM(own[0].shape, jnp.float32)] * len(returned),
        compiler_params=params(54),
        cost_estimate=cost(60_000_000),
        name="first_total",
    )(live, other_live, source_index, other_index, *own, *returned)


def finish(
    count, live, source_index, total, returned, first, table, state, width, near, relations, rel_state, next_index, next_batches
):
    row_count = table.shape[0] // 2
    height = returned[0].shape[0]
    groups = row_count // LANES
    step_rows = 1024
    steps = row_count // step_rows
    last = next_index is None
    indices = [live, source_index] + ([] if last else [next_index])

    def body(*refs):
        refs = list(refs)

        def take(number):
            taken = refs[:number]
            del refs[:number]
            return taken

        live_ref, index_ref, *next_ref = take(len(indices))
        (total_hbm,) = take(1)
        back_refs = take(len(returned))
        table_hbm, state_ref = take(2)
        near_refs = take(len(near))
        rel_ref, rel_state_ref, out_hbm, state_out, new_rel, new_rel_state = take(6)
        next_outs = take(len(next_batches))
        total_v, other_v, table_v, state_t, mean_t, sems = take(6)
        rows = take(len(returned))
        out_v = refs[0] if last else table_v
        load_total = pltpu.make_async_copy(total_hbm, total_v, sems.at[0])
        load_table = pltpu.make_async_copy(table_hbm, table_v, sems.at[1])
        load_total.start()
        load_table.start()
        other_v[...] = jnp.zeros_like(other_v)
        for ref, long in zip(back_refs, rows):
            spread(ref, long)
        rel_total = pair_sum([ref[...] for ref in near_refs])
        rel_new = rel_state_ref[...] + rel_total * rel_total
        new_rel_state[...] = rel_new
        new_rel[...] = rel_ref[...] - rel_rate * rel_total / jnp.sqrt(rel_new)
        spare = jnp.zeros((LANES - groups, LANES), jnp.float32)
        state_t[...] = jnp.concatenate([state_ref[...], spare], axis=0).T
        mean_t[...] = jnp.zeros_like(mean_t)
        load_total.wait()
        totals = (other_v, total_v)
        scatter_live(
            live_ref,
            [(index_ref, first + i, long, totals[i % 2]) for i, long in enumerate(rows)],
            count,
        )
        load_table.wait()
        lane = lax.broadcasted_iota(jnp.int32, (LANES, LANES), 1)
        saves = []
        for step in range(steps):

            @pl.loop(step * step_rows // LANES, (step + 1) * step_rows // LANES)
            def _(group):
                base = pl.multiple_of(group * LANES, LANES)
                sides = [half(base, LANES, side) for side in range(2)]
                grads = [total_v[side, :] + other_v[side, :] for side in sides]
                square = grads[0] * grads[0] + grads[1] * grads[1]
                mean = jnp.sum(square, axis=1, keepdims=True) * (1.0 / width)
                mine = lane == group
                old = jnp.sum(jnp.where(mine, state_t[...], 0.0), axis=1, keepdims=True)
                mean_t[...] = jnp.where(mine, mean, mean_t[...])
                scale = learn_rate / jnp.sqrt(old + mean)
                values = [table_v[side, :] - grad * scale for side, grad in zip(sides, grads)]
                for number, value in enumerate(values):
                    if last:
                        out_v[pl.ds(base, LANES), number * LANES : (number + 1) * LANES] = value
                    else:
                        out_v[sides[number], :] = value

            tall = step_rows if last else 2 * step_rows
            part = pl.ds(step * tall, tall)
            save = pltpu.make_async_copy(out_v.at[part], out_hbm.at[part], sems.at[2 + step])
            save.start()
            saves.append(save)
        state_out[...] = (state_t[...] + mean_t[...]).T[:groups]
        for out, batch in zip(next_outs, next_batches):
            gather_rows(next_ref[0], batch, count, table_v, rows[0], out)
        for save in saves:
            save.wait()

    out_shape = (row_count, width) if last else table.shape
    rel_shape = jax.ShapeDtypeStruct(relations.shape, jnp.float32)
    return pl.pallas_call(
        body,
        out_shape=[
            jax.ShapeDtypeStruct(out_shape, jnp.float32),
            jax.ShapeDtypeStruct((groups, LANES), jnp.float32),
            rel_shape,
            rel_shape,
        ]
        + [jax.ShapeDtypeStruct((height, width), jnp.bfloat16)] * len(next_batches),
        in_specs=[SMEM] * len(indices)
        + [ANY]
        + [VMEM] * len(returned)
        + [HBM]
        + [VMEM] * (len(near) + 3),
        out_specs=[HBM] + [VMEM] * (3 + len(next_batches)),
        scratch_shapes=[
            pltpu.VMEM(table.shape, jnp.float32),
            pltpu.VMEM(table.shape, jnp.float32),
            pltpu.VMEM(table.shape, jnp.float32),
            pltpu.VMEM((LANES, LANES), jnp.float32),
            pltpu.VMEM((LANES, LANES), jnp.float32),
            pltpu.SemaphoreType.DMA((2 + steps,)),
        ]
        + [pltpu.VMEM((2 * height, LANES), jnp.float32)] * len(returned)
        + ([pltpu.VMEM((row_count, width), jnp.float32)] if last else []),
        compiler_params=params(44 if last else 48),
        cost_estimate=cost(50_000_000),
        name="finish_last" if last else "finish_next",
    )(*indices, total, *returned, table, state, *near, relations, rel_state)


def flip(index, bits):
    for place in range(8):
        step = 1 << place
        if bits & step:
            index = index + step * (1 - 2 * ((index // step) % 2))
    return index


def relation_kernel(stages, own, summed, *scratch):
    parts, received = (own,) + scratch[:-3], scratch[-3]
    send_sems, recv_sems = scratch[-2:]
    dom, rep = lax.axis_index("dom"), lax.axis_index("rep")

    def device(peer):
        return (flip(dom, peer[0]), flip(rep, peer[1]))

    barrier = pltpu.get_barrier_semaphore()
    peers = [peer for stage in stages for peer in stage]
    for peer in peers:
        pl.semaphore_signal(
            barrier, inc=1, device_id=device(peer), device_id_type=pl.DeviceIdType.MESH
        )
    pl.semaphore_wait(barrier, len(peers))
    slot = 0
    for number, stage in enumerate(stages):
        copies = []
        for peer in stage:
            copy = pltpu.make_async_remote_copy(
                src_ref=parts[number],
                dst_ref=received.at[slot],
                send_sem=send_sems.at[slot],
                recv_sem=recv_sems.at[slot],
                device_id=device(peer),
                device_id_type=pl.DeviceIdType.MESH,
            )
            copy.start()
            copies.append(copy)
            slot += 1
        for copy in copies:
            copy.wait()
        first = slot - len(stage)
        total = pair_sum([parts[number][...]] + [received[first + i] for i in range(len(stage))])
        if number + 1 < len(stages):
            parts[number + 1][...] = total
    summed[...] = total


def pair_sum(values):
    while len(values) > 1:
        values = [values[i] + values[i + 1] for i in range(0, len(values), 2)]
    return values[0]


def relation_sum(rel_grad):
    stages = [
        [(0, 1), (0, 2), (0, 3)],
        [(1, 0), (2, 0), (3, 0)],
        [(4, 0)],
    ]
    slots = sum(len(stage) for stage in stages)
    shape = rel_grad.shape
    return pl.pallas_call(
        functools.partial(relation_kernel, stages),
        out_shape=jax.ShapeDtypeStruct(shape, jnp.float32),
        in_specs=[VMEM],
        out_specs=VMEM,
        scratch_shapes=[pltpu.VMEM(shape, jnp.float32)] * (len(stages) - 1)
        + [
            pltpu.VMEM((slots,) + shape, jnp.float32),
            pltpu.SemaphoreType.DMA((slots,)),
            pltpu.SemaphoreType.DMA((slots,)),
        ],
        compiler_params=pltpu.CompilerParams(
            collective_id=0, has_side_effects=True, vmem_limit_bytes=4 * MIB
        ),
        cost_estimate=cost(20_000_000),
        name="relation_sum",
    )(rel_grad)


def from_partner(shard, axis, distance):
    return from_peer(shard, axis, 1 << distance)


def from_peer(shard, axis, bits):
    return lax.ppermute(shard, axis, [(i, i ^ bits) for i in range(lax.axis_size(axis))])


def on_device(
    embeddings, row_state, relations, rel_state, edge_src, edge_dst, edge_rel, batch_count
):
    bit_count = lax.axis_size("dom").bit_length() - 1
    row_count, width = embeddings.shape
    batches, count = edge_src.shape[-2:]
    padded = round_up(count, BLOCK)
    state = row_state.reshape(row_count // LANES, LANES)
    spots = [bit_count - 1 - number for number in range(ROUNDS)]
    firsts = (0, 1)
    others = tuple(range(len(firsts), batches))
    table, *told = pack_first(
        edge_src[0, 0, 0], embeddings, edge_dst[0, 0], edge_rel[0, 0], batch_count[0, 0], firsts
    )
    told, sent = told[:ROUNDS], told[ROUNDS:]
    for number in range(ROUNDS):
        last = number + 1 == ROUNDS
        swap_bit = spots[number]
        source_index = edge_src[0, 0, number]
        live = batch_count[0, 0, number].reshape(1)
        note = from_partner(told[number], "dom", swap_bit)
        arrived = []
        for rows in sent:
            arrived.append(from_partner(rows, "dom", swap_bit))
        more = pack(source_index, table, others, count, width)
        for batch, rows in zip(others, more):
            arrived.append(from_partner(rows, "dom", swap_bit))
        other_index = note[:batches]
        other_live = note[2 * batches, :1]
        kinds = jnp.pad(
            note[batches : 2 * batches], ((0, 0), (0, padded - count)), constant_values=-1
        )
        targets = pack(other_index, table, tuple(range(batches)), count, width)
        rel_grad = jnp.zeros(relations.shape, jnp.float32)
        own, returned = [], []
        for batch in range(batches):
            grad_source, grad_target, rel_grad = run_batch(
                batch,
                count,
                other_live,
                kinds[batch][None],
                arrived[batch],
                targets[batch],
                relations,
                rel_grad,
            )
            own.append(grad_target)
            returned.append(from_partner(grad_source, "dom", swap_bit))
        near = [relation_sum(rel_grad)]
        for bits in (8, 16, 24):
            near.append(from_peer(near[0], "dom", bits))
        early = batches - 2
        total = first_total(
            count, row_count, other_live, live, other_index, source_index, own, returned[:early]
        )
        table, state, relations, rel_state, *sent = finish(
            count,
            live,
            source_index,
            total,
            returned[early:],
            early,
            table,
            state,
            width,
            near,
            relations,
            rel_state,
            None if last else edge_src[0, 0, number + 1],
            () if last else firsts,
        )
    return (table, state.reshape(row_count), relations, rel_state)


def solution(mesh):
    return sharded(mesh)


def sharded(mesh):
    return jax.shard_map(
        on_device,
        mesh=mesh,
        in_specs=(
            P(("dom", "rep"), None),
            P(("dom", "rep")),
            P(),
            P(),
            P("dom", "rep", None, None, None),
            P("dom", "rep", None, None, None),
            P("dom", "rep", None, None, None),
            P("dom", "rep", None),
        ),
        out_specs=(P(("dom", "rep"), None), P(("dom", "rep")), P(), P()),
        check_vma=False,
    )
```

```python
import functools

import jax
import jax.numpy as jnp
from jax import lax
from jax.experimental import pallas as pl
from jax.experimental.pallas import tpu as pltpu
from jax.sharding import PartitionSpec as P


ROUNDS = 2

learn_rate = 0.1
rel_rate = 0.1


SMEM = pl.BlockSpec(memory_space=pltpu.SMEM)
VMEM = pl.BlockSpec(memory_space=pltpu.VMEM)
ANY = pl.BlockSpec(memory_space=pl.ANY)
HBM = pl.BlockSpec(memory_space=pltpu.HBM)
GATHER_UNROLL = 20
SCATTER_UNROLL = 8
BLOCK = 256
LANES = 128
MIB = 1024 * 1024


def params(mib, **kw):
    return pltpu.CompilerParams(vmem_limit_bytes=mib * MIB, **kw)


def cost(nbytes):
    return pl.CostEstimate(flops=0, bytes_accessed=nbytes, transcendentals=0)


def round_up(n, m):
    return (n + m - 1) // m * m


def piece(row):
    return pl.ds(pl.multiple_of(row * 2, 2), 2)


def half(start, count, side):
    return pl.ds(start * 2 + side, count, stride=2)


def gather_rows(index_ref, batches, count, table, rows, out):
    height = rows.shape[0] // 2
    if height > count:
        rows[2 * count :, :] = jnp.zeros((2 * (height - count), LANES), rows.dtype)
    for place, batch in enumerate(batches):

        @pl.loop(0, count // GATHER_UNROLL)
        def _(step):
            base = step * GATHER_UNROLL
            for j in range(GATHER_UNROLL):
                rows[piece(base + j), :] = table[piece(index_ref[batch * count + base + j]), :]

        for side in range(2):
            out[place * height : (place + 1) * height, side * LANES : (side + 1) * LANES] = rows[
                half(0, height, side), :
            ].astype(out.dtype)


def scatter_rows(jobs, count):
    @pl.loop(0, count // SCATTER_UNROLL)
    def _(step):
        base = step * SCATTER_UNROLL
        for j in range(SCATTER_UNROLL):
            spots = [piece(job[0][job[1] * count + base + j]) for job in jobs]
            olds = [job[4][spot, :] for spot, job in zip(spots, jobs)]
            for spot, old, (_, _, rows, start, total) in zip(spots, olds, jobs):
                total[spot, :] = old + rows[piece(start + base + j), :]


def scatter_live(live_ref, jobs, count):
    for first in range(0, len(jobs), 2):
        pair = jobs[first : first + 2]
        if len(pair) == 2:

            @pl.when(pair[1][1] < live_ref[0])
            def _():
                scatter_rows(pair, count)

        @pl.when((pair[0][1] < live_ref[0]) & (pair[-1][1] >= live_ref[0]))
        def _():
            scatter_rows(pair[:1], count)


def jobs_of(index, first, group_rows, totals, groups):
    jobs = []
    for group, rows in zip(groups[first:], group_rows):
        height = rows.shape[0] // (2 * len(group))
        for place, batch in enumerate(group):
            jobs.append((index, batch, rows, place * height, totals[batch % 2]))
    return jobs


def spread(ref, rows):
    for side in range(2):
        rows[half(0, ref.shape[0], side), :] = ref[:, side * LANES : (side + 1) * LANES].astype(
            jnp.float32
        )


def pack_first(index, table, edge_dst, edge_rel, batch_count, batches):
    rounds, slots, count = edge_dst.shape
    height = round_up(count, 16)
    row_count, width = table.shape
    parts = 8
    part_rows = row_count // parts

    def body(index_ref, count_ref, table_hbm, dst_ref, rel_ref, long_hbm, *refs):
        notes, refs = refs[:rounds], refs[rounds:]
        out, table_v, long_v, rows, sems = refs
        loads = []
        for part in range(parts):
            here = pl.ds(part * part_rows, part_rows)
            load = pltpu.make_async_copy(table_hbm.at[here], table_v.at[here], sems.at[part])
            load.start()
            loads.append(load)
        for number, note in enumerate(notes):
            note[:slots] = dst_ref[number]
            note[slots : 2 * slots] = rel_ref[number]
            note[2 * slots :] = jnp.full((1, count), count_ref[number], jnp.int32)
        for part in range(parts):
            loads[part].wait()

            @pl.loop(part * part_rows // LANES, (part + 1) * part_rows // LANES)
            def _(step):
                here = pl.multiple_of(step * LANES, LANES)
                for side in range(2):
                    long_v[half(here, LANES, side), :] = table_v[
                        pl.ds(here, LANES), side * LANES : (side + 1) * LANES
                    ]

        save = pltpu.make_async_copy(long_v, long_hbm, sems.at[parts])
        save.start()
        gather_rows(index_ref, batches, count, long_v, rows, out)
        save.wait()

    return pl.pallas_call(
        body,
        out_shape=[jax.ShapeDtypeStruct((2 * row_count, LANES), jnp.float32)]
        + [jax.ShapeDtypeStruct((2 * slots + 1, count), jnp.int32)] * rounds
        + [jax.ShapeDtypeStruct((len(batches) * height, width), jnp.bfloat16)],
        in_specs=[SMEM, SMEM, HBM, VMEM, VMEM],
        out_specs=[HBM] + [VMEM] * (rounds + 1),
        scratch_shapes=[
            pltpu.VMEM((row_count, width), jnp.float32),
            pltpu.VMEM((2 * row_count, LANES), jnp.float32),
            pltpu.VMEM((2 * height, LANES), jnp.float32),
            pltpu.SemaphoreType.DMA((parts + 1,)),
        ],
        compiler_params=params(56),
        cost_estimate=cost(25_000_000),
        name="pack_first",
    )(index, batch_count, table, edge_dst, edge_rel)


def pack(index, table, groups, count, width, grant):
    height = round_up(count, 16)

    def body(index_ref, table_hbm, *refs):
        outs, (table_v, rows, sem) = refs[:-3], refs[-3:]
        load = pltpu.make_async_copy(table_hbm, table_v, sem)
        load.start()
        load.wait()
        for out, group in zip(outs, groups):
            gather_rows(index_ref, group, count, table_v, rows, out)

    return pl.pallas_call(
        body,
        out_shape=[
            jax.ShapeDtypeStruct((len(group) * height, width), jnp.bfloat16) for group in groups
        ],
        in_specs=[SMEM, HBM],
        out_specs=[VMEM] * len(groups),
        scratch_shapes=[
            pltpu.VMEM(table.shape, jnp.float32),
            pltpu.VMEM((2 * height, LANES), jnp.float32),
            pltpu.SemaphoreType.DMA,
        ],
        compiler_params=params(grant),
        cost_estimate=cost(30_000_000),
    )(index, table)


def batch_kernel(group, count, live_ref, kind_ref, source_ref, target_ref, rel_ref, rel_in,
                 grad_source, grad_target, rel_out, query_t, total_t, product):
    height, width = source_ref.shape[0] // len(group), source_ref.shape[1]
    full = round_up(height, BLOCK)
    kinds = rel_ref.shape[0]
    neg_share = 0.5 / (count - 1)
    rel_out[...] = rel_in[...]

    @pl.loop(0, jnp.clip(live_ref[0] - group[0], 0, len(group)))
    def _(place):
        start = pl.multiple_of(place * height, 16)
        rel = rel_ref[...]
        high = rel.astype(jnp.bfloat16)
        rest = rel - high.astype(jnp.float32)
        mid = rest.astype(jnp.bfloat16)
        low = (rest - mid.astype(jnp.float32)).astype(jnp.bfloat16)
        parts = jnp.concatenate([high, mid, low], axis=0)
        kind = jnp.broadcast_to(kind_ref[pl.ds(place, 1), :], (3 * kinds, full))
        row = lax.broadcasted_iota(jnp.int32, (3 * kinds, full), 0)
        hot = jnp.where((row % kinds) == kind, 1.0, 0.0).astype(jnp.bfloat16)
        diagonal = lax.dot_general(
            hot, parts, (((0,), (0,)), ((), ())), preferred_element_type=jnp.float32
        )
        source = source_ref[pl.ds(start, height), :].astype(jnp.float32)
        target = target_ref[pl.ds(start, height), :]
        if full > height:
            gap = jnp.zeros((full - height, width), jnp.float32)
            source = jnp.concatenate([source, gap], axis=0)
            target = jnp.concatenate([target, gap.astype(target.dtype)], axis=0)
        query_full = (source * diagonal).astype(jnp.bfloat16).astype(jnp.float32)
        query_t[...] = query_full.T.astype(jnp.bfloat16)
        half_query = (query_full * 0.5).astype(jnp.bfloat16)
        eye = lax.broadcasted_iota(jnp.int32, (BLOCK, BLOCK), 0) == lax.broadcasted_iota(
            jnp.int32, (BLOCK, BLOCK), 1
        )
        for block in range(full // BLOCK):
            here = slice(block * BLOCK, (block + 1) * BLOCK)
            pieces = []
            for col in range(full // BLOCK):
                there = slice(col * BLOCK, (col + 1) * BLOCK)
                slope = jnp.tanh(
                    lax.dot_general(
                        half_query[here],
                        target[there],
                        (((1,), (1,)), ((), ())),
                        preferred_element_type=jnp.float32,
                    )
                )
                weight = slope * neg_share + neg_share
                if col == block:
                    weight = jnp.where(eye, slope * 0.5 - 0.5, weight)
                pieces.append(weight.astype(jnp.bfloat16))
            weights = jnp.concatenate(pieces, axis=1)
            grad_query = jnp.dot(weights, target, preferred_element_type=jnp.float32)
            tall = min(height - block * BLOCK, BLOCK)
            grad_rows = (grad_query * diagonal[here])[:tall]
            spot = pl.multiple_of(start + block * BLOCK, 16)
            grad_source[pl.ds(spot, tall), :] = grad_rows.astype(grad_source.dtype)
            product[here, :] = grad_query * source[here]
            part = jnp.dot(query_t[:, here], weights, preferred_element_type=jnp.float32)
            if block == 0:
                total_t[...] = part
            else:
                total_t[...] += part
        grad_rows = total_t[...].T[:height]
        for side in range(2):
            grad_target[half(start, height, side), :] = grad_rows[:, side * LANES : (side + 1) * LANES]
        value = product[...]
        upper = value.astype(jnp.bfloat16)
        lower = (value - upper.astype(jnp.float32)).astype(jnp.bfloat16)
        one = hot[:kinds]
        rel_out[...] = (
            rel_out[...]
            + jnp.dot(one, upper, preferred_element_type=jnp.float32)
            + jnp.dot(one, lower, preferred_element_type=jnp.float32)
        )


def run_group(group, count, live, kind, source, target, relations, rel_grad):
    height, width = source.shape
    full = round_up(height // len(group), BLOCK)
    return pl.pallas_call(
        functools.partial(batch_kernel, group, count),
        out_shape=[
            jax.ShapeDtypeStruct((height, width), jnp.bfloat16),
            jax.ShapeDtypeStruct((2 * height, LANES), jnp.float32),
            jax.ShapeDtypeStruct(rel_grad.shape, jnp.float32),
        ],
        in_specs=[SMEM] + [VMEM] * 5,
        out_specs=[VMEM] * 3,
        scratch_shapes=[
            pltpu.VMEM((width, full), jnp.bfloat16),
            pltpu.VMEM((width, full), jnp.float32),
            pltpu.VMEM((full, width), jnp.float32),
        ],
        compiler_params=params(24),
        cost_estimate=cost(15_000_000),
        name="batch_terms",
    )(live, kind, source, target, relations, rel_grad)


def first_total(count, groups, row_count, live, other_live, source_index, other_index, own, returned):
    def body(live_ref, other_ref, source_ref, index_ref, *refs):
        own_refs = refs[: len(own)]
        back_refs = refs[len(own) : len(own) + len(returned)]
        total, other = refs[len(own) + len(returned) :][:2]
        rows = refs[len(own) + len(returned) + 2 :]
        totals = (total, other)
        total[...] = jnp.zeros_like(total)
        other[...] = jnp.zeros_like(other)
        for ref, long in zip(back_refs, rows):
            spread(ref, long)
        scatter_live(
            live_ref,
            jobs_of(source_ref, 0, own_refs, totals, groups),
            count,
        )
        scatter_live(
            other_ref,
            jobs_of(index_ref, 0, rows, totals, groups),
            count,
        )
        total[...] += other[...]

    return pl.pallas_call(
        body,
        out_shape=jax.ShapeDtypeStruct((2 * row_count, LANES), jnp.float32),
        in_specs=[SMEM] * 4 + [VMEM] * (len(own) + len(returned)),
        out_specs=VMEM,
        scratch_shapes=[pltpu.VMEM((2 * row_count, LANES), jnp.float32)]
        + [pltpu.VMEM(own[0].shape, jnp.float32)] * len(returned),
        compiler_params=params(50),
        cost_estimate=cost(60_000_000),
        name="first_total",
    )(live, other_live, source_index, other_index, *own, *returned)


def finish(
    count, groups, live, source_index, total, returned, first, table, state, width, near, relations, rel_state, next_index, next_batches
):
    row_count = table.shape[0] // 2
    height = returned[0].shape[0]
    tiles = row_count // LANES
    step_rows = 1024
    steps = row_count // step_rows
    last = next_index is None
    indices = [live, source_index] + ([] if last else [next_index])

    def body(*refs):
        refs = list(refs)

        def take(number):
            taken = refs[:number]
            del refs[:number]
            return taken

        live_ref, index_ref, *next_ref = take(len(indices))
        (total_hbm,) = take(1)
        back_refs = take(len(returned))
        table_hbm, state_ref = take(2)
        near_refs = take(len(near))
        rel_ref, rel_state_ref, out_hbm, state_out, new_rel, new_rel_state = take(6)
        next_outs = take(0 if last else 1)
        total_v, other_v, table_v, state_t, mean_t, sems = take(6)
        rows = take(len(returned))
        out_v = refs[0] if last else table_v
        load_total = pltpu.make_async_copy(total_hbm, total_v, sems.at[0])
        load_table = pltpu.make_async_copy(table_hbm, table_v, sems.at[1])
        load_total.start()
        load_table.start()
        other_v[...] = jnp.zeros_like(other_v)
        for ref, long in zip(back_refs, rows):
            spread(ref, long)
        rel_total = pair_sum([ref[...] for ref in near_refs])
        rel_new = rel_state_ref[...] + rel_total * rel_total
        new_rel_state[...] = rel_new
        new_rel[...] = rel_ref[...] - rel_rate * rel_total / jnp.sqrt(rel_new)
        spare = jnp.zeros((LANES - tiles, LANES), jnp.float32)
        state_t[...] = jnp.concatenate([state_ref[...], spare], axis=0).T
        mean_t[...] = jnp.zeros_like(mean_t)
        load_total.wait()
        totals = (other_v, total_v)
        scatter_live(
            live_ref,
            jobs_of(index_ref, first, rows, totals, groups),
            count,
        )
        load_table.wait()
        lane = lax.broadcasted_iota(jnp.int32, (LANES, LANES), 1)
        saves = []
        for step in range(steps):

            @pl.loop(step * step_rows // LANES, (step + 1) * step_rows // LANES)
            def _(group):
                base = pl.multiple_of(group * LANES, LANES)
                sides = [half(base, LANES, side) for side in range(2)]
                grads = [total_v[side, :] + other_v[side, :] for side in sides]
                square = grads[0] * grads[0] + grads[1] * grads[1]
                mean = jnp.sum(square, axis=1, keepdims=True) * (1.0 / width)
                mine = lane == group
                old = jnp.sum(jnp.where(mine, state_t[...], 0.0), axis=1, keepdims=True)
                mean_t[...] = jnp.where(mine, mean, mean_t[...])
                scale = learn_rate / jnp.sqrt(old + mean)
                values = [table_v[side, :] - grad * scale for side, grad in zip(sides, grads)]
                for number, value in enumerate(values):
                    if last:
                        out_v[pl.ds(base, LANES), number * LANES : (number + 1) * LANES] = value
                    else:
                        out_v[sides[number], :] = value

            tall = step_rows if last else 2 * step_rows
            part = pl.ds(step * tall, tall)
            save = pltpu.make_async_copy(out_v.at[part], out_hbm.at[part], sems.at[2 + step])
            save.start()
            saves.append(save)
        state_out[...] = (state_t[...] + mean_t[...]).T[:tiles]
        for out in next_outs:
            gather_rows(
                next_ref[0], next_batches, count, table_v, rows[0].at[: 2 * round_up(count, 16)], out
            )
        for save in saves:
            save.wait()

    out_shape = (row_count, width) if last else table.shape
    rel_shape = jax.ShapeDtypeStruct(relations.shape, jnp.float32)
    return pl.pallas_call(
        body,
        out_shape=[
            jax.ShapeDtypeStruct(out_shape, jnp.float32),
            jax.ShapeDtypeStruct((tiles, LANES), jnp.float32),
            rel_shape,
            rel_shape,
        ]
        + [jax.ShapeDtypeStruct((len(next_batches) * round_up(count, 16), width), jnp.bfloat16)]
        * (not last),
        in_specs=[SMEM] * len(indices)
        + [ANY]
        + [VMEM] * len(returned)
        + [HBM]
        + [VMEM] * (len(near) + 3),
        out_specs=[HBM] + [VMEM] * (3 + (not last)),
        scratch_shapes=[
            pltpu.VMEM(table.shape, jnp.float32),
            pltpu.VMEM(table.shape, jnp.float32),
            pltpu.VMEM(table.shape, jnp.float32),
            pltpu.VMEM((LANES, LANES), jnp.float32),
            pltpu.VMEM((LANES, LANES), jnp.float32),
            pltpu.SemaphoreType.DMA((2 + steps,)),
        ]
        + [pltpu.VMEM((2 * height, LANES), jnp.float32)] * len(returned)
        + ([pltpu.VMEM((row_count, width), jnp.float32)] if last else []),
        compiler_params=params(50),
        cost_estimate=cost(50_000_000),
        name="finish_last" if last else "finish_next",
    )(*indices, total, *returned, table, state, *near, relations, rel_state)


def flip(index, bits):
    for place in range(8):
        step = 1 << place
        if bits & step:
            index = index + step * (1 - 2 * ((index // step) % 2))
    return index


def relation_kernel(stages, own, summed, *scratch):
    parts, received = (own,) + scratch[:-3], scratch[-3]
    send_sems, recv_sems = scratch[-2:]
    dom, rep = lax.axis_index("dom"), lax.axis_index("rep")

    def device(peer):
        return (flip(dom, peer[0]), flip(rep, peer[1]))

    barrier = pltpu.get_barrier_semaphore()
    peers = [peer for stage in stages for peer in stage]
    for peer in peers:
        pl.semaphore_signal(
            barrier, inc=1, device_id=device(peer), device_id_type=pl.DeviceIdType.MESH
        )
    pl.semaphore_wait(barrier, len(peers))
    slot = 0
    for number, stage in enumerate(stages):
        copies = []
        for peer in stage:
            copy = pltpu.make_async_remote_copy(
                src_ref=parts[number],
                dst_ref=received.at[slot],
                send_sem=send_sems.at[slot],
                recv_sem=recv_sems.at[slot],
                device_id=device(peer),
                device_id_type=pl.DeviceIdType.MESH,
            )
            copy.start()
            copies.append(copy)
            slot += 1
        for copy in copies:
            copy.wait()
        first = slot - len(stage)
        total = pair_sum([parts[number][...]] + [received[first + i] for i in range(len(stage))])
        if number + 1 < len(stages):
            parts[number + 1][...] = total
    summed[...] = total


def pair_sum(values):
    while len(values) > 1:
        values = [values[i] + values[i + 1] for i in range(0, len(values), 2)]
    return values[0]


def relation_sum(rel_grad):
    stages = [
        [(0, 1), (0, 2), (0, 3)],
        [(1, 0), (2, 0), (3, 0)],
        [(4, 0)],
    ]
    slots = sum(len(stage) for stage in stages)
    shape = rel_grad.shape
    return pl.pallas_call(
        functools.partial(relation_kernel, stages),
        out_shape=jax.ShapeDtypeStruct(shape, jnp.float32),
        in_specs=[VMEM],
        out_specs=VMEM,
        scratch_shapes=[pltpu.VMEM(shape, jnp.float32)] * (len(stages) - 1)
        + [
            pltpu.VMEM((slots,) + shape, jnp.float32),
            pltpu.SemaphoreType.DMA((slots,)),
            pltpu.SemaphoreType.DMA((slots,)),
        ],
        compiler_params=pltpu.CompilerParams(
            collective_id=0, has_side_effects=True, vmem_limit_bytes=4 * MIB
        ),
        cost_estimate=cost(20_000_000),
        name="relation_sum",
    )(rel_grad)


def from_partner(shard, axis, distance):
    return from_peer(shard, axis, 1 << distance)


def from_peer(shard, axis, bits):
    return lax.ppermute(shard, axis, [(i, i ^ bits) for i in range(lax.axis_size(axis))])


def on_device(
    embeddings, row_state, relations, rel_state, edge_src, edge_dst, edge_rel, batch_count
):
    bit_count = lax.axis_size("dom").bit_length() - 1
    row_count, width = embeddings.shape
    batches, count = edge_src.shape[-2:]
    padded = round_up(count, BLOCK)
    state = row_state.reshape(row_count // LANES, LANES)
    spots = [bit_count - 1 - number for number in range(ROUNDS)]
    groups = tuple(
        tuple(range(first, min(first + 2, batches))) for first in range(0, batches, 2)
    )
    sources = [edge_src[0, 0, number].reshape(-1) for number in range(ROUNDS)]
    table, *told = pack_first(
        sources[0], embeddings, edge_dst[0, 0], edge_rel[0, 0], batch_count[0, 0], groups[0]
    )
    told, sent = told[:ROUNDS], told[ROUNDS:]
    for number in range(ROUNDS):
        last = number + 1 == ROUNDS
        swap_bit = spots[number]
        source_index = sources[number]
        live = batch_count[0, 0, number].reshape(1)
        note = from_partner(told[number], "dom", swap_bit)
        arrived = [from_partner(sent[0], "dom", swap_bit)]
        more = pack(source_index, table, groups[1:], count, width, 54)
        for rows in more:
            arrived.append(from_partner(rows, "dom", swap_bit))
        other_index = note[:batches].reshape(-1)
        other_live = note[2 * batches, :1]
        kinds = jnp.pad(
            note[batches : 2 * batches], ((0, 0), (0, padded - count)), constant_values=-1
        )
        targets = pack(other_index, table, groups, count, width, 50)
        rel_grad = jnp.zeros(relations.shape, jnp.float32)
        own, returned = [], []
        for place, group in enumerate(groups):
            grad_source, grad_target, rel_grad = run_group(
                group,
                count,
                other_live,
                kinds[group[0] : group[-1] + 1],
                arrived[place],
                targets[place],
                relations,
                rel_grad,
            )
            own.append(grad_target)
            returned.append(from_partner(grad_source, "dom", swap_bit))
        near = [relation_sum(rel_grad)]
        for bits in (8, 16, 24):
            near.append(from_peer(near[0], "dom", bits))
        early = len(groups) - 1
        total = first_total(
            count, groups, row_count, other_live, live, other_index, source_index, own, returned[:early]
        )
        table, state, relations, rel_state, *sent = finish(
            count,
            groups,
            live,
            source_index,
            total,
            returned[early:],
            early,
            table,
            state,
            width,
            near,
            relations,
            rel_state,
            None if last else sources[number + 1],
            () if last else groups[0],
        )
    return (table, state.reshape(row_count), relations, rel_state)


def solution(mesh):
    return sharded(mesh)


def sharded(mesh):
    return jax.shard_map(
        on_device,
        mesh=mesh,
        in_specs=(
            P(("dom", "rep"), None),
            P(("dom", "rep")),
            P(),
            P(),
            P("dom", "rep", None, None, None),
            P("dom", "rep", None, None, None),
            P("dom", "rep", None, None, None),
            P("dom", "rep", None),
        ),
        out_specs=(P(("dom", "rep"), None), P(("dom", "rep")), P(), P()),
        check_vma=False,
    )
```

```python
import functools

import jax
import jax.numpy as jnp
from jax import lax
from jax.experimental import pallas as pl
from jax.experimental.pallas import tpu as pltpu
from jax.sharding import PartitionSpec as P


ROUNDS = 2

learn_rate = 0.1
rel_rate = 0.1


SMEM = pl.BlockSpec(memory_space=pltpu.SMEM)
VMEM = pl.BlockSpec(memory_space=pltpu.VMEM)
ANY = pl.BlockSpec(memory_space=pl.ANY)
HBM = pl.BlockSpec(memory_space=pltpu.HBM)
GATHER_UNROLL = 20
SCATTER_UNROLL = 8
BLOCK = 256
LANES = 128
MIB = 1024 * 1024


def params(mib, **kw):
    return pltpu.CompilerParams(vmem_limit_bytes=mib * MIB, **kw)


def cost(nbytes):
    return pl.CostEstimate(flops=0, bytes_accessed=nbytes, transcendentals=0)


def round_up(n, m):
    return (n + m - 1) // m * m


def piece(row):
    return pl.ds(pl.multiple_of(row * 2, 2), 2)


def half(start, count, side):
    return pl.ds(start * 2 + side, count, stride=2)


def gather_rows(index_ref, batches, count, table, rows, out):
    height = rows.shape[0] // 2
    if height > count:
        rows[2 * count :, :] = jnp.zeros((2 * (height - count), LANES), rows.dtype)
    for place, batch in enumerate(batches):

        @pl.loop(0, count // GATHER_UNROLL)
        def _(step):
            base = step * GATHER_UNROLL
            for j in range(GATHER_UNROLL):
                rows[piece(base + j), :] = table[piece(index_ref[batch * count + base + j]), :]

        for side in range(2):
            out[place * height : (place + 1) * height, side * LANES : (side + 1) * LANES] = rows[
                half(0, height, side), :
            ].astype(out.dtype)


def scatter_rows(jobs, count):
    @pl.loop(0, count // SCATTER_UNROLL)
    def _(step):
        base = step * SCATTER_UNROLL
        for j in range(SCATTER_UNROLL):
            spots = [piece(job[0][job[1] * count + base + j]) for job in jobs]
            olds = [job[4][spot, :] for spot, job in zip(spots, jobs)]
            for spot, old, (_, _, rows, start, total) in zip(spots, olds, jobs):
                total[spot, :] = old + rows[piece(start + base + j), :]


def scatter_live(live_ref, jobs, count):
    for first in range(0, len(jobs), 2):
        pair = jobs[first : first + 2]
        if len(pair) == 2:

            @pl.when(pair[1][1] < live_ref[0])
            def _():
                scatter_rows(pair, count)

        @pl.when((pair[0][1] < live_ref[0]) & (pair[-1][1] >= live_ref[0]))
        def _():
            scatter_rows(pair[:1], count)


def jobs_of(index, first, group_rows, totals, groups):
    jobs = []
    for group, rows in zip(groups[first:], group_rows):
        height = rows.shape[0] // (2 * len(group))
        for place, batch in enumerate(group):
            jobs.append((index, batch, rows, place * height, totals[batch % 2]))
    return jobs


def spread(ref, rows):
    for side in range(2):
        rows[half(0, ref.shape[0], side), :] = ref[:, side * LANES : (side + 1) * LANES].astype(
            jnp.float32
        )


def pack_first(index, table, edge_dst, edge_rel, batch_count, batches):
    rounds, slots, count = edge_dst.shape
    height = round_up(count, 16)
    row_count, width = table.shape
    parts = 8
    part_rows = row_count // parts

    def body(index_ref, count_ref, table_hbm, dst_ref, rel_ref, long_hbm, *refs):
        notes, refs = refs[:rounds], refs[rounds:]
        out, table_v, long_v, rows, sems = refs
        loads = []
        for part in range(parts):
            here = pl.ds(part * part_rows, part_rows)
            load = pltpu.make_async_copy(table_hbm.at[here], table_v.at[here], sems.at[part])
            load.start()
            loads.append(load)
        for number, note in enumerate(notes):
            note[:slots] = dst_ref[number]
            note[slots : 2 * slots] = rel_ref[number]
            note[2 * slots :] = jnp.full((1, count), count_ref[number], jnp.int32)
        for part in range(parts):
            loads[part].wait()

            @pl.loop(part * part_rows // LANES, (part + 1) * part_rows // LANES)
            def _(step):
                here = pl.multiple_of(step * LANES, LANES)
                for side in range(2):
                    long_v[half(here, LANES, side), :] = table_v[
                        pl.ds(here, LANES), side * LANES : (side + 1) * LANES
                    ]

        save = pltpu.make_async_copy(long_v, long_hbm, sems.at[parts])
        save.start()
        gather_rows(index_ref, batches, count, long_v, rows, out)
        save.wait()

    return pl.pallas_call(
        body,
        out_shape=[jax.ShapeDtypeStruct((2 * row_count, LANES), jnp.float32)]
        + [jax.ShapeDtypeStruct((2 * slots + 1, count), jnp.int32)] * rounds
        + [jax.ShapeDtypeStruct((len(batches) * height, width), jnp.bfloat16)],
        in_specs=[SMEM, SMEM, HBM, VMEM, VMEM],
        out_specs=[HBM] + [VMEM] * (rounds + 1),
        scratch_shapes=[
            pltpu.VMEM((row_count, width), jnp.float32),
            pltpu.VMEM((2 * row_count, LANES), jnp.float32),
            pltpu.VMEM((2 * height, LANES), jnp.float32),
            pltpu.SemaphoreType.DMA((parts + 1,)),
        ],
        compiler_params=params(56),
        cost_estimate=cost(25_000_000),
        name="pack_first",
    )(index, batch_count, table, edge_dst, edge_rel)


def pack(index, table, groups, count, width, grant):
    height = round_up(count, 16)

    def body(index_ref, table_hbm, *refs):
        outs, (table_v, rows, sem) = refs[:-3], refs[-3:]
        load = pltpu.make_async_copy(table_hbm, table_v, sem)
        load.start()
        load.wait()
        for out, group in zip(outs, groups):
            gather_rows(index_ref, group, count, table_v, rows, out)

    return pl.pallas_call(
        body,
        out_shape=[
            jax.ShapeDtypeStruct((len(group) * height, width), jnp.bfloat16) for group in groups
        ],
        in_specs=[SMEM, HBM],
        out_specs=[VMEM] * len(groups),
        scratch_shapes=[
            pltpu.VMEM(table.shape, jnp.float32),
            pltpu.VMEM((2 * height, LANES), jnp.float32),
            pltpu.SemaphoreType.DMA,
        ],
        compiler_params=params(grant),
        cost_estimate=cost(30_000_000),
    )(index, table)


def batch_kernel(group, count, live_ref, kind_ref, source_ref, target_ref, rel_ref, rel_in,
                 grad_source, grad_target, rel_out, query_t, total_t, product):
    height, width = source_ref.shape[0] // len(group), source_ref.shape[1]
    full = round_up(height, BLOCK)
    kinds = rel_ref.shape[0]
    neg_share = 0.5 / (count - 1)
    rel_out[...] = rel_in[...]

    @pl.loop(0, jnp.clip(live_ref[0] - group[0], 0, len(group)))
    def _(place):
        start = pl.multiple_of(place * height, 16)
        rel = rel_ref[...]
        high = rel.astype(jnp.bfloat16)
        rest = rel - high.astype(jnp.float32)
        mid = rest.astype(jnp.bfloat16)
        low = (rest - mid.astype(jnp.float32)).astype(jnp.bfloat16)
        parts = jnp.concatenate([high, mid, low], axis=0)
        kind = jnp.broadcast_to(kind_ref[pl.ds(place, 1), :], (3 * kinds, full))
        row = lax.broadcasted_iota(jnp.int32, (3 * kinds, full), 0)
        hot = jnp.where((row % kinds) == kind, 1.0, 0.0).astype(jnp.bfloat16)
        diagonal = lax.dot_general(
            hot, parts, (((0,), (0,)), ((), ())), preferred_element_type=jnp.float32
        )
        source = source_ref[pl.ds(start, height), :].astype(jnp.float32)
        target = target_ref[pl.ds(start, height), :]
        if full > height:
            gap = jnp.zeros((full - height, width), jnp.float32)
            source = jnp.concatenate([source, gap], axis=0)
            target = jnp.concatenate([target, gap.astype(target.dtype)], axis=0)
        query_full = (source * diagonal).astype(jnp.bfloat16).astype(jnp.float32)
        query_t[...] = query_full.T.astype(jnp.bfloat16)
        half_query = (query_full * 0.5).astype(jnp.bfloat16)
        eye = lax.broadcasted_iota(jnp.int32, (BLOCK, BLOCK), 0) == lax.broadcasted_iota(
            jnp.int32, (BLOCK, BLOCK), 1
        )
        for block in range(full // BLOCK):
            here = slice(block * BLOCK, (block + 1) * BLOCK)
            pieces = []
            for col in range(full // BLOCK):
                there = slice(col * BLOCK, (col + 1) * BLOCK)
                slope = jnp.tanh(
                    lax.dot_general(
                        half_query[here],
                        target[there],
                        (((1,), (1,)), ((), ())),
                        preferred_element_type=jnp.float32,
                    )
                )
                weight = slope * neg_share + neg_share
                if col == block:
                    weight = jnp.where(eye, slope * 0.5 - 0.5, weight)
                pieces.append(weight.astype(jnp.bfloat16))
            weights = jnp.concatenate(pieces, axis=1)
            grad_query = jnp.dot(weights, target, preferred_element_type=jnp.float32)
            tall = min(height - block * BLOCK, BLOCK)
            grad_rows = (grad_query * diagonal[here])[:tall]
            spot = pl.multiple_of(start + block * BLOCK, 16)
            grad_source[pl.ds(spot, tall), :] = grad_rows.astype(grad_source.dtype)
            product[here, :] = grad_query * source[here]
            part = jnp.dot(query_t[:, here], weights, preferred_element_type=jnp.float32)
            if block == 0:
                total_t[...] = part
            else:
                total_t[...] += part
        grad_rows = total_t[...].T[:height]
        for side in range(2):
            grad_target[half(start, height, side), :] = grad_rows[:, side * LANES : (side + 1) * LANES]
        value = product[...]
        upper = value.astype(jnp.bfloat16)
        lower = (value - upper.astype(jnp.float32)).astype(jnp.bfloat16)
        one = hot[:kinds]
        rel_out[...] = (
            rel_out[...]
            + jnp.dot(one, upper, preferred_element_type=jnp.float32)
            + jnp.dot(one, lower, preferred_element_type=jnp.float32)
        )


def run_group(group, count, live, kind, source, target, relations, rel_grad):
    height, width = source.shape
    full = round_up(height // len(group), BLOCK)
    return pl.pallas_call(
        functools.partial(batch_kernel, group, count),
        out_shape=[
            jax.ShapeDtypeStruct((height, width), jnp.bfloat16),
            jax.ShapeDtypeStruct((2 * height, LANES), jnp.float32),
            jax.ShapeDtypeStruct(rel_grad.shape, jnp.float32),
        ],
        in_specs=[SMEM] + [VMEM] * 5,
        out_specs=[VMEM] * 3,
        scratch_shapes=[
            pltpu.VMEM((width, full), jnp.bfloat16),
            pltpu.VMEM((width, full), jnp.float32),
            pltpu.VMEM((full, width), jnp.float32),
        ],
        compiler_params=params(24),
        cost_estimate=cost(15_000_000),
        name="batch_terms",
    )(live, kind, source, target, relations, rel_grad)


def first_total(count, groups, row_count, live, other_live, source_index, other_index, own, returned):
    parts = 8
    part_rows = 2 * row_count // parts
    loads = len(own) + len(returned)

    def body(live_ref, other_ref, source_ref, index_ref, *refs):
        inputs, out_hbm = refs[:loads], refs[loads]
        buffers = refs[loads + 1 : 2 * loads + 1]
        rows = refs[2 * loads + 1 : -3]
        total, other, sems = refs[-3:]
        totals = (total, other)
        copies = [
            pltpu.make_async_copy(ref, buffer, sems.at[number])
            for number, (ref, buffer) in enumerate(zip(inputs, buffers))
        ]
        for copy in copies:
            copy.start()
        total[...] = jnp.zeros_like(total)
        other[...] = jnp.zeros_like(other)
        for copy in copies:
            copy.wait()
        for buffer, long in zip(buffers[len(own) :], rows):
            spread(buffer, long)
        scatter_live(
            live_ref,
            jobs_of(source_ref, 0, buffers[: len(own)], totals, groups),
            count,
        )
        scatter_live(
            other_ref,
            jobs_of(index_ref, 0, rows, totals, groups),
            count,
        )
        saves = []
        for part in range(parts):
            here = pl.ds(part * part_rows, part_rows)
            total[here, :] += other[here, :]
            save = pltpu.make_async_copy(total.at[here], out_hbm.at[here], sems.at[loads + part])
            save.start()
            saves.append(save)
        for save in saves:
            save.wait()

    return pl.pallas_call(
        body,
        out_shape=jax.ShapeDtypeStruct((2 * row_count, LANES), jnp.float32),
        in_specs=[SMEM] * 4 + [ANY] * loads,
        out_specs=ANY,
        scratch_shapes=[pltpu.VMEM(array.shape, array.dtype) for array in (*own, *returned)]
        + [pltpu.VMEM(own[0].shape, jnp.float32)] * len(returned)
        + [pltpu.VMEM((2 * row_count, LANES), jnp.float32)] * 2
        + [pltpu.SemaphoreType.DMA((loads + parts,))],
        compiler_params=params(50),
        cost_estimate=cost(60_000_000),
        name="first_total",
    )(live, other_live, source_index, other_index, *own, *returned)


def finish(
    count, groups, live, source_index, total, returned, first, table, state, width, near, relations, rel_state, next_index, next_batches
):
    row_count = table.shape[0] // 2
    height = returned[0].shape[0]
    tiles = row_count // LANES
    step_rows = 1024
    steps = row_count // step_rows
    last = next_index is None
    indices = [live, source_index] + ([] if last else [next_index])

    def body(*refs):
        refs = list(refs)

        def take(number):
            taken = refs[:number]
            del refs[:number]
            return taken

        live_ref, index_ref, *next_ref = take(len(indices))
        (total_hbm,) = take(1)
        back_refs = take(len(returned))
        table_hbm, state_ref = take(2)
        near_refs = take(len(near))
        rel_ref, rel_state_ref, out_hbm, state_out, new_rel, new_rel_state = take(6)
        next_outs = take(0 if last else 1)
        total_v, other_v, third_v, table_v, state_t, mean_t, sems = take(7)
        rows = take(len(returned))
        out_v = refs[0] if last else table_v
        load_total = pltpu.make_async_copy(total_hbm, total_v, sems.at[0])
        load_table = pltpu.make_async_copy(table_hbm, table_v, sems.at[1])
        load_total.start()
        load_table.start()
        other_v[...] = jnp.zeros_like(other_v)
        third_v[...] = jnp.zeros_like(third_v)
        for ref, long in zip(back_refs, rows):
            spread(ref, long)
        rel_total = pair_sum([ref[...] for ref in near_refs])
        rel_new = rel_state_ref[...] + rel_total * rel_total
        new_rel_state[...] = rel_new
        new_rel[...] = rel_ref[...] - rel_rate * rel_total / jnp.sqrt(rel_new)
        spare = jnp.zeros((LANES - tiles, LANES), jnp.float32)
        state_t[...] = jnp.concatenate([state_ref[...], spare], axis=0).T
        mean_t[...] = jnp.zeros_like(mean_t)
        totals = (other_v, third_v)
        scatter_live(
            live_ref,
            jobs_of(index_ref, first, rows, totals, groups),
            count,
        )
        load_total.wait()
        load_table.wait()
        lane = lax.broadcasted_iota(jnp.int32, (LANES, LANES), 1)
        saves = []
        for step in range(steps):

            @pl.loop(step * step_rows // LANES, (step + 1) * step_rows // LANES, unroll=4)
            def _(group):
                base = pl.multiple_of(group * LANES, LANES)
                sides = [half(base, LANES, side) for side in range(2)]
                grads = [total_v[side, :] + (other_v[side, :] + third_v[side, :]) for side in sides]
                square = grads[0] * grads[0] + grads[1] * grads[1]
                mean = jnp.sum(square, axis=1, keepdims=True) * (1.0 / width)
                mine = lane == group
                old = jnp.sum(jnp.where(mine, state_t[...], 0.0), axis=1, keepdims=True)
                mean_t[...] = jnp.where(mine, mean, mean_t[...])
                scale = learn_rate / jnp.sqrt(old + mean)
                values = [table_v[side, :] - grad * scale for side, grad in zip(sides, grads)]
                for number, value in enumerate(values):
                    if last:
                        out_v[pl.ds(base, LANES), number * LANES : (number + 1) * LANES] = value
                    else:
                        out_v[sides[number], :] = value

            tall = step_rows if last else 2 * step_rows
            part = pl.ds(step * tall, tall)
            save = pltpu.make_async_copy(out_v.at[part], out_hbm.at[part], sems.at[2 + step])
            save.start()
            saves.append(save)
        state_out[...] = (state_t[...] + mean_t[...]).T[:tiles]
        for out in next_outs:
            gather_rows(
                next_ref[0], next_batches, count, table_v, rows[0].at[: 2 * round_up(count, 16)], out
            )
        for save in saves:
            save.wait()

    out_shape = (row_count, width) if last else table.shape
    rel_shape = jax.ShapeDtypeStruct(relations.shape, jnp.float32)
    return pl.pallas_call(
        body,
        out_shape=[
            jax.ShapeDtypeStruct(out_shape, jnp.float32),
            jax.ShapeDtypeStruct((tiles, LANES), jnp.float32),
            rel_shape,
            rel_shape,
        ]
        + [jax.ShapeDtypeStruct((len(next_batches) * round_up(count, 16), width), jnp.bfloat16)]
        * (not last),
        in_specs=[SMEM] * len(indices)
        + [ANY]
        + [VMEM] * len(returned)
        + [HBM]
        + [VMEM] * (len(near) + 3),
        out_specs=[HBM] + [VMEM] * (3 + (not last)),
        scratch_shapes=[
            pltpu.VMEM(table.shape, jnp.float32),
            pltpu.VMEM(table.shape, jnp.float32),
            pltpu.VMEM(table.shape, jnp.float32),
            pltpu.VMEM(table.shape, jnp.float32),
            pltpu.VMEM((LANES, LANES), jnp.float32),
            pltpu.VMEM((LANES, LANES), jnp.float32),
            pltpu.SemaphoreType.DMA((2 + steps,)),
        ]
        + [pltpu.VMEM((2 * height, LANES), jnp.float32)] * len(returned)
        + ([pltpu.VMEM((row_count, width), jnp.float32)] if last else []),
        compiler_params=params(50),
        cost_estimate=cost(50_000_000),
        name="finish_last" if last else "finish_next",
    )(*indices, total, *returned, table, state, *near, relations, rel_state)


def flip(index, bits):
    for place in range(8):
        step = 1 << place
        if bits & step:
            index = index + step * (1 - 2 * ((index // step) % 2))
    return index


def relation_kernel(stages, own, summed, *scratch):
    parts, received = (own,) + scratch[:-3], scratch[-3]
    send_sems, recv_sems = scratch[-2:]
    dom, rep = lax.axis_index("dom"), lax.axis_index("rep")

    def device(peer):
        return (flip(dom, peer[0]), flip(rep, peer[1]))

    barrier = pltpu.get_barrier_semaphore()
    peers = [peer for stage in stages for peer in stage]
    for peer in peers:
        pl.semaphore_signal(
            barrier, inc=1, device_id=device(peer), device_id_type=pl.DeviceIdType.MESH
        )
    pl.semaphore_wait(barrier, len(peers))
    slot = 0
    for number, stage in enumerate(stages):
        copies = []
        for peer in stage:
            copy = pltpu.make_async_remote_copy(
                src_ref=parts[number],
                dst_ref=received.at[slot],
                send_sem=send_sems.at[slot],
                recv_sem=recv_sems.at[slot],
                device_id=device(peer),
                device_id_type=pl.DeviceIdType.MESH,
            )
            copy.start()
            copies.append(copy)
            slot += 1
        for copy in copies:
            copy.wait()
        first = slot - len(stage)
        total = pair_sum([parts[number][...]] + [received[first + i] for i in range(len(stage))])
        if number + 1 < len(stages):
            parts[number + 1][...] = total
    summed[...] = total


def pair_sum(values):
    while len(values) > 1:
        values = [values[i] + values[i + 1] for i in range(0, len(values), 2)]
    return values[0]


def relation_sum(rel_grad):
    stages = [
        [(0, 1), (0, 2), (0, 3)],
        [(1, 0), (2, 0), (3, 0)],
        [(4, 0)],
    ]
    slots = sum(len(stage) for stage in stages)
    shape = rel_grad.shape
    return pl.pallas_call(
        functools.partial(relation_kernel, stages),
        out_shape=jax.ShapeDtypeStruct(shape, jnp.float32),
        in_specs=[VMEM],
        out_specs=VMEM,
        scratch_shapes=[pltpu.VMEM(shape, jnp.float32)] * (len(stages) - 1)
        + [
            pltpu.VMEM((slots,) + shape, jnp.float32),
            pltpu.SemaphoreType.DMA((slots,)),
            pltpu.SemaphoreType.DMA((slots,)),
        ],
        compiler_params=pltpu.CompilerParams(
            collective_id=0, has_side_effects=True, vmem_limit_bytes=4 * MIB
        ),
        cost_estimate=cost(20_000_000),
        name="relation_sum",
    )(rel_grad)


def from_partner(shard, axis, distance):
    return from_peer(shard, axis, 1 << distance)


def from_peer(shard, axis, bits):
    return lax.ppermute(shard, axis, [(i, i ^ bits) for i in range(lax.axis_size(axis))])


def on_device(
    embeddings, row_state, relations, rel_state, edge_src, edge_dst, edge_rel, batch_count
):
    bit_count = lax.axis_size("dom").bit_length() - 1
    row_count, width = embeddings.shape
    batches, count = edge_src.shape[-2:]
    padded = round_up(count, BLOCK)
    state = row_state.reshape(row_count // LANES, LANES)
    spots = [bit_count - 1 - number for number in range(ROUNDS)]
    groups = tuple(
        tuple(range(first, min(first + 2, batches))) for first in range(0, batches, 2)
    )
    sources = [edge_src[0, 0, number].reshape(-1) for number in range(ROUNDS)]
    table, *told = pack_first(
        sources[0], embeddings, edge_dst[0, 0], edge_rel[0, 0], batch_count[0, 0], groups[0]
    )
    told, sent = told[:ROUNDS], told[ROUNDS:]
    for number in range(ROUNDS):
        last = number + 1 == ROUNDS
        swap_bit = spots[number]
        source_index = sources[number]
        live = batch_count[0, 0, number].reshape(1)
        note = from_partner(told[number], "dom", swap_bit)
        arrived = [from_partner(sent[0], "dom", swap_bit)]
        more = pack(source_index, table, groups[1:], count, width, 54)
        for rows in more:
            arrived.append(from_partner(rows, "dom", swap_bit))
        other_index = note[:batches].reshape(-1)
        other_live = note[2 * batches, :1]
        kinds = jnp.pad(
            note[batches : 2 * batches], ((0, 0), (0, padded - count)), constant_values=-1
        )
        targets = pack(other_index, table, groups, count, width, 50)
        rel_grad = jnp.zeros(relations.shape, jnp.float32)
        own, returned = [], []
        for place, group in enumerate(groups):
            grad_source, grad_target, rel_grad = run_group(
                group,
                count,
                other_live,
                kinds[group[0] : group[-1] + 1],
                arrived[place],
                targets[place],
                relations,
                rel_grad,
            )
            own.append(grad_target)
            returned.append(from_partner(grad_source, "dom", swap_bit))
        near = [relation_sum(rel_grad)]
        for bits in (8, 16, 24):
            near.append(from_peer(near[0], "dom", bits))
        early = len(groups) - 1
        total = first_total(
            count, groups, row_count, other_live, live, other_index, source_index, own, returned[:early]
        )
        table, state, relations, rel_state, *sent = finish(
            count,
            groups,
            live,
            source_index,
            total,
            returned[early:],
            early,
            table,
            state,
            width,
            near,
            relations,
            rel_state,
            None if last else sources[number + 1],
            () if last else groups[0],
        )
    return (table, state.reshape(row_count), relations, rel_state)


def solution(mesh):
    return sharded(mesh)


def sharded(mesh):
    return jax.shard_map(
        on_device,
        mesh=mesh,
        in_specs=(
            P(("dom", "rep"), None),
            P(("dom", "rep")),
            P(),
            P(),
            P("dom", "rep", None, None, None),
            P("dom", "rep", None, None, None),
            P("dom", "rep", None, None, None),
            P("dom", "rep", None),
        ),
        out_specs=(P(("dom", "rep"), None), P(("dom", "rep")), P(), P()),
        check_vma=False,
    )
```

```python
import functools

import jax
import jax.numpy as jnp
from jax import lax
from jax.experimental import pallas as pl
from jax.experimental.pallas import tpu as pltpu
from jax.sharding import PartitionSpec as P


ROUNDS = 2

learn_rate = 0.1
rel_rate = 0.1


SMEM = pl.BlockSpec(memory_space=pltpu.SMEM)
VMEM = pl.BlockSpec(memory_space=pltpu.VMEM)
ANY = pl.BlockSpec(memory_space=pl.ANY)
HBM = pl.BlockSpec(memory_space=pltpu.HBM)
GATHER_UNROLL = 40
SCATTER_UNROLL = 8
UPDATE_UNROLL = 8
BLOCK = 256
LANES = 128
MIB = 1024 * 1024


def params(mib, **kw):
    return pltpu.CompilerParams(vmem_limit_bytes=mib * MIB, **kw)


def cost(nbytes):
    return pl.CostEstimate(flops=0, bytes_accessed=nbytes, transcendentals=0)


def round_up(n, m):
    return (n + m - 1) // m * m


def piece(row):
    return pl.ds(pl.multiple_of(row * 2, 2), 2)


def half(start, count, side):
    return pl.ds(start * 2 + side, count, stride=2)


def gather_rows(index_ref, batches, count, table, rows, out):
    height = rows.shape[0] // 2
    if height > count:
        rows[2 * count :, :] = jnp.zeros((2 * (height - count), LANES), rows.dtype)
    for place, batch in enumerate(batches):

        @pl.loop(0, count // GATHER_UNROLL)
        def _(step):
            base = step * GATHER_UNROLL
            for j in range(GATHER_UNROLL):
                rows[piece(base + j), :] = table[piece(index_ref[batch * count + base + j]), :]

        for side in range(2):
            out[place * height : (place + 1) * height, side * LANES : (side + 1) * LANES] = rows[
                half(0, height, side), :
            ].astype(out.dtype)


def scatter_rows(jobs, count):
    @pl.loop(0, count // SCATTER_UNROLL)
    def _(step):
        base = step * SCATTER_UNROLL
        for j in range(SCATTER_UNROLL):
            spots = [piece(job[0][job[1] * count + base + j]) for job in jobs]
            olds = [job[4][spot, :] for spot, job in zip(spots, jobs)]
            for spot, old, (_, _, rows, start, total) in zip(spots, olds, jobs):
                total[spot, :] = old + rows[piece(start + base + j), :]


def scatter_live(live_ref, jobs, count):
    for first in range(0, len(jobs), 2):
        pair = jobs[first : first + 2]
        if len(pair) == 2:

            @pl.when(pair[1][1] < live_ref[0])
            def _():
                scatter_rows(pair, count)

        @pl.when((pair[0][1] < live_ref[0]) & (pair[-1][1] >= live_ref[0]))
        def _():
            scatter_rows(pair[:1], count)


def jobs_of(index, first, group_rows, totals, groups):
    jobs = []
    for group, rows in zip(groups[first:], group_rows):
        height = rows.shape[0] // (2 * len(group))
        for place, batch in enumerate(group):
            jobs.append((index, batch, rows, place * height, totals[batch % 2]))
    return jobs


def spread(ref, rows):
    for side in range(2):
        rows[half(0, ref.shape[0], side), :] = ref[:, side * LANES : (side + 1) * LANES].astype(
            jnp.float32
        )


def pack_first(index, table, edge_dst, edge_rel, batch_count, batches):
    rounds, slots, count = edge_dst.shape
    height = round_up(count, 16)
    row_count, width = table.shape
    parts = 8
    part_rows = row_count // parts

    def body(index_ref, count_ref, table_hbm, dst_ref, rel_ref, long_hbm, *refs):
        notes, refs = refs[:rounds], refs[rounds:]
        out, table_v, long_v, rows, sems = refs
        loads = []
        for part in range(parts):
            here = pl.ds(part * part_rows, part_rows)
            load = pltpu.make_async_copy(table_hbm.at[here], table_v.at[here], sems.at[part])
            load.start()
            loads.append(load)
        for number, note in enumerate(notes):
            note[:slots] = dst_ref[number]
            note[slots : 2 * slots] = rel_ref[number]
            note[2 * slots :] = jnp.full((1, count), count_ref[number], jnp.int32)
        for part in range(parts):
            loads[part].wait()

            @pl.loop(part * part_rows // LANES, (part + 1) * part_rows // LANES)
            def _(step):
                here = pl.multiple_of(step * LANES, LANES)
                for side in range(2):
                    long_v[half(here, LANES, side), :] = table_v[
                        pl.ds(here, LANES), side * LANES : (side + 1) * LANES
                    ]

        save = pltpu.make_async_copy(long_v, long_hbm, sems.at[parts])
        save.start()
        gather_rows(index_ref, batches, count, long_v, rows, out)
        save.wait()

    return pl.pallas_call(
        body,
        out_shape=[jax.ShapeDtypeStruct((2 * row_count, LANES), jnp.float32)]
        + [jax.ShapeDtypeStruct((2 * slots + 1, count), jnp.int32)] * rounds
        + [jax.ShapeDtypeStruct((len(batches) * height, width), jnp.bfloat16)],
        in_specs=[SMEM, SMEM, HBM, VMEM, VMEM],
        out_specs=[HBM] + [VMEM] * (rounds + 1),
        scratch_shapes=[
            pltpu.VMEM((row_count, width), jnp.float32),
            pltpu.VMEM((2 * row_count, LANES), jnp.float32),
            pltpu.VMEM((2 * height, LANES), jnp.float32),
            pltpu.SemaphoreType.DMA((parts + 1,)),
        ],
        compiler_params=params(56),
        cost_estimate=cost(25_000_000),
        name="pack_first",
    )(index, batch_count, table, edge_dst, edge_rel)


def pack(index, table, groups, count, width, grant):
    height = round_up(count, 16)

    def body(index_ref, table_hbm, *refs):
        outs, (table_v, rows, sem) = refs[:-3], refs[-3:]
        load = pltpu.make_async_copy(table_hbm, table_v, sem)
        load.start()
        load.wait()
        for out, group in zip(outs, groups):
            gather_rows(index_ref, group, count, table_v, rows, out)

    return pl.pallas_call(
        body,
        out_shape=[
            jax.ShapeDtypeStruct((len(group) * height, width), jnp.bfloat16) for group in groups
        ],
        in_specs=[SMEM, HBM],
        out_specs=[VMEM] * len(groups),
        scratch_shapes=[
            pltpu.VMEM(table.shape, jnp.float32),
            pltpu.VMEM((2 * height, LANES), jnp.float32),
            pltpu.SemaphoreType.DMA,
        ],
        compiler_params=params(grant),
        cost_estimate=cost(30_000_000),
    )(index, table)


def batch_kernel(group, count, live_ref, kind_ref, source_ref, target_ref, rel_ref, rel_in,
                 grad_source, grad_target, rel_out, query_t, total_t, product):
    height, width = source_ref.shape[0] // len(group), source_ref.shape[1]
    full = round_up(height, BLOCK)
    kinds = rel_ref.shape[0]
    neg_share = 0.5 / (count - 1)
    rel_out[...] = rel_in[...]

    @pl.loop(0, jnp.clip(live_ref[0] - group[0], 0, len(group)))
    def _(place):
        start = pl.multiple_of(place * height, 16)
        rel = rel_ref[...]
        high = rel.astype(jnp.bfloat16)
        rest = rel - high.astype(jnp.float32)
        mid = rest.astype(jnp.bfloat16)
        low = (rest - mid.astype(jnp.float32)).astype(jnp.bfloat16)
        parts = jnp.concatenate([high, mid, low], axis=0)
        kind = jnp.broadcast_to(kind_ref[pl.ds(place, 1), :], (3 * kinds, full))
        row = lax.broadcasted_iota(jnp.int32, (3 * kinds, full), 0)
        hot = jnp.where((row % kinds) == kind, 1.0, 0.0).astype(jnp.bfloat16)
        diagonal = lax.dot_general(
            hot, parts, (((0,), (0,)), ((), ())), preferred_element_type=jnp.float32
        )
        source = source_ref[pl.ds(start, height), :].astype(jnp.float32)
        target = target_ref[pl.ds(start, height), :]
        if full > height:
            gap = jnp.zeros((full - height, width), jnp.float32)
            source = jnp.concatenate([source, gap], axis=0)
            target = jnp.concatenate([target, gap.astype(target.dtype)], axis=0)
        query_full = (source * diagonal).astype(jnp.bfloat16).astype(jnp.float32)
        query_t[...] = query_full.T.astype(jnp.bfloat16)
        half_query = (query_full * 0.5).astype(jnp.bfloat16)
        eye = lax.broadcasted_iota(jnp.int32, (BLOCK, BLOCK), 0) == lax.broadcasted_iota(
            jnp.int32, (BLOCK, BLOCK), 1
        )
        for block in range(full // BLOCK):
            here = slice(block * BLOCK, (block + 1) * BLOCK)
            pieces = []
            for col in range(full // BLOCK):
                there = slice(col * BLOCK, (col + 1) * BLOCK)
                slope = jnp.tanh(
                    lax.dot_general(
                        half_query[here],
                        target[there],
                        (((1,), (1,)), ((), ())),
                        preferred_element_type=jnp.float32,
                    )
                )
                weight = slope * neg_share + neg_share
                if col == block:
                    weight = jnp.where(eye, slope * 0.5 - 0.5, weight)
                pieces.append(weight.astype(jnp.bfloat16))
            weights = jnp.concatenate(pieces, axis=1)
            grad_query = jnp.dot(weights, target, preferred_element_type=jnp.float32)
            tall = min(height - block * BLOCK, BLOCK)
            grad_rows = (grad_query * diagonal[here])[:tall]
            spot = pl.multiple_of(start + block * BLOCK, 16)
            grad_source[pl.ds(spot, tall), :] = grad_rows.astype(grad_source.dtype)
            product[here, :] = grad_query * source[here]
            part = jnp.dot(query_t[:, here], weights, preferred_element_type=jnp.float32)
            if block == 0:
                total_t[...] = part
            else:
                total_t[...] += part
        grad_rows = total_t[...].T[:height]
        for side in range(2):
            grad_target[half(start, height, side), :] = grad_rows[:, side * LANES : (side + 1) * LANES]
        value = product[...]
        upper = value.astype(jnp.bfloat16)
        lower = (value - upper.astype(jnp.float32)).astype(jnp.bfloat16)
        one = hot[:kinds]
        rel_out[...] = (
            rel_out[...]
            + jnp.dot(one, upper, preferred_element_type=jnp.float32)
            + jnp.dot(one, lower, preferred_element_type=jnp.float32)
        )


def run_group(group, count, live, kind, source, target, relations, rel_grad):
    height, width = source.shape
    full = round_up(height // len(group), BLOCK)
    return pl.pallas_call(
        functools.partial(batch_kernel, group, count),
        out_shape=[
            jax.ShapeDtypeStruct((height, width), jnp.bfloat16),
            jax.ShapeDtypeStruct((2 * height, LANES), jnp.float32),
            jax.ShapeDtypeStruct(rel_grad.shape, jnp.float32),
        ],
        in_specs=[SMEM] + [VMEM] * 5,
        out_specs=[VMEM] * 3,
        scratch_shapes=[
            pltpu.VMEM((width, full), jnp.bfloat16),
            pltpu.VMEM((width, full), jnp.float32),
            pltpu.VMEM((full, width), jnp.float32),
        ],
        compiler_params=params(24),
        cost_estimate=cost(15_000_000),
        name="batch_terms",
    )(live, kind, source, target, relations, rel_grad)


def first_total(count, groups, row_count, live, other_live, source_index, other_index, own, returned):
    parts = 8
    part_rows = 2 * row_count // parts
    loads = len(own) + len(returned)

    def body(live_ref, other_ref, source_ref, index_ref, *refs):
        inputs, out_hbm = refs[:loads], refs[loads]
        buffers = refs[loads + 1 : 2 * loads + 1]
        rows = refs[2 * loads + 1 : -3]
        total, other, sems = refs[-3:]
        totals = (total, other)
        copies = [
            pltpu.make_async_copy(ref, buffer, sems.at[number])
            for number, (ref, buffer) in enumerate(zip(inputs, buffers))
        ]
        for copy in copies:
            copy.start()
        total[...] = jnp.zeros_like(total)
        other[...] = jnp.zeros_like(other)
        for copy in copies:
            copy.wait()
        for buffer, long in zip(buffers[len(own) :], rows):
            spread(buffer, long)
        scatter_live(
            live_ref,
            jobs_of(source_ref, 0, buffers[: len(own)], totals, groups),
            count,
        )
        scatter_live(
            other_ref,
            jobs_of(index_ref, 0, rows, totals, groups),
            count,
        )
        saves = []
        for part in range(parts):
            here = pl.ds(part * part_rows, part_rows)
            total[here, :] += other[here, :]
            save = pltpu.make_async_copy(total.at[here], out_hbm.at[here], sems.at[loads + part])
            save.start()
            saves.append(save)
        for save in saves:
            save.wait()

    return pl.pallas_call(
        body,
        out_shape=jax.ShapeDtypeStruct((2 * row_count, LANES), jnp.float32),
        in_specs=[SMEM] * 4 + [ANY] * loads,
        out_specs=ANY,
        scratch_shapes=[pltpu.VMEM(array.shape, array.dtype) for array in (*own, *returned)]
        + [pltpu.VMEM(own[0].shape, jnp.float32)] * len(returned)
        + [pltpu.VMEM((2 * row_count, LANES), jnp.float32)] * 2
        + [pltpu.SemaphoreType.DMA((loads + parts,))],
        compiler_params=params(50),
        cost_estimate=cost(60_000_000),
        name="first_total",
    )(live, other_live, source_index, other_index, *own, *returned)


def finish(
    count, groups, live, source_index, total, returned, first, table, state, width, near, relations, rel_state, next_index, next_batches
):
    row_count = table.shape[0] // 2
    height = returned[0].shape[0]
    tiles = row_count // LANES
    step_rows = 1024
    steps = row_count // step_rows
    last = next_index is None
    indices = [live, source_index] + ([] if last else [next_index])

    def body(*refs):
        refs = list(refs)

        def take(number):
            taken = refs[:number]
            del refs[:number]
            return taken

        live_ref, index_ref, *next_ref = take(len(indices))
        (total_hbm,) = take(1)
        back_refs = take(len(returned))
        table_hbm, state_ref = take(2)
        near_refs = take(len(near))
        rel_refs = take(2 if last else 0)
        out_hbm, state_out = take(2)
        new_rel_refs = take(2 if last else 0)
        next_outs = take(0 if last else 1)
        total_v, other_v, third_v, table_v, state_t, mean_t, sems = take(7)
        rows = take(len(returned))
        out_v = refs[0] if last else table_v
        load_total = pltpu.make_async_copy(total_hbm, total_v, sems.at[0])
        load_table = pltpu.make_async_copy(table_hbm, table_v, sems.at[1])
        load_total.start()
        load_table.start()
        other_v[...] = jnp.zeros_like(other_v)
        third_v[...] = jnp.zeros_like(third_v)
        for ref, long in zip(back_refs, rows):
            spread(ref, long)
        if last:
            rel_total = pair_sum([ref[...] for ref in near_refs])
            rel_new = rel_refs[1][...] + rel_total * rel_total
            new_rel_refs[1][...] = rel_new
            new_rel_refs[0][...] = rel_refs[0][...] - rel_rate * rel_total / jnp.sqrt(rel_new)
        spare = jnp.zeros((LANES - tiles, LANES), jnp.float32)
        state_t[...] = jnp.concatenate([state_ref[...], spare], axis=0).T
        mean_t[...] = jnp.zeros_like(mean_t)
        totals = (other_v, third_v)
        scatter_live(
            live_ref,
            jobs_of(index_ref, first, rows, totals, groups),
            count,
        )
        load_total.wait()
        load_table.wait()
        lane = lax.broadcasted_iota(jnp.int32, (LANES, LANES), 1)
        saves = []
        for step in range(steps):

            @pl.loop(step * step_rows // LANES, (step + 1) * step_rows // LANES, unroll=UPDATE_UNROLL)
            def _(group):
                base = pl.multiple_of(group * LANES, LANES)
                sides = [half(base, LANES, side) for side in range(2)]
                grads = [total_v[side, :] + (other_v[side, :] + third_v[side, :]) for side in sides]
                square = grads[0] * grads[0] + grads[1] * grads[1]
                mean = jnp.sum(square, axis=1, keepdims=True) * (1.0 / width)
                mine = lane == group
                old = jnp.sum(jnp.where(mine, state_t[...], 0.0), axis=1, keepdims=True)
                mean_t[...] = jnp.where(mine, mean, mean_t[...])
                scale = learn_rate / jnp.sqrt(old + mean)
                values = [table_v[side, :] - grad * scale for side, grad in zip(sides, grads)]
                for number, value in enumerate(values):
                    if last:
                        out_v[pl.ds(base, LANES), number * LANES : (number + 1) * LANES] = value
                    else:
                        out_v[sides[number], :] = value

            tall = step_rows if last else 2 * step_rows
            part = pl.ds(step * tall, tall)
            save = pltpu.make_async_copy(out_v.at[part], out_hbm.at[part], sems.at[2 + step])
            save.start()
            saves.append(save)
        state_out[...] = (state_t[...] + mean_t[...]).T[:tiles]
        for out in next_outs:
            gather_rows(
                next_ref[0], next_batches, count, table_v, rows[0].at[: 2 * round_up(count, 16)], out
            )
        for save in saves:
            save.wait()

    out_shape = (row_count, width) if last else table.shape
    rel_shape = jax.ShapeDtypeStruct(relations.shape, jnp.float32)
    return pl.pallas_call(
        body,
        out_shape=[
            jax.ShapeDtypeStruct(out_shape, jnp.float32),
            jax.ShapeDtypeStruct((tiles, LANES), jnp.float32),
        ]
        + [rel_shape] * (2 * last)
        + [jax.ShapeDtypeStruct((len(next_batches) * round_up(count, 16), width), jnp.bfloat16)]
        * (not last),
        in_specs=[SMEM] * len(indices)
        + [ANY]
        + [VMEM] * len(returned)
        + [HBM]
        + [VMEM] * (1 + len(near) + 2 * last),
        out_specs=[HBM] + [VMEM] * (1 + 2 * last + (not last)),
        scratch_shapes=[
            pltpu.VMEM(table.shape, jnp.float32),
            pltpu.VMEM(table.shape, jnp.float32),
            pltpu.VMEM(table.shape, jnp.float32),
            pltpu.VMEM(table.shape, jnp.float32),
            pltpu.VMEM((LANES, LANES), jnp.float32),
            pltpu.VMEM((LANES, LANES), jnp.float32),
            pltpu.SemaphoreType.DMA((2 + steps,)),
        ]
        + [pltpu.VMEM((2 * height, LANES), jnp.float32)] * len(returned)
        + ([pltpu.VMEM((row_count, width), jnp.float32)] if last else []),
        compiler_params=params(50),
        cost_estimate=cost(50_000_000),
        name="finish_last" if last else "finish_next",
    )(*indices, total, *returned, table, state, *near, *((relations, rel_state) if last else ()))


def flip(index, bits):
    for place in range(8):
        step = 1 << place
        if bits & step:
            index = index + step * (1 - 2 * ((index // step) % 2))
    return index


def relation_kernel(stages, near, finish, *scratch):
    parts, received = scratch[:-3], scratch[-3]
    send_sems, recv_sems = scratch[-2:]
    dom, rep = lax.axis_index("dom"), lax.axis_index("rep")

    def device(peer):
        return (flip(dom, peer[0]), flip(rep, peer[1]))

    barrier = pltpu.get_barrier_semaphore()
    peers = [peer for stage in stages for peer in stage]
    for peer in peers:
        pl.semaphore_signal(
            barrier, inc=1, device_id=device(peer), device_id_type=pl.DeviceIdType.MESH
        )
    pl.semaphore_wait(barrier, len(peers))
    parts[0][...] = pair_sum([ref[...] for ref in near])
    slot = 0
    for number, stage in enumerate(stages):
        copies = []
        for peer in stage:
            copy = pltpu.make_async_remote_copy(
                src_ref=parts[number],
                dst_ref=received.at[slot],
                send_sem=send_sems.at[slot],
                recv_sem=recv_sems.at[slot],
                device_id=device(peer),
                device_id_type=pl.DeviceIdType.MESH,
            )
            copy.start()
            copies.append(copy)
            slot += 1
        for copy in copies:
            copy.wait()
        first = slot - len(stage)
        total = pair_sum([parts[number][...]] + [received[first + i] for i in range(len(stage))])
        if number + 1 < len(stages):
            parts[number + 1][...] = total
    finish(total)


def pair_sum(values):
    while len(values) > 1:
        values = [values[i] + values[i + 1] for i in range(0, len(values), 2)]
    return values[0]


def relation_call(body, inputs, outputs, collective_id):
    slots = sum(len(stage) for stage in STAGES)
    shape = inputs[0].shape
    return pl.pallas_call(
        body,
        out_shape=[jax.ShapeDtypeStruct(shape, jnp.float32)] * outputs,
        in_specs=[VMEM] * len(inputs),
        out_specs=[VMEM] * outputs,
        scratch_shapes=[pltpu.VMEM(shape, jnp.float32)] * len(STAGES)
        + [
            pltpu.VMEM((slots,) + shape, jnp.float32),
            pltpu.SemaphoreType.DMA((slots,)),
            pltpu.SemaphoreType.DMA((slots,)),
        ],
        compiler_params=pltpu.CompilerParams(
            collective_id=collective_id, has_side_effects=True, vmem_limit_bytes=4 * MIB
        ),
        cost_estimate=cost(20_000_000),
    )(*inputs)


STAGES = (
    ((0, 1), (0, 2), (0, 3)),
    ((1, 0), (2, 0), (3, 0)),
    ((4, 0),),
)


def relation_sum(rel_grad):
    def body(own, summed, *scratch):
        def finish(total):
            summed[...] = total

        relation_kernel(STAGES, [own], finish, *scratch)

    return relation_call(body, [rel_grad], 1, 0)[0]


def relation_step(near, relations, rel_state):
    count = len(near)

    def body(*refs):
        near_refs = refs[:count]
        rel_ref, state_ref, new_rel, new_state = refs[count : count + 4]

        def finish(total):
            state = state_ref[...] + total * total
            new_state[...] = state
            new_rel[...] = rel_ref[...] - rel_rate * total / jnp.sqrt(state)

        relation_kernel(STAGES, near_refs, finish, *refs[count + 4 :])

    return relation_call(body, [*near, relations, rel_state], 2, 1)


def from_partner(shard, axis, distance):
    return from_peer(shard, axis, 1 << distance)


def from_peer(shard, axis, bits):
    return lax.ppermute(shard, axis, [(i, i ^ bits) for i in range(lax.axis_size(axis))])


def on_device(
    embeddings, row_state, relations, rel_state, edge_src, edge_dst, edge_rel, batch_count
):
    bit_count = lax.axis_size("dom").bit_length() - 1
    row_count, width = embeddings.shape
    batches, count = edge_src.shape[-2:]
    padded = round_up(count, BLOCK)
    state = row_state.reshape(row_count // LANES, LANES)
    spots = [bit_count - 1 - number for number in range(ROUNDS)]
    groups = tuple(
        tuple(range(first, min(first + 2, batches))) for first in range(0, batches, 2)
    )
    sources = [edge_src[0, 0, number].reshape(-1) for number in range(ROUNDS)]
    table, *told = pack_first(
        sources[0], embeddings, edge_dst[0, 0], edge_rel[0, 0], batch_count[0, 0], groups[0]
    )
    told, sent = told[:ROUNDS], told[ROUNDS:]
    for number in range(ROUNDS):
        last = number + 1 == ROUNDS
        swap_bit = spots[number]
        source_index = sources[number]
        live = batch_count[0, 0, number].reshape(1)
        note = from_partner(told[number], "dom", swap_bit)
        arrived = [from_partner(sent[0], "dom", swap_bit)]
        more = pack(source_index, table, groups[1:], count, width, 54)
        for rows in more:
            arrived.append(from_partner(rows, "dom", swap_bit))
        other_index = note[:batches].reshape(-1)
        other_live = note[2 * batches, :1]
        kinds = jnp.pad(
            note[batches : 2 * batches], ((0, 0), (0, padded - count)), constant_values=-1
        )
        targets = pack(other_index, table, groups, count, width, 50)
        if number:
            near, targets = lax.optimization_barrier((near, targets))
            relations, rel_state = relation_step(near, relations, rel_state)
        rel_grad = jnp.zeros(relations.shape, jnp.float32)
        own, returned = [], []
        for place, group in enumerate(groups):
            grad_source, grad_target, rel_grad = run_group(
                group,
                count,
                other_live,
                kinds[group[0] : group[-1] + 1],
                arrived[place],
                targets[place],
                relations,
                rel_grad,
            )
            own.append(grad_target)
            returned.append(from_partner(grad_source, "dom", swap_bit))
        if last:
            rel_grad = relation_sum(rel_grad)
        near = [rel_grad]
        for bits in (8, 16, 24):
            near.append(from_peer(rel_grad, "dom", bits))
        early = len(groups) - 1
        total = first_total(
            count, groups, row_count, other_live, live, other_index, source_index, own, returned[:early]
        )
        table, state, *more = finish(
            count,
            groups,
            live,
            source_index,
            total,
            returned[early:],
            early,
            table,
            state,
            width,
            near if last else (),
            relations,
            rel_state,
            None if last else sources[number + 1],
            () if last else groups[0],
        )
        if last:
            relations, rel_state = more
        else:
            sent = more
    return (table, state.reshape(row_count), relations, rel_state)


def solution(mesh):
    return sharded(mesh)


def sharded(mesh):
    return jax.shard_map(
        on_device,
        mesh=mesh,
        in_specs=(
            P(("dom", "rep"), None),
            P(("dom", "rep")),
            P(),
            P(),
            P("dom", "rep", None, None, None),
            P("dom", "rep", None, None, None),
            P("dom", "rep", None, None, None),
            P("dom", "rep", None),
        ),
        out_specs=(P(("dom", "rep"), None), P(("dom", "rep")), P(), P()),
        check_vma=False,
    )
```

```python
import functools

import jax
import jax.numpy as jnp
from jax import lax
from jax.experimental import pallas as pl
from jax.experimental.pallas import tpu as pltpu
from jax.sharding import PartitionSpec as P


ROUNDS = 2

learn_rate = 0.1
rel_rate = 0.1


SMEM = pl.BlockSpec(memory_space=pltpu.SMEM)
VMEM = pl.BlockSpec(memory_space=pltpu.VMEM)
ANY = pl.BlockSpec(memory_space=pl.ANY)
HBM = pl.BlockSpec(memory_space=pltpu.HBM)
GATHER_UNROLL = 40
SCATTER_UNROLL = 8
UPDATE_UNROLL = 8
BLOCK = 256
LANES = 128
MIB = 1024 * 1024


def params(mib, **kw):
    return pltpu.CompilerParams(vmem_limit_bytes=mib * MIB, **kw)


def cost(nbytes):
    return pl.CostEstimate(flops=0, bytes_accessed=nbytes, transcendentals=0)


def round_up(n, m):
    return (n + m - 1) // m * m


def piece(row):
    return pl.ds(pl.multiple_of(row * 2, 2), 2)


def half(start, count, side):
    return pl.ds(start * 2 + side, count, stride=2)


def gather_rows(index_ref, batches, count, table, rows, out):
    height = rows.shape[0] // 2
    if height > count:
        rows[2 * count :, :] = jnp.zeros((2 * (height - count), LANES), rows.dtype)
    for place, batch in enumerate(batches):

        @pl.loop(0, count // GATHER_UNROLL)
        def _(step):
            base = step * GATHER_UNROLL
            for j in range(GATHER_UNROLL):
                rows[piece(base + j), :] = table[piece(index_ref[batch * count + base + j]), :]

        for side in range(2):
            out[place * height : (place + 1) * height, side * LANES : (side + 1) * LANES] = rows[
                half(0, height, side), :
            ].astype(out.dtype)


def scatter_rows(jobs, count):
    @pl.loop(0, count // SCATTER_UNROLL)
    def _(step):
        base = step * SCATTER_UNROLL
        for j in range(SCATTER_UNROLL):
            spots = [piece(job[0][job[1] * count + base + j]) for job in jobs]
            olds = [job[4][spot, :] for spot, job in zip(spots, jobs)]
            for spot, old, (_, _, rows, start, total) in zip(spots, olds, jobs):
                total[spot, :] = old + rows[piece(start + base + j), :]


def scatter_live(live_ref, jobs, count):
    for first in range(0, len(jobs), 2):
        pair = jobs[first : first + 2]
        if len(pair) == 2:

            @pl.when(pair[1][1] < live_ref[0])
            def _():
                scatter_rows(pair, count)

        @pl.when((pair[0][1] < live_ref[0]) & (pair[-1][1] >= live_ref[0]))
        def _():
            scatter_rows(pair[:1], count)


def jobs_of(index, first, group_rows, totals, groups):
    jobs = []
    for group, rows in zip(groups[first:], group_rows):
        height = rows.shape[0] // (2 * len(group))
        for place, batch in enumerate(group):
            jobs.append((index, batch, rows, place * height, totals[batch % 2]))
    return jobs


def spread(ref, rows):
    for side in range(2):
        rows[half(0, ref.shape[0], side), :] = ref[:, side * LANES : (side + 1) * LANES].astype(
            jnp.float32
        )


def pack_first(index, table, edge_dst, edge_rel, batch_count, batches):
    rounds, slots, count = edge_dst.shape
    height = round_up(count, 16)
    row_count, width = table.shape
    parts = 8
    part_rows = row_count // parts

    def body(index_ref, count_ref, table_hbm, dst_ref, rel_ref, long_hbm, *refs):
        notes, refs = refs[:rounds], refs[rounds:]
        out, table_v, long_v, rows, sems = refs
        loads = []
        for part in range(parts):
            here = pl.ds(part * part_rows, part_rows)
            load = pltpu.make_async_copy(table_hbm.at[here], table_v.at[here], sems.at[part])
            load.start()
            loads.append(load)
        for number, note in enumerate(notes):
            note[:slots] = dst_ref[number] + rel_ref[number] * row_count
            note[slots:] = jnp.full((1, count), count_ref[number], jnp.int32)
        for part in range(parts):
            loads[part].wait()

            @pl.loop(part * part_rows // LANES, (part + 1) * part_rows // LANES)
            def _(step):
                here = pl.multiple_of(step * LANES, LANES)
                for side in range(2):
                    long_v[half(here, LANES, side), :] = table_v[
                        pl.ds(here, LANES), side * LANES : (side + 1) * LANES
                    ]

        save = pltpu.make_async_copy(long_v, long_hbm, sems.at[parts])
        save.start()
        gather_rows(index_ref, batches, count, long_v, rows, out)
        save.wait()

    return pl.pallas_call(
        body,
        out_shape=[jax.ShapeDtypeStruct((2 * row_count, LANES), jnp.float32)]
        + [jax.ShapeDtypeStruct((slots + 1, count), jnp.int32)] * rounds
        + [jax.ShapeDtypeStruct((len(batches) * height, width), jnp.bfloat16)],
        in_specs=[SMEM, SMEM, HBM, VMEM, VMEM],
        out_specs=[HBM] + [VMEM] * (rounds + 1),
        scratch_shapes=[
            pltpu.VMEM((row_count, width), jnp.float32),
            pltpu.VMEM((2 * row_count, LANES), jnp.float32),
            pltpu.VMEM((2 * height, LANES), jnp.float32),
            pltpu.SemaphoreType.DMA((parts + 1,)),
        ],
        compiler_params=params(56),
        cost_estimate=cost(25_000_000),
        name="pack_first",
    )(index, batch_count, table, edge_dst, edge_rel)


def pack(index, table, groups, count, width, grant):
    height = round_up(count, 16)

    def body(index_ref, table_hbm, *refs):
        outs, (table_v, rows, sem) = refs[:-3], refs[-3:]
        load = pltpu.make_async_copy(table_hbm, table_v, sem)
        load.start()
        load.wait()
        for out, group in zip(outs, groups):
            gather_rows(index_ref, group, count, table_v, rows, out)

    return pl.pallas_call(
        body,
        out_shape=[
            jax.ShapeDtypeStruct((len(group) * height, width), jnp.bfloat16) for group in groups
        ],
        in_specs=[SMEM, HBM],
        out_specs=[VMEM] * len(groups),
        scratch_shapes=[
            pltpu.VMEM(table.shape, jnp.float32),
            pltpu.VMEM((2 * height, LANES), jnp.float32),
            pltpu.SemaphoreType.DMA,
        ],
        compiler_params=params(grant),
        cost_estimate=cost(30_000_000),
    )(index, table)


def batch_kernel(group, count, live_ref, kind_ref, source_ref, target_ref, rel_ref, rel_in,
                 grad_source, grad_target, rel_out, query_t, total_t, product):
    height, width = source_ref.shape[0] // len(group), source_ref.shape[1]
    full = round_up(height, BLOCK)
    kinds = rel_ref.shape[0]
    neg_share = 0.5 / (count - 1)
    rel_out[...] = rel_in[...]

    @pl.loop(0, jnp.clip(live_ref[0] - group[0], 0, len(group)))
    def _(place):
        start = pl.multiple_of(place * height, 16)
        rel = rel_ref[...]
        high = rel.astype(jnp.bfloat16)
        rest = rel - high.astype(jnp.float32)
        mid = rest.astype(jnp.bfloat16)
        low = (rest - mid.astype(jnp.float32)).astype(jnp.bfloat16)
        parts = jnp.concatenate([high, mid, low], axis=0)
        kind = jnp.broadcast_to(kind_ref[pl.ds(place, 1), :], (3 * kinds, full))
        row = lax.broadcasted_iota(jnp.int32, (3 * kinds, full), 0)
        hot = jnp.where((row % kinds) == kind, 1.0, 0.0).astype(jnp.bfloat16)
        diagonal = lax.dot_general(
            hot, parts, (((0,), (0,)), ((), ())), preferred_element_type=jnp.float32
        )
        source = source_ref[pl.ds(start, height), :].astype(jnp.float32)
        target = target_ref[pl.ds(start, height), :]
        if full > height:
            gap = jnp.zeros((full - height, width), jnp.float32)
            source = jnp.concatenate([source, gap], axis=0)
            target = jnp.concatenate([target, gap.astype(target.dtype)], axis=0)
        query_full = (source * diagonal).astype(jnp.bfloat16).astype(jnp.float32)
        query_t[...] = query_full.T.astype(jnp.bfloat16)
        half_query = (query_full * 0.5).astype(jnp.bfloat16)
        eye = lax.broadcasted_iota(jnp.int32, (BLOCK, BLOCK), 0) == lax.broadcasted_iota(
            jnp.int32, (BLOCK, BLOCK), 1
        )
        for block in range(full // BLOCK):
            here = slice(block * BLOCK, (block + 1) * BLOCK)
            pieces = []
            for col in range(full // BLOCK):
                there = slice(col * BLOCK, (col + 1) * BLOCK)
                slope = jnp.tanh(
                    lax.dot_general(
                        half_query[here],
                        target[there],
                        (((1,), (1,)), ((), ())),
                        preferred_element_type=jnp.float32,
                    )
                )
                weight = slope * neg_share + neg_share
                if col == block:
                    weight = jnp.where(eye, slope * 0.5 - 0.5, weight)
                pieces.append(weight.astype(jnp.bfloat16))
            weights = jnp.concatenate(pieces, axis=1)
            grad_query = jnp.dot(weights, target, preferred_element_type=jnp.float32)
            tall = min(height - block * BLOCK, BLOCK)
            grad_rows = (grad_query * diagonal[here])[:tall]
            spot = pl.multiple_of(start + block * BLOCK, 16)
            grad_source[pl.ds(spot, tall), :] = grad_rows.astype(grad_source.dtype)
            product[here, :] = grad_query * source[here]
            part = jnp.dot(query_t[:, here], weights, preferred_element_type=jnp.float32)
            if block == 0:
                total_t[...] = part
            else:
                total_t[...] += part
        grad_rows = total_t[...].T[:height]
        for side in range(2):
            grad_target[half(start, height, side), :] = grad_rows[:, side * LANES : (side + 1) * LANES]
        value = product[...]
        upper = value.astype(jnp.bfloat16)
        lower = (value - upper.astype(jnp.float32)).astype(jnp.bfloat16)
        one = hot[:kinds]
        rel_out[...] = (
            rel_out[...]
            + jnp.dot(one, upper, preferred_element_type=jnp.float32)
            + jnp.dot(one, lower, preferred_element_type=jnp.float32)
        )


def run_group(group, count, live, kind, source, target, relations, rel_grad):
    height, width = source.shape
    full = round_up(height // len(group), BLOCK)
    return pl.pallas_call(
        functools.partial(batch_kernel, group, count),
        out_shape=[
            jax.ShapeDtypeStruct((height, width), jnp.bfloat16),
            jax.ShapeDtypeStruct((2 * height, LANES), jnp.float32),
            jax.ShapeDtypeStruct(rel_grad.shape, jnp.float32),
        ],
        in_specs=[SMEM] + [VMEM] * 5,
        out_specs=[VMEM] * 3,
        scratch_shapes=[
            pltpu.VMEM((width, full), jnp.bfloat16),
            pltpu.VMEM((width, full), jnp.float32),
            pltpu.VMEM((full, width), jnp.float32),
        ],
        compiler_params=params(24),
        cost_estimate=cost(15_000_000),
        name="batch_terms",
    )(live, kind, source, target, relations, rel_grad)


def first_total(count, groups, row_count, live, other_live, source_index, other_index, own, returned):
    parts = 8
    part_rows = 2 * row_count // parts
    loads = len(own) + len(returned)

    def body(live_ref, other_ref, source_ref, index_ref, *refs):
        inputs, out_hbm = refs[:loads], refs[loads]
        buffers = refs[loads + 1 : 2 * loads + 1]
        rows = refs[2 * loads + 1 : -3]
        total, other, sems = refs[-3:]
        totals = (total, other)
        copies = [
            pltpu.make_async_copy(ref, buffer, sems.at[number])
            for number, (ref, buffer) in enumerate(zip(inputs, buffers))
        ]
        for copy in copies:
            copy.start()
        total[...] = jnp.zeros_like(total)
        other[...] = jnp.zeros_like(other)
        for copy in copies:
            copy.wait()
        for buffer, long in zip(buffers[len(own) :], rows):
            spread(buffer, long)
        scatter_live(
            live_ref,
            jobs_of(source_ref, 0, buffers[: len(own)], totals, groups),
            count,
        )
        scatter_live(
            other_ref,
            jobs_of(index_ref, 0, rows, totals, groups),
            count,
        )
        saves = []
        for part in range(parts):
            here = pl.ds(part * part_rows, part_rows)
            total[here, :] += other[here, :]
            save = pltpu.make_async_copy(total.at[here], out_hbm.at[here], sems.at[loads + part])
            save.start()
            saves.append(save)
        for save in saves:
            save.wait()

    return pl.pallas_call(
        body,
        out_shape=jax.ShapeDtypeStruct((2 * row_count, LANES), jnp.float32),
        in_specs=[SMEM] * 4 + [ANY] * loads,
        out_specs=ANY,
        scratch_shapes=[pltpu.VMEM(array.shape, array.dtype) for array in (*own, *returned)]
        + [pltpu.VMEM(own[0].shape, jnp.float32)] * len(returned)
        + [pltpu.VMEM((2 * row_count, LANES), jnp.float32)] * 2
        + [pltpu.SemaphoreType.DMA((loads + parts,))],
        compiler_params=params(44),
        cost_estimate=cost(60_000_000),
        name="first_total",
    )(live, other_live, source_index, other_index, *own, *returned)


def finish(
    count, groups, live, source_index, total, returned, first, table, state, width, near, relations, rel_state, next_index, next_batches
):
    row_count = table.shape[0] // 2
    height = returned[0].shape[0]
    tiles = row_count // LANES
    step_rows = 1024
    steps = row_count // step_rows
    last = next_index is None
    indices = [live, source_index] + ([] if last else [next_index])

    def body(*refs):
        refs = list(refs)

        def take(number):
            taken = refs[:number]
            del refs[:number]
            return taken

        live_ref, index_ref, *next_ref = take(len(indices))
        (total_hbm,) = take(1)
        back_refs = take(len(returned))
        table_hbm, state_ref = take(2)
        near_refs = take(len(near))
        rel_refs = take(2 if last else 0)
        out_hbm, state_out = take(2)
        new_rel_refs = take(2 if last else 0)
        next_outs = take(0 if last else 1)
        total_v, other_v, third_v, table_v, state_t, mean_t, sems = take(7)
        rows = take(len(returned))
        out_v = refs[0] if last else table_v
        load_total = pltpu.make_async_copy(total_hbm, total_v, sems.at[0])
        load_table = pltpu.make_async_copy(table_hbm, table_v, sems.at[1])
        load_total.start()
        load_table.start()
        other_v[...] = jnp.zeros_like(other_v)
        third_v[...] = jnp.zeros_like(third_v)
        for ref, long in zip(back_refs, rows):
            spread(ref, long)
        if last:
            rel_total = pair_sum([ref[...] for ref in near_refs])
            rel_new = rel_refs[1][...] + rel_total * rel_total
            new_rel_refs[1][...] = rel_new
            new_rel_refs[0][...] = rel_refs[0][...] - rel_rate * rel_total / jnp.sqrt(rel_new)
        spare = jnp.zeros((LANES - tiles, LANES), jnp.float32)
        state_t[...] = jnp.concatenate([state_ref[...], spare], axis=0).T
        mean_t[...] = jnp.zeros_like(mean_t)
        totals = (other_v, third_v)
        scatter_live(
            live_ref,
            jobs_of(index_ref, first, rows, totals, groups),
            count,
        )
        load_total.wait()
        load_table.wait()
        lane = lax.broadcasted_iota(jnp.int32, (LANES, LANES), 1)
        saves = []
        for step in range(steps):

            @pl.loop(step * step_rows // LANES, (step + 1) * step_rows // LANES, unroll=UPDATE_UNROLL)
            def _(group):
                base = pl.multiple_of(group * LANES, LANES)
                sides = [half(base, LANES, side) for side in range(2)]
                grads = [total_v[side, :] + (other_v[side, :] + third_v[side, :]) for side in sides]
                square = grads[0] * grads[0] + grads[1] * grads[1]
                mean = jnp.sum(square, axis=1, keepdims=True) * (1.0 / width)
                mine = lane == group
                old = jnp.sum(jnp.where(mine, state_t[...], 0.0), axis=1, keepdims=True)
                mean_t[...] = jnp.where(mine, mean, mean_t[...])
                scale = learn_rate / jnp.sqrt(old + mean)
                values = [table_v[side, :] - grad * scale for side, grad in zip(sides, grads)]
                for number, value in enumerate(values):
                    if last:
                        out_v[pl.ds(base, LANES), number * LANES : (number + 1) * LANES] = value
                    else:
                        out_v[sides[number], :] = value

            tall = step_rows if last else 2 * step_rows
            part = pl.ds(step * tall, tall)
            save = pltpu.make_async_copy(out_v.at[part], out_hbm.at[part], sems.at[2 + step])
            save.start()
            saves.append(save)
        state_out[...] = (state_t[...] + mean_t[...]).T[:tiles]
        for out in next_outs:
            gather_rows(
                next_ref[0], next_batches, count, table_v, rows[0].at[: 2 * round_up(count, 16)], out
            )
        for save in saves:
            save.wait()

    out_shape = (row_count, width) if last else table.shape
    rel_shape = jax.ShapeDtypeStruct(relations.shape, jnp.float32)
    return pl.pallas_call(
        body,
        out_shape=[
            jax.ShapeDtypeStruct(out_shape, jnp.float32),
            jax.ShapeDtypeStruct((tiles, LANES), jnp.float32),
        ]
        + [rel_shape] * (2 * last)
        + [jax.ShapeDtypeStruct((len(next_batches) * round_up(count, 16), width), jnp.bfloat16)]
        * (not last),
        in_specs=[SMEM] * len(indices)
        + [ANY]
        + [VMEM] * len(returned)
        + [HBM]
        + [VMEM] * (1 + len(near) + 2 * last),
        out_specs=[HBM] + [VMEM] * (1 + 2 * last + (not last)),
        scratch_shapes=[
            pltpu.VMEM(table.shape, jnp.float32),
            pltpu.VMEM(table.shape, jnp.float32),
            pltpu.VMEM(table.shape, jnp.float32),
            pltpu.VMEM(table.shape, jnp.float32),
            pltpu.VMEM((LANES, LANES), jnp.float32),
            pltpu.VMEM((LANES, LANES), jnp.float32),
            pltpu.SemaphoreType.DMA((2 + steps,)),
        ]
        + [pltpu.VMEM((2 * height, LANES), jnp.float32)] * len(returned)
        + ([pltpu.VMEM((row_count, width), jnp.float32)] if last else []),
        compiler_params=params(50),
        cost_estimate=cost(50_000_000),
        name="finish_last" if last else "finish_next",
    )(*indices, total, *returned, table, state, *near, *((relations, rel_state) if last else ()))


def flip(index, bits):
    for place in range(8):
        step = 1 << place
        if bits & step:
            index = index + step * (1 - 2 * ((index // step) % 2))
    return index


def relation_kernel(near, finish, whole, parts, received, send_sems, recv_sems):
    dom, rep = lax.axis_index("dom"), lax.axis_index("rep")
    rows = parts.shape[1]
    core = rep % 2

    def device(peer):
        return (flip(dom, peer[0]), flip(rep, peer[1]))

    def mine(which):
        return pl.ds(pl.multiple_of(which * rows, rows), rows)

    barrier = pltpu.get_barrier_semaphore()
    peers = [peer for stage in STAGES[:-1] for peer in stage]
    for peer in peers:
        pl.semaphore_signal(
            barrier, inc=1, device_id=device(peer), device_id_type=pl.DeviceIdType.MESH
        )
    pl.semaphore_wait(barrier, len(peers))
    whole[...] = pair_sum([ref[...] for ref in near])
    slot = 0
    for number, stage in enumerate(STAGES):
        source = whole.at[mine(1 - core)] if number == 0 else parts.at[number - 1]
        copies = []
        for peer in stage:
            copy = pltpu.make_async_remote_copy(
                src_ref=source,
                dst_ref=received.at[slot],
                send_sem=send_sems.at[slot],
                recv_sem=recv_sems.at[slot],
                device_id=device(peer),
                device_id_type=pl.DeviceIdType.MESH,
            )
            copy.start()
            copies.append(copy)
            slot += 1
        for copy in copies:
            copy.wait()
        own = whole[mine(core), :] if number == 0 else parts[number - 1]
        news = [received[slot - len(stage) + i] for i in range(len(stage))]
        if number + 1 < len(STAGES):
            parts[number] = pair_sum([own] + news)
        else:
            low = jnp.where(core == 0, own, news[0])
            high = jnp.where(core == 0, news[0], own)
            finish(jnp.concatenate([low, high], axis=0))


def pair_sum(values):
    while len(values) > 1:
        values = [values[i] + values[i + 1] for i in range(0, len(values), 2)]
    return values[0]


STAGES = (
    ((0, 1),),
    ((0, 2),),
    ((1, 0), (2, 0), (3, 0)),
    ((4, 0),),
    ((0, 1),),
)


def relation_call(body, inputs, outputs, collective_id):
    slots = sum(len(stage) for stage in STAGES)
    shape = inputs[0].shape
    half_shape = (shape[0] // 2, shape[1])
    return pl.pallas_call(
        body,
        out_shape=[jax.ShapeDtypeStruct(shape, jnp.float32)] * outputs,
        in_specs=[VMEM] * len(inputs),
        out_specs=[VMEM] * outputs,
        scratch_shapes=[
            pltpu.VMEM(shape, jnp.float32),
            pltpu.VMEM((len(STAGES) - 1,) + half_shape, jnp.float32),
            pltpu.VMEM((slots,) + half_shape, jnp.float32),
            pltpu.SemaphoreType.DMA((slots,)),
            pltpu.SemaphoreType.DMA((slots,)),
        ],
        compiler_params=pltpu.CompilerParams(
            collective_id=collective_id, has_side_effects=True, vmem_limit_bytes=4 * MIB
        ),
        cost_estimate=cost(20_000_000),
    )(*inputs)


def relation_sum(rel_grad):
    def body(own, summed, *scratch):
        def finish(total):
            summed[...] = total

        relation_kernel([own], finish, *scratch)

    return relation_call(body, [rel_grad], 1, 0)[0]


def relation_step(near, relations, rel_state):
    count = len(near)

    def body(*refs):
        near_refs = refs[:count]
        rel_ref, state_ref, new_rel, new_state = refs[count : count + 4]

        def finish(total):
            state = state_ref[...] + total * total
            new_state[...] = state
            new_rel[...] = rel_ref[...] - rel_rate * total / jnp.sqrt(state)

        relation_kernel(near_refs, finish, *refs[count + 4 :])

    return relation_call(body, [*near, relations, rel_state], 2, 1)


def from_partner(shard, axis, distance):
    return from_peer(shard, axis, 1 << distance)


def from_peer(shard, axis, bits):
    return lax.ppermute(shard, axis, [(i, i ^ bits) for i in range(lax.axis_size(axis))])


def on_device(
    embeddings, row_state, relations, rel_state, edge_src, edge_dst, edge_rel, batch_count
):
    bit_count = lax.axis_size("dom").bit_length() - 1
    row_count, width = embeddings.shape
    batches, count = edge_src.shape[-2:]
    padded = round_up(count, BLOCK)
    state = row_state.reshape(row_count // LANES, LANES)
    spots = [bit_count - 1 - number for number in range(ROUNDS)]
    groups = tuple(
        tuple(range(first, min(first + 2, batches))) for first in range(0, batches, 2)
    )
    sources = [edge_src[0, 0, number].reshape(-1) for number in range(ROUNDS)]
    table, *told = pack_first(
        sources[0], embeddings, edge_dst[0, 0], edge_rel[0, 0], batch_count[0, 0], groups[0]
    )
    told, sent = told[:ROUNDS], told[ROUNDS:]
    for number in range(ROUNDS):
        last = number + 1 == ROUNDS
        swap_bit = spots[number]
        source_index = sources[number]
        live = batch_count[0, 0, number].reshape(1)
        note = from_partner(told[number], "dom", swap_bit)
        arrived = [from_partner(sent[0], "dom", swap_bit)]
        more = pack(source_index, table, groups[1:], count, width, 54)
        for rows in more:
            arrived.append(from_partner(rows, "dom", swap_bit))
        other_index = (note[:batches] % row_count).reshape(-1)
        other_live = note[batches, :1]
        kinds = jnp.pad(
            note[:batches] // row_count, ((0, 0), (0, padded - count)), constant_values=-1
        )
        targets = pack(other_index, table, groups, count, width, 50)
        if number:
            near, targets = lax.optimization_barrier((near, targets))
            relations, rel_state = relation_step(near, relations, rel_state)
        rel_grad = jnp.zeros(relations.shape, jnp.float32)
        own, returned = [], []
        for place, group in enumerate(groups):
            grad_source, grad_target, rel_grad = run_group(
                group,
                count,
                other_live,
                kinds[group[0] : group[-1] + 1],
                arrived[place],
                targets[place],
                relations,
                rel_grad,
            )
            own.append(grad_target)
            returned.append(from_partner(grad_source, "dom", swap_bit))
        if last:
            rel_grad = relation_sum(rel_grad)
        near = [rel_grad]
        for bits in (8, 16, 24):
            near.append(from_peer(rel_grad, "dom", bits))
        early = len(groups) - 1
        total = first_total(
            count, groups, row_count, other_live, live, other_index, source_index, own, returned[:early]
        )
        table, state, *more = finish(
            count,
            groups,
            live,
            source_index,
            total,
            returned[early:],
            early,
            table,
            state,
            width,
            near if last else (),
            relations,
            rel_state,
            None if last else sources[number + 1],
            () if last else groups[0],
        )
        if last:
            relations, rel_state = more
        else:
            sent = more
    return (table, state.reshape(row_count), relations, rel_state)


def solution(mesh):
    return sharded(mesh)


def sharded(mesh):
    return jax.shard_map(
        on_device,
        mesh=mesh,
        in_specs=(
            P(("dom", "rep"), None),
            P(("dom", "rep")),
            P(),
            P(),
            P("dom", "rep", None, None, None),
            P("dom", "rep", None, None, None),
            P("dom", "rep", None, None, None),
            P("dom", "rep", None),
        ),
        out_specs=(P(("dom", "rep"), None), P(("dom", "rep")), P(), P()),
        check_vma=False,
    )
```

```python
import functools

import jax
import jax.numpy as jnp
from jax import lax
from jax.experimental import pallas as pl
from jax.experimental.pallas import tpu as pltpu
from jax.sharding import PartitionSpec as P


ROUNDS = 2

learn_rate = 0.1
rel_rate = 0.1


SMEM = pl.BlockSpec(memory_space=pltpu.SMEM)
VMEM = pl.BlockSpec(memory_space=pltpu.VMEM)
ANY = pl.BlockSpec(memory_space=pl.ANY)
HBM = pl.BlockSpec(memory_space=pltpu.HBM)
GATHER_UNROLL = 40
SCATTER_UNROLL = 8
UPDATE_UNROLL = 8
BLOCK = 256
LANES = 128
MIB = 1024 * 1024


def params(mib, **kw):
    return pltpu.CompilerParams(vmem_limit_bytes=mib * MIB, **kw)


def cost(nbytes):
    return pl.CostEstimate(flops=0, bytes_accessed=nbytes, transcendentals=0)


def round_up(n, m):
    return (n + m - 1) // m * m


def piece(row):
    return pl.ds(pl.multiple_of(row * 2, 2), 2)


def half(start, count, side):
    return pl.ds(start * 2 + side, count, stride=2)


def gather_rows(index_ref, batches, count, table, rows, out):
    height = rows.shape[0] // 2
    if height > count:
        rows[2 * count :, :] = jnp.zeros((2 * (height - count), LANES), rows.dtype)
    for place, batch in enumerate(batches):

        @pl.loop(0, count // GATHER_UNROLL)
        def _(step):
            base = step * GATHER_UNROLL
            for j in range(GATHER_UNROLL):
                rows[piece(base + j), :] = table[piece(index_ref[batch * count + base + j]), :]

        for side in range(2):
            out[place * height : (place + 1) * height, side * LANES : (side + 1) * LANES] = rows[
                half(0, height, side), :
            ].astype(out.dtype)


def scatter_rows(jobs, count):
    @pl.loop(0, count // SCATTER_UNROLL)
    def _(step):
        base = step * SCATTER_UNROLL
        for j in range(SCATTER_UNROLL):
            spots = [piece(job[0][job[1] * count + base + j]) for job in jobs]
            olds = [job[4][spot, :] for spot, job in zip(spots, jobs)]
            for spot, old, (_, _, rows, start, total) in zip(spots, olds, jobs):
                total[spot, :] = old + rows[piece(start + base + j), :]


def scatter_live(live_ref, jobs, count):
    for first in range(0, len(jobs), 2):
        pair = jobs[first : first + 2]
        if len(pair) == 2:

            @pl.when(pair[1][1] < live_ref[0])
            def _():
                scatter_rows(pair, count)

        @pl.when((pair[0][1] < live_ref[0]) & (pair[-1][1] >= live_ref[0]))
        def _():
            scatter_rows(pair[:1], count)


def jobs_of(index, first, group_rows, totals, groups):
    jobs = []
    for group, rows in zip(groups[first:], group_rows):
        height = rows.shape[0] // (2 * len(group))
        for place, batch in enumerate(group):
            jobs.append((index, batch, rows, place * height, totals[batch % 2]))
    return jobs


def spread(ref, rows):
    for side in range(2):
        rows[half(0, ref.shape[0], side), :] = ref[:, side * LANES : (side + 1) * LANES].astype(
            jnp.float32
        )


def pack_first(index, table, edge_dst, edge_rel, batch_count, batches):
    rounds, slots, count = edge_dst.shape
    height = round_up(count, 16)
    row_count, width = table.shape
    parts = 8
    part_rows = row_count // parts

    def body(index_ref, count_ref, table_hbm, dst_ref, rel_ref, long_hbm, *refs):
        notes, refs = refs[:rounds], refs[rounds:]
        out, table_v, long_v, rows, sems = refs
        loads = []
        for part in range(parts):
            here = pl.ds(part * part_rows, part_rows)
            load = pltpu.make_async_copy(table_hbm.at[here], table_v.at[here], sems.at[part])
            load.start()
            loads.append(load)
        for number, note in enumerate(notes):
            note[:slots] = dst_ref[number] + rel_ref[number] * row_count
            note[slots:] = jnp.full((1, count), count_ref[number], jnp.int32)
        for part in range(parts):
            loads[part].wait()

            @pl.loop(part * part_rows // LANES, (part + 1) * part_rows // LANES)
            def _(step):
                here = pl.multiple_of(step * LANES, LANES)
                for side in range(2):
                    long_v[half(here, LANES, side), :] = table_v[
                        pl.ds(here, LANES), side * LANES : (side + 1) * LANES
                    ]

        save = pltpu.make_async_copy(long_v, long_hbm, sems.at[parts])
        save.start()
        gather_rows(index_ref, batches, count, long_v, rows, out)
        save.wait()

    return pl.pallas_call(
        body,
        out_shape=[jax.ShapeDtypeStruct((2 * row_count, LANES), jnp.float32)]
        + [jax.ShapeDtypeStruct((slots + 1, count), jnp.int32)] * rounds
        + [jax.ShapeDtypeStruct((len(batches) * height, width), jnp.bfloat16)],
        in_specs=[SMEM, SMEM, HBM, VMEM, VMEM],
        out_specs=[HBM] + [VMEM] * (rounds + 1),
        scratch_shapes=[
            pltpu.VMEM((row_count, width), jnp.float32),
            pltpu.VMEM((2 * row_count, LANES), jnp.float32),
            pltpu.VMEM((2 * height, LANES), jnp.float32),
            pltpu.SemaphoreType.DMA((parts + 1,)),
        ],
        compiler_params=params(56),
        cost_estimate=cost(25_000_000),
        name="pack_first",
    )(index, batch_count, table, edge_dst, edge_rel)


def pack(index, table, groups, count, width, grant):
    height = round_up(count, 16)

    def body(index_ref, table_hbm, *refs):
        outs, (table_v, rows, sem) = refs[:-3], refs[-3:]
        load = pltpu.make_async_copy(table_hbm, table_v, sem)
        load.start()
        load.wait()
        for out, group in zip(outs, groups):
            gather_rows(index_ref, group, count, table_v, rows, out)

    return pl.pallas_call(
        body,
        out_shape=[
            jax.ShapeDtypeStruct((len(group) * height, width), jnp.bfloat16) for group in groups
        ],
        in_specs=[SMEM, HBM],
        out_specs=[VMEM] * len(groups),
        scratch_shapes=[
            pltpu.VMEM(table.shape, jnp.float32),
            pltpu.VMEM((2 * height, LANES), jnp.float32),
            pltpu.SemaphoreType.DMA,
        ],
        compiler_params=params(grant),
        cost_estimate=cost(30_000_000),
    )(index, table)


def batch_kernel(group, count, live_ref, kind_ref, source_ref, target_ref, rel_ref, rel_in,
                 grad_source, grad_target, rel_out, query_t, total_t, product):
    height, width = source_ref.shape[0] // len(group), source_ref.shape[1]
    full = round_up(height, BLOCK)
    kinds = rel_ref.shape[0]
    neg_share = 0.5 / (count - 1)
    rel_out[...] = rel_in[...]

    @pl.loop(0, jnp.clip(live_ref[0] - group[0], 0, len(group)))
    def _(place):
        start = pl.multiple_of(place * height, 16)
        rel = rel_ref[...]
        high = rel.astype(jnp.bfloat16)
        rest = rel - high.astype(jnp.float32)
        mid = rest.astype(jnp.bfloat16)
        low = (rest - mid.astype(jnp.float32)).astype(jnp.bfloat16)
        parts = jnp.concatenate([high, mid, low], axis=0)
        kind = jnp.broadcast_to(kind_ref[pl.ds(place, 1), :], (3 * kinds, full))
        row = lax.broadcasted_iota(jnp.int32, (3 * kinds, full), 0)
        hot = jnp.where((row % kinds) == kind, 1.0, 0.0).astype(jnp.bfloat16)
        diagonal = lax.dot_general(
            hot, parts, (((0,), (0,)), ((), ())), preferred_element_type=jnp.float32
        )
        source = source_ref[pl.ds(start, height), :].astype(jnp.float32)
        target = target_ref[pl.ds(start, height), :]
        if full > height:
            gap = jnp.zeros((full - height, width), jnp.float32)
            source = jnp.concatenate([source, gap], axis=0)
            target = jnp.concatenate([target, gap.astype(target.dtype)], axis=0)
        query_full = (source * diagonal).astype(jnp.bfloat16).astype(jnp.float32)
        query_t[...] = query_full.T.astype(jnp.bfloat16)
        half_query = (query_full * 0.5).astype(jnp.bfloat16)
        eye = lax.broadcasted_iota(jnp.int32, (BLOCK, BLOCK), 0) == lax.broadcasted_iota(
            jnp.int32, (BLOCK, BLOCK), 1
        )
        for block in range(full // BLOCK):
            here = slice(block * BLOCK, (block + 1) * BLOCK)
            pieces = []
            for col in range(full // BLOCK):
                there = slice(col * BLOCK, (col + 1) * BLOCK)
                slope = jnp.tanh(
                    lax.dot_general(
                        half_query[here],
                        target[there],
                        (((1,), (1,)), ((), ())),
                        preferred_element_type=jnp.float32,
                    )
                )
                weight = slope * neg_share + neg_share
                if col == block:
                    weight = jnp.where(eye, slope * 0.5 - 0.5, weight)
                pieces.append(weight.astype(jnp.bfloat16))
            weights = jnp.concatenate(pieces, axis=1)
            grad_query = jnp.dot(weights, target, preferred_element_type=jnp.float32)
            tall = min(height - block * BLOCK, BLOCK)
            grad_rows = (grad_query * diagonal[here])[:tall]
            spot = pl.multiple_of(start + block * BLOCK, 16)
            grad_source[pl.ds(spot, tall), :] = grad_rows.astype(grad_source.dtype)
            product[here, :] = grad_query * source[here]
            part = jnp.dot(query_t[:, here], weights, preferred_element_type=jnp.float32)
            if block == 0:
                total_t[...] = part
            else:
                total_t[...] += part
        grad_rows = total_t[...].T[:height]
        for side in range(2):
            grad_target[half(start, height, side), :] = grad_rows[:, side * LANES : (side + 1) * LANES]
        value = product[...]
        upper = value.astype(jnp.bfloat16)
        lower = (value - upper.astype(jnp.float32)).astype(jnp.bfloat16)
        one = hot[:kinds]
        rel_out[...] = (
            rel_out[...]
            + jnp.dot(one, upper, preferred_element_type=jnp.float32)
            + jnp.dot(one, lower, preferred_element_type=jnp.float32)
        )


def run_group(group, count, live, kind, source, target, relations, rel_grad):
    height, width = source.shape
    full = round_up(height // len(group), BLOCK)
    return pl.pallas_call(
        functools.partial(batch_kernel, group, count),
        out_shape=[
            jax.ShapeDtypeStruct((height, width), jnp.bfloat16),
            jax.ShapeDtypeStruct((2 * height, LANES), jnp.float32),
            jax.ShapeDtypeStruct(rel_grad.shape, jnp.float32),
        ],
        in_specs=[SMEM] + [VMEM] * 5,
        out_specs=[VMEM] * 3,
        scratch_shapes=[
            pltpu.VMEM((width, full), jnp.bfloat16),
            pltpu.VMEM((width, full), jnp.float32),
            pltpu.VMEM((full, width), jnp.float32),
        ],
        compiler_params=params(24),
        cost_estimate=cost(15_000_000),
        name="batch_terms",
    )(live, kind, source, target, relations, rel_grad)


def first_total(count, groups, row_count, live, other_live, source_index, other_index, own, returned):
    parts = 8
    part_rows = 2 * row_count // parts
    loads = len(own) + len(returned)

    def body(live_ref, other_ref, source_ref, index_ref, *refs):
        inputs, out_hbm = refs[:loads], refs[loads]
        buffers = refs[loads + 1 : 2 * loads + 1]
        rows = refs[2 * loads + 1 : -3]
        total, other, sems = refs[-3:]
        totals = (total, other)
        copies = [
            pltpu.make_async_copy(ref, buffer, sems.at[number])
            for number, (ref, buffer) in enumerate(zip(inputs, buffers))
        ]
        for copy in copies:
            copy.start()
        total[...] = jnp.zeros_like(total)
        other[...] = jnp.zeros_like(other)
        for copy in copies:
            copy.wait()
        for buffer, long in zip(buffers[len(own) :], rows):
            spread(buffer, long)
        scatter_live(
            live_ref,
            jobs_of(source_ref, 0, buffers[: len(own)], totals, groups),
            count,
        )
        scatter_live(
            other_ref,
            jobs_of(index_ref, 0, rows, totals, groups),
            count,
        )
        saves = []
        for part in range(parts):
            here = pl.ds(part * part_rows, part_rows)
            total[here, :] += other[here, :]
            save = pltpu.make_async_copy(total.at[here], out_hbm.at[here], sems.at[loads + part])
            save.start()
            saves.append(save)
        for save in saves:
            save.wait()

    return pl.pallas_call(
        body,
        out_shape=jax.ShapeDtypeStruct((2 * row_count, LANES), jnp.float32),
        in_specs=[SMEM] * 4 + [ANY] * loads,
        out_specs=ANY,
        scratch_shapes=[pltpu.VMEM(array.shape, array.dtype) for array in (*own, *returned)]
        + [pltpu.VMEM(own[0].shape, jnp.float32)] * len(returned)
        + [pltpu.VMEM((2 * row_count, LANES), jnp.float32)] * 2
        + [pltpu.SemaphoreType.DMA((loads + parts,))],
        compiler_params=params(44),
        cost_estimate=cost(60_000_000),
        name="first_total",
    )(live, other_live, source_index, other_index, *own, *returned)


def finish(
    count, groups, live, source_index, total, returned, first, table, state, width, next_index, next_batches
):
    row_count = table.shape[0] // 2
    height = returned[0].shape[0]
    tiles = row_count // LANES
    step_rows = 1024
    steps = row_count // step_rows
    last = next_index is None
    indices = [live, source_index] + ([] if last else [next_index])

    def body(*refs):
        refs = list(refs)

        def take(number):
            taken = refs[:number]
            del refs[:number]
            return taken

        live_ref, index_ref, *next_ref = take(len(indices))
        (total_hbm,) = take(1)
        back_refs = take(len(returned))
        table_hbm, state_ref = take(2)
        out_hbm, state_out = take(2)
        next_outs = take(0 if last else 1)
        total_v, other_v, third_v, table_v, state_t, mean_t, sems = take(7)
        rows = take(len(returned))
        out_v = refs[0] if last else table_v
        load_total = pltpu.make_async_copy(total_hbm, total_v, sems.at[0])
        load_table = pltpu.make_async_copy(table_hbm, table_v, sems.at[1])
        load_total.start()
        load_table.start()
        other_v[...] = jnp.zeros_like(other_v)
        third_v[...] = jnp.zeros_like(third_v)
        for ref, long in zip(back_refs, rows):
            spread(ref, long)
        spare = jnp.zeros((LANES - tiles, LANES), jnp.float32)
        state_t[...] = jnp.concatenate([state_ref[...], spare], axis=0).T
        mean_t[...] = jnp.zeros_like(mean_t)
        totals = (other_v, third_v)
        scatter_live(
            live_ref,
            jobs_of(index_ref, first, rows, totals, groups),
            count,
        )
        load_total.wait()
        load_table.wait()
        lane = lax.broadcasted_iota(jnp.int32, (LANES, LANES), 1)
        saves = []
        for step in range(steps):

            @pl.loop(step * step_rows // LANES, (step + 1) * step_rows // LANES, unroll=UPDATE_UNROLL)
            def _(group):
                base = pl.multiple_of(group * LANES, LANES)
                sides = [half(base, LANES, side) for side in range(2)]
                grads = [total_v[side, :] + (other_v[side, :] + third_v[side, :]) for side in sides]
                square = grads[0] * grads[0] + grads[1] * grads[1]
                mean = jnp.sum(square, axis=1, keepdims=True) * (1.0 / width)
                mine = lane == group
                old = jnp.sum(jnp.where(mine, state_t[...], 0.0), axis=1, keepdims=True)
                mean_t[...] = jnp.where(mine, mean, mean_t[...])
                scale = learn_rate / jnp.sqrt(old + mean)
                values = [table_v[side, :] - grad * scale for side, grad in zip(sides, grads)]
                for number, value in enumerate(values):
                    if last:
                        out_v[pl.ds(base, LANES), number * LANES : (number + 1) * LANES] = value
                    else:
                        out_v[sides[number], :] = value

            tall = step_rows if last else 2 * step_rows
            part = pl.ds(step * tall, tall)
            save = pltpu.make_async_copy(out_v.at[part], out_hbm.at[part], sems.at[2 + step])
            save.start()
            saves.append(save)
        state_out[...] = (state_t[...] + mean_t[...]).T[:tiles]
        for out in next_outs:
            gather_rows(
                next_ref[0], next_batches, count, table_v, rows[0].at[: 2 * round_up(count, 16)], out
            )
        for save in saves:
            save.wait()

    out_shape = (row_count, width) if last else table.shape
    return pl.pallas_call(
        body,
        out_shape=[
            jax.ShapeDtypeStruct(out_shape, jnp.float32),
            jax.ShapeDtypeStruct((tiles, LANES), jnp.float32),
        ]
        + [jax.ShapeDtypeStruct((len(next_batches) * round_up(count, 16), width), jnp.bfloat16)]
        * (not last),
        in_specs=[SMEM] * len(indices)
        + [ANY]
        + [VMEM] * len(returned)
        + [HBM]
        + [VMEM],
        out_specs=[HBM] + [VMEM] * (1 + (not last)),
        scratch_shapes=[
            pltpu.VMEM(table.shape, jnp.float32),
            pltpu.VMEM(table.shape, jnp.float32),
            pltpu.VMEM(table.shape, jnp.float32),
            pltpu.VMEM(table.shape, jnp.float32),
            pltpu.VMEM((LANES, LANES), jnp.float32),
            pltpu.VMEM((LANES, LANES), jnp.float32),
            pltpu.SemaphoreType.DMA((2 + steps,)),
        ]
        + [pltpu.VMEM((2 * height, LANES), jnp.float32)] * len(returned)
        + ([pltpu.VMEM((row_count, width), jnp.float32)] if last else []),
        compiler_params=params(50),
        cost_estimate=cost(50_000_000),
        name="finish_last" if last else "finish_next",
    )(*indices, total, *returned, table, state)


def flip(index, bits):
    for place in range(8):
        step = 1 << place
        if bits & step:
            index = index + step * (1 - 2 * ((index // step) % 2))
    return index


def relation_kernel(near, finish, whole, parts, received, send_sems, recv_sems):
    dom, rep = lax.axis_index("dom"), lax.axis_index("rep")
    rows = parts.shape[1]
    core = rep % 2

    def device(peer):
        return (flip(dom, peer[0]), flip(rep, peer[1]))

    def mine(which):
        return pl.ds(pl.multiple_of(which * rows, rows), rows)

    barrier = pltpu.get_barrier_semaphore()
    peers = [peer for stage in STAGES[:-1] for peer in stage]
    for peer in peers:
        pl.semaphore_signal(
            barrier, inc=1, device_id=device(peer), device_id_type=pl.DeviceIdType.MESH
        )
    pl.semaphore_wait(barrier, len(peers))
    whole[...] = pair_sum([ref[...] for ref in near])
    slot = 0
    for number, stage in enumerate(STAGES):
        source = whole.at[mine(1 - core)] if number == 0 else parts.at[number - 1]
        copies = []
        for peer in stage:
            copy = pltpu.make_async_remote_copy(
                src_ref=source,
                dst_ref=received.at[slot],
                send_sem=send_sems.at[slot],
                recv_sem=recv_sems.at[slot],
                device_id=device(peer),
                device_id_type=pl.DeviceIdType.MESH,
            )
            copy.start()
            copies.append(copy)
            slot += 1
        for copy in copies:
            copy.wait()
        own = whole[mine(core), :] if number == 0 else parts[number - 1]
        news = [received[slot - len(stage) + i] for i in range(len(stage))]
        if number + 1 < len(STAGES):
            parts[number] = pair_sum([own] + news)
        else:
            low = jnp.where(core == 0, own, news[0])
            high = jnp.where(core == 0, news[0], own)
            finish(jnp.concatenate([low, high], axis=0))


def pair_sum(values):
    while len(values) > 1:
        values = [values[i] + values[i + 1] for i in range(0, len(values), 2)]
    return values[0]


STAGES = (
    ((0, 1),),
    ((0, 2),),
    ((1, 0), (2, 0), (3, 0)),
    ((4, 0),),
    ((0, 1),),
)


def relation_call(body, inputs, outputs, collective_id):
    slots = sum(len(stage) for stage in STAGES)
    shape = inputs[0].shape
    half_shape = (shape[0] // 2, shape[1])
    return pl.pallas_call(
        body,
        out_shape=[jax.ShapeDtypeStruct(shape, jnp.float32)] * outputs,
        in_specs=[VMEM] * len(inputs),
        out_specs=[VMEM] * outputs,
        scratch_shapes=[
            pltpu.VMEM(shape, jnp.float32),
            pltpu.VMEM((len(STAGES) - 1,) + half_shape, jnp.float32),
            pltpu.VMEM((slots,) + half_shape, jnp.float32),
            pltpu.SemaphoreType.DMA((slots,)),
            pltpu.SemaphoreType.DMA((slots,)),
        ],
        compiler_params=pltpu.CompilerParams(
            collective_id=collective_id, has_side_effects=True, vmem_limit_bytes=4 * MIB
        ),
        cost_estimate=cost(20_000_000),
    )(*inputs)


def relation_sum(rel_grad):
    def body(own, summed, *scratch):
        def finish(total):
            summed[...] = total

        relation_kernel([own], finish, *scratch)

    return relation_call(body, [rel_grad], 1, 0)[0]


def relation_step(near, relations, rel_state):
    count = len(near)

    def body(*refs):
        near_refs = refs[:count]
        rel_ref, state_ref, new_rel, new_state = refs[count : count + 4]

        def finish(total):
            state = state_ref[...] + total * total
            new_state[...] = state
            new_rel[...] = rel_ref[...] - rel_rate * total / jnp.sqrt(state)

        relation_kernel(near_refs, finish, *refs[count + 4 :])

    return relation_call(body, [*near, relations, rel_state], 2, 1)


def from_partner(shard, axis, distance):
    return from_peer(shard, axis, 1 << distance)


def from_peer(shard, axis, bits):
    return lax.ppermute(shard, axis, [(i, i ^ bits) for i in range(lax.axis_size(axis))])


def on_device(
    embeddings, row_state, relations, rel_state, edge_src, edge_dst, edge_rel, batch_count
):
    bit_count = lax.axis_size("dom").bit_length() - 1
    row_count, width = embeddings.shape
    batches, count = edge_src.shape[-2:]
    padded = round_up(count, BLOCK)
    state = row_state.reshape(row_count // LANES, LANES)
    spots = [bit_count - 1 - number for number in range(ROUNDS)]
    groups = tuple(
        tuple(range(first, min(first + 2, batches))) for first in range(0, batches, 2)
    )
    sources = [edge_src[0, 0, number].reshape(-1) for number in range(ROUNDS)]
    table, *told = pack_first(
        sources[0], embeddings, edge_dst[0, 0], edge_rel[0, 0], batch_count[0, 0], groups[0]
    )
    told, sent = told[:ROUNDS], told[ROUNDS:]
    for number in range(ROUNDS):
        last = number + 1 == ROUNDS
        swap_bit = spots[number]
        source_index = sources[number]
        live = batch_count[0, 0, number].reshape(1)
        note = from_partner(told[number], "dom", swap_bit)
        arrived = [from_partner(sent[0], "dom", swap_bit)]
        more = pack(source_index, table, groups[1:], count, width, 54)
        for rows in more:
            arrived.append(from_partner(rows, "dom", swap_bit))
        other_index = (note[:batches] % row_count).reshape(-1)
        other_live = note[batches, :1]
        kinds = jnp.pad(
            note[:batches] // row_count, ((0, 0), (0, padded - count)), constant_values=-1
        )
        targets = pack(other_index, table, groups, count, width, 50)
        if number:
            near, targets = lax.optimization_barrier((near, targets))
            relations, rel_state = relation_step(near, relations, rel_state)
        rel_grad = jnp.zeros(relations.shape, jnp.float32)
        own, returned = [], []
        for place, group in enumerate(groups):
            grad_source, grad_target, rel_grad = run_group(
                group,
                count,
                other_live,
                kinds[group[0] : group[-1] + 1],
                arrived[place],
                targets[place],
                relations,
                rel_grad,
            )
            own.append(grad_target)
            returned.append(from_partner(grad_source, "dom", swap_bit))
        if last:
            rel_grad = relation_sum(rel_grad)
        near = [rel_grad]
        for bits in (8, 16, 24):
            near.append(from_peer(rel_grad, "dom", bits))
        early = len(groups) - 1
        total = first_total(
            count, groups, row_count, other_live, live, other_index, source_index, own, returned[:early]
        )
        table, state, *sent = finish(
            count,
            groups,
            live,
            source_index,
            total,
            returned[early:],
            early,
            table,
            state,
            width,
            None if last else sources[number + 1],
            () if last else groups[0],
        )
    rel_total = pair_sum(near)
    rel_state = rel_state + rel_total * rel_total
    relations = relations - rel_rate * rel_total / jnp.sqrt(rel_state)
    return (table, state.reshape(row_count), relations, rel_state)


def solution(mesh):
    return sharded(mesh)


def sharded(mesh):
    return jax.shard_map(
        on_device,
        mesh=mesh,
        in_specs=(
            P(("dom", "rep"), None),
            P(("dom", "rep")),
            P(),
            P(),
            P("dom", "rep", None, None, None),
            P("dom", "rep", None, None, None),
            P("dom", "rep", None, None, None),
            P("dom", "rep", None),
        ),
        out_specs=(P(("dom", "rep"), None), P(("dom", "rep")), P(), P()),
        check_vma=False,
    )
```
